32 devices in a mesh: depth: 8 (over z, x), tile: 4 (over y, core).
Axes of the slice: x: 2, y: 2, z: 4, core: 2. Of those that a mesh axis runs over, the one named last changes fastest.
Arguments:
- vorticity: bfloat16 [32, 256, 1024], P('depth', None, 'tile'), may hold values from -6 to 6
- tf_color: float32 [3, 16], replicated, may hold values from 0.05 to 1
- tf_extinction: float32 [16], replicated, may hold values from 0.001 to 10
Outputs:
- final_image: float32 [4, 256, 1024], P(None, 'depth', 'tile')
The draws below stay inside these ranges and needn't reach their ends.
All inputs are finite; a program needn't handle non-finite values.
Results may differ from the reference program's by a relative error of at most 0.002.
Values may be sent and summed in bfloat16 or wider, within the bound.
A program may use at most 64 MiB of HBM per device.

```python
import math
import jax
import jax.numpy as jnp
from jax import lax

NX = 256
KNOTS = 16
NZ = 32
NY = 1024


def shard_levels(key, dims, split, least, top_value):
    def one(dim, parts):
        heights = jax.random.uniform(jax.random.fold_in(jax.random.fold_in(key, 6), dim), (parts,), jnp.float32, least / len(split), top_value / len(split))
        return jnp.repeat(jnp.exp(heights), dims[dim] // parts).reshape((-1,) + (1,) * (len(dims) - dim - 1))

    loudness = one(*split[0])
    for cut in split[1:]:
        loudness = loudness * one(*cut)
    return loudness


def noise(own_key, shape, width, reach, pieces=(), held_as=jnp.bfloat16):
    entries = jax.random.normal(own_key, shape, jnp.float32) * width
    if len(pieces) > 0:
        entries = shard_levels(own_key, shape, pieces, -0.22, 0.18) * entries
    return jnp.clip(entries, min=-reach, max=reach).astype(held_as)


def setup_inputs(seed: int = 0) -> dict:
    keys = jax.random.split(jax.random.key(seed), 4)
    return {
        "vorticity": noise(keys[0], (NZ, NX, NY), 1.0, 6.0, ((0, 8), (2, 4))),
        "tf_color": jnp.clip(jax.random.uniform(keys[1], (3, KNOTS), jnp.float32, 0.05, 1.0), 0.05, 1.0),
        "tf_extinction": jnp.clip(jnp.exp(jax.random.uniform(keys[2], (KNOTS,), jnp.float32, math.log(0.001), math.log(10.0))), 0.001, 10.0),
    }


def shade_sample(slab_below, slab_here, slab_above, tf_color, tf_extinction, thickness):
    middle = slab_here.astype(jnp.float32)
    grad_z = 0.5 * (slab_above[1:-1, 1:-1].astype(jnp.float32) - slab_below[1:-1, 1:-1].astype(jnp.float32))
    grad_x = 0.5 * (middle[2:, 1:-1] - middle[:-2, 1:-1])
    grad_y = 0.5 * (middle[1:-1, 2:] - middle[1:-1, :-2])
    scalar = middle[1:-1, 1:-1]
    facing = 0.48 * grad_x + 0.6 * grad_y + 0.64 * grad_z
    lighting = 0.55 + 0.45 * facing / jnp.sqrt(grad_x * grad_x + grad_y * grad_y + grad_z * grad_z + 0.25)
    count_knots = tf_extinction.shape[0]
    position = jnp.clip((scalar + 4.0) * ((count_knots - 1) / 8.0), 0.0, count_knots - 1.0)
    knot_points = jnp.arange(count_knots, dtype=jnp.float32)
    weights = jnp.maximum(0.0, 1.0 - jnp.abs(position[None] - knot_points[:, None, None]))
    colour_mix = jnp.einsum('ck,kxy->cxy', tf_color, weights, precision=lax.Precision.HIGHEST)
    extinction = jnp.einsum('k,kxy->xy', tf_extinction, weights, precision=lax.Precision.HIGHEST)
    opacity = 1.0 - jnp.exp(-extinction * thickness)
    return jnp.concatenate([opacity[None] * lighting[None] * colour_mix, opacity[None]], axis=0)

def reference(vorticity, tf_color, tf_extinction):
    padded = jnp.pad(vorticity, 1)
    total_slices = vorticity.shape[0]
    thickness = 1.0 / total_slices

    def advance(accumulated, slice_index):
        slab_below = lax.dynamic_index_in_dim(padded, slice_index, 0, keepdims=False)
        slab_here = lax.dynamic_index_in_dim(padded, slice_index + 1, 0, keepdims=False)
        slab_above = lax.dynamic_index_in_dim(padded, slice_index + 2, 0, keepdims=False)
        sample = shade_sample(slab_below, slab_here, slab_above, tf_color, tf_extinction, thickness)
        return (accumulated + (1.0 - accumulated[3:4]) * sample, None)
    blank_image = jnp.zeros((4, vorticity.shape[1], vorticity.shape[2]), jnp.float32)
    final_image = lax.scan(advance, blank_image, jnp.arange(total_slices, dtype=jnp.int32))[0]
    return final_image
```

```python
import functools

import jax
import jax.numpy as jnp
from jax import lax
from jax.experimental import pallas as pl
from jax.experimental.pallas import tpu as pltpu
from jax.sharding import PartitionSpec as P


def extended(cells, sides, width):
    for axis, dim in sides:
        count = lax.axis_size(axis)
        ends = count - 1
        head = lax.slice_in_dim(cells, 0, width, axis=dim)
        tail = lax.slice_in_dim(cells, cells.shape[dim] - width, cells.shape[dim], axis=dim)
        cells = jnp.concatenate(
            [
                lax.ppermute(tail, axis, [(i, (i + 1) % count) for i in range(ends)]),
                cells,
                lax.ppermute(head, axis, [((i + 1) % count, i) for i in range(ends)]),
            ],
            axis=dim,
        )
    return cells


def shade_sample(slab_below, slab_here, slab_above, tf_color, tf_extinction, thickness):
    middle = slab_here.astype(jnp.float32)
    grad_z = 0.5 * (
        slab_above[1:-1, 1:-1].astype(jnp.float32) - slab_below[1:-1, 1:-1].astype(jnp.float32)
    )
    grad_x = 0.5 * (middle[2:, 1:-1] - middle[:-2, 1:-1])
    grad_y = 0.5 * (middle[1:-1, 2:] - middle[1:-1, :-2])
    scalar = middle[1:-1, 1:-1]
    facing = 0.48 * grad_x + 0.6 * grad_y + 0.64 * grad_z
    lighting = 0.55 + 0.45 * facing / jnp.sqrt(
        grad_x * grad_x + grad_y * grad_y + grad_z * grad_z + 0.25
    )
    count_knots = tf_extinction.shape[0]
    position = jnp.clip((scalar + 4.0) * ((count_knots - 1) / 8.0), 0.0, count_knots - 1.0)
    knot_points = jnp.arange(count_knots, dtype=jnp.float32)
    weights = jnp.maximum(0.0, 1.0 - jnp.abs(position[None] - knot_points[:, None, None]))
    colour_mix = jnp.einsum("ck,kxy->cxy", tf_color, weights, precision=lax.Precision.HIGHEST)
    extinction = jnp.einsum("k,kxy->xy", tf_extinction, weights, precision=lax.Precision.HIGHEST)
    opacity = 1.0 - jnp.exp(-extinction * thickness)
    return jnp.concatenate([opacity[None] * lighting[None] * colour_mix, opacity[None]], axis=0)


def composite(nearer, farther):
    return nearer + (1.0 - nearer[3:4]) * farther


def local(vorticity, tf_color, tf_extinction):
    depth_count = lax.axis_size("depth")
    local_slices = vorticity.shape[0]
    tile_rows = vorticity.shape[1]
    tile_cols = vorticity.shape[2]
    thickness = 1.0 / (local_slices * depth_count)
    padded = extended(vorticity, (("depth", 0), ("tile", 2)), 1)
    widened = jnp.pad(padded, ((0, 0), (1, 1), (0, 0)))

    def march(slice_index, accumulated):
        slab_below = lax.dynamic_index_in_dim(widened, slice_index, 0, keepdims=False)
        slab_here = lax.dynamic_index_in_dim(widened, slice_index + 1, 0, keepdims=False)
        slab_above = lax.dynamic_index_in_dim(widened, slice_index + 2, 0, keepdims=False)
        sample = shade_sample(slab_below, slab_here, slab_above, tf_color, tf_extinction, thickness)
        return composite(accumulated, sample)

    blank_image = jnp.zeros((4, tile_rows, tile_cols), jnp.float32)
    partial_value = lax.fori_loop(0, local_slices, march, blank_image)
    block_rows = tile_rows // depth_count
    rounds = depth_count.bit_length() - 1
    stacked = partial_value.reshape(4, 1, tile_rows, tile_cols)
    pieces = lax.all_to_all(
        stacked.astype(jnp.bfloat16), "depth", split_axis=2, concat_axis=1, tiled=True
    ).astype(stacked.dtype)
    for halving in range(rounds):
        paired = pieces.reshape(4, pieces.shape[1] // 2, 2, block_rows, tile_cols)
        pieces = composite(paired[:, :, 0], paired[:, :, 1])
    final_image = pieces[:, 0]
    return final_image


MESH = pl.DeviceIdType.MESH
LANES = 128
PAIR = 2
SUBLANES = 8
VMEM_BYTES = 24 * 2**20


def iota(shape, dim):
    return lax.broadcasted_iota(jnp.int32, shape, dim)


def stencil(chosen_up, chosen_down):
    return jnp.where(chosen_up, 0.5, jnp.where(chosen_down, -0.5, 0.0))


def render_kernel(
    depth_count,
    tile_count,
    vort_hbm,
    color_hbm,
    extinction_hbm,
    out_ref,
    color_ref,
    extinction_ref,
    brick,
    slabs,
    row_out,
    row_in,
    edge_out,
    edge_in,
    part_out,
    part_in,
    part_own,
    local_sem,
    table_sem,
    own_sem,
    send_sem,
    recv_sem,
    row_send_sem,
    row_recv_sem,
    edge_send_sem,
    edge_recv_sem,
    halo_send_sem,
    halo_recv_sem,
    part_send_sem,
    part_recv_sem,
):
    local_slices, pairs, _, rows, tile_cols = vort_hbm.shape
    tile_rows = depth_count * rows
    knots = extinction_hbm.shape[0]
    thickness = 1.0 / (local_slices * depth_count)
    group = local_slices * rows
    pair_slices = PAIR * local_slices
    depth = lax.axis_index("depth")
    tile = lax.axis_index("tile")
    pair = depth // PAIR
    member = depth % PAIR
    mate = 1 - member
    left = lax.rem(tile + tile_count - 1, tile_count)
    right = lax.rem(tile + 1, tile_count)

    whole = pltpu.make_async_copy(vort_hbm, brick, local_sem)
    whole.start()
    loads = [
        pltpu.make_async_copy(color_hbm, color_ref, table_sem.at[0]),
        pltpu.make_async_copy(extinction_hbm, extinction_ref, table_sem.at[1]),
    ]
    for copy in loads:
        copy.start()

    def slot(chunk, which):
        return slabs.at[chunk, pl.ds(1 + which * local_slices, local_slices)]

    own = [
        pltpu.make_async_copy(vort_hbm.at[:, chunk, member], slot(chunk, member), own_sem.at[chunk])
        for chunk in range(pairs)
    ]
    for copy in own:
        copy.start()

    barrier = pltpu.get_barrier_semaphore()
    for step in range(depth_count - 1, 0, -1):
        peer = depth ^ step
        pl.semaphore_signal(barrier, inc=1, device_id=(peer, tile), device_id_type=MESH)
    for which in range(PAIR):
        for side in (left, right):
            pl.semaphore_signal(
                barrier, inc=1, device_id=(pair * PAIR + which, side), device_id_type=MESH
            )
    whole.wait()
    packed = depth_count * 2 * local_slices
    line = iota((packed, 1), 0)
    line_block = line // (2 * local_slices)
    line_slice = (line % (2 * local_slices)) // 2
    line_row = line_block * rows + jnp.where(line % 2 == 0, -1, rows)
    inside = (line_row >= 0) & (line_row < tile_rows)
    wanted = jnp.where(inside, line_slice * tile_rows + line_row, -1)
    pick = jnp.where(iota((packed, local_slices * tile_rows), 1) == wanted, 1.0, 0.0)
    flat = brick[...].reshape(local_slices * tile_rows, tile_cols)
    outside = jnp.dot(pick.astype(jnp.bfloat16), flat, preferred_element_type=jnp.float32)
    for block in range(depth_count):
        first = block * 2 * local_slices
        row_out[block % PAIR, block // PAIR] = outside[first : first + 2 * local_slices].astype(jnp.bfloat16)
    column = iota((SUBLANES, tile_cols), 1)
    ends = iota((SUBLANES, tile_cols), 0)
    pick_ends = ((ends == 0) & (column == 0)) | ((ends == 1) & (column == tile_cols - 1))
    by_block = jnp.concatenate(
        [
            brick[z, block // PAIR, block % PAIR]
            for block in range(depth_count)
            for z in range(local_slices)
        ],
        axis=0,
    )
    columns = lax.dot_general(
        jnp.where(pick_ends, 1.0, 0.0).astype(jnp.bfloat16),
        by_block,
        (((1,), (1,)), ((), ())),
        preferred_element_type=jnp.float32,
    )
    for block in range(depth_count):
        for end in range(2):
            edge_out[end, block % PAIR, block // PAIR] = columns[end : end + 1, block * group : (block + 1) * group]

    blank = jnp.zeros((pairs, 1, rows, tile_cols), jnp.bfloat16)

    @pl.when(pair == 0)
    def _():
        slabs[:, 0:1] = blank

    @pl.when(pair == pairs - 1)
    def _():
        slabs[:, pair_slices + 1 : pair_slices + 2] = blank

    pl.semaphore_wait(barrier, depth_count - 1 + 2 * PAIR)

    def remote(src, dst, sent, received, target):
        return pltpu.make_async_remote_copy(
            src_ref=src,
            dst_ref=dst,
            send_sem=sent,
            recv_sem=received,
            device_id=target,
            device_id_type=MESH,
        )

    def order(step):
        return pair ^ (pairs - 1 - step)

    sends = []
    row_in[member] = row_out[member]
    copy = remote(
        row_out.at[mate],
        row_in.at[member],
        row_send_sem,
        row_recv_sem,
        (pair * PAIR + mate, tile),
    )
    copy.start()
    sends.append(copy)
    for which in range(PAIR):
        for end, beside in enumerate((left, right)):
            copy = remote(
                edge_out.at[end, which],
                edge_in.at[1 - end, member],
                edge_send_sem.at[end, which],
                edge_recv_sem.at[1 - end, member],
                (pair * PAIR + which, beside),
            )
            copy.start()
            sends.append(copy)

    def halo(which, beyond):
        at = PAIR * local_slices + 1 if beyond < 0 else 0
        return remote(
            vort_hbm.at[0 if beyond < 0 else local_slices - 1, :, which],
            slabs.at[:, at],
            halo_send_sem.at[which],
            halo_recv_sem.at[0 if beyond > 0 else 1],
            ((pair + beyond) * PAIR + which, tile),
        )

    to_below = (member == 0) & (pair > 0)
    to_above = (member == PAIR - 1) & (pair < pairs - 1)

    @pl.when(to_below)
    def _():
        for which in range(PAIR):
            halo(which, -1).start()

    @pl.when(to_above)
    def _():
        for which in range(PAIR):
            halo(which, 1).start()

    for step in range(pairs):
        chunk = order(step)
        copy = remote(
            vort_hbm.at[:, chunk, mate],
            slot(chunk, member),
            send_sem.at[step],
            recv_sem.at[chunk],
            (pair * PAIR + mate, tile),
        )
        copy.start()
        sends.append(copy)

    spread = (2 + local_slices) * rows
    extra = 2 * SUBLANES
    cell = iota((group, spread + extra), 0)
    source = iota((group, spread + extra), 1)
    cell_row = cell % rows
    in_slabs = source < spread
    up = in_slabs & (source == cell + rows + 1) & (cell_row < rows - 1)
    down = in_slabs & (source == cell + rows - 1) & (cell_row > 0)
    packed_line = spread + 2 * (cell // rows)
    up = up | ((source == packed_line + 1) & (cell_row == rows - 1))
    down = down | ((source == packed_line) & (cell_row == 0))
    along_x = stencil(up, down).astype(jnp.bfloat16)
    along_z = stencil(in_slabs & (source == cell + 2 * rows), in_slabs & (source == cell)).astype(jnp.bfloat16)
    to_col = iota((tile_cols, tile_cols), 1)
    from_col = iota((tile_cols, tile_cols), 0)
    along_y = stencil(from_col == to_col + 1, from_col == to_col - 1).astype(jnp.bfloat16)
    has_left = jnp.where(tile > 0, -0.5, 0.0)
    has_right = jnp.where(tile < tile_count - 1, 0.5, 0.0)
    place = jnp.where(
        (ends == 0) & (column == 0),
        has_left,
        jnp.where((ends == 1) & (column == tile_cols - 1), has_right, 0.0),
    ).astype(jnp.bfloat16)

    for copy in loads:
        copy.wait()
    folds = rows // SUBLANES
    banks = -(-knots // SUBLANES)
    knot = iota((SUBLANES, LANES), 0)

    def wide(read, count):
        spread_out = []
        for bank in range(banks):
            value = jnp.zeros((SUBLANES, LANES), jnp.float32)
            for k in range(bank * SUBLANES, min(count, (bank + 1) * SUBLANES)):
                value = jnp.where(knot == k - bank * SUBLANES, read(k), value)
            spread_out.append(jnp.concatenate([value] * (folds * tile_cols // LANES), axis=1))
        return spread_out

    def table(read):
        return wide(read, knots), wide(lambda k: read(k + 1) - read(k), knots - 1)

    tables = [table(lambda k, c=c: color_ref[c, k]) for c in range(3)]
    tables.append(table(lambda k: -thickness * extinction_ref[k]))

    def fold(value):
        return jnp.concatenate(
            [value[first : first + SUBLANES] for first in range(0, rows, SUBLANES)], axis=1
        )

    def unfold(value):
        return jnp.concatenate(
            [value[:, first * tile_cols : (first + 1) * tile_cols] for first in range(folds)], axis=0
        )

    def pick_from(choices, index):
        found = None
        for bank, choice in enumerate(choices):
            got = jnp.take_along_axis(choice, index % SUBLANES, axis=0, mode="promise_in_bounds")
            found = got if found is None else jnp.where(index >= bank * SUBLANES, got, found)
        return found

    def lookup(which, index, part):
        value, slope = tables[which]
        return pick_from(value, index) + part * pick_from(slope, index)

    def wait_recv(dst, sem):
        remote(dst, dst, row_send_sem, sem, (depth, tile)).wait_recv()

    for copy in own:
        copy.wait()

    @pl.when(pair > 0)
    def _():
        wait_recv(slabs.at[:, 0], halo_recv_sem.at[0])

    @pl.when(pair < pairs - 1)
    def _():
        wait_recv(slabs.at[:, pair_slices + 1], halo_recv_sem.at[1])

    wait_recv(row_in.at[mate], row_recv_sem)
    for end in range(2):
        for which in range(PAIR):
            wait_recv(edge_in.at[end, which], edge_recv_sem.at[end, which])

    def over(near, far):
        clear = 1.0 - near[3]
        return tuple(n + clear * f for n, f in zip(near, far))

    def shade(chunk, which, partial):
        around = slabs[chunk, which * local_slices : (which + 1) * local_slices + 2].reshape(spread, tile_cols)
        lines = row_in[which, chunk].astype(jnp.float32)
        lines = jnp.concatenate(
            [lines, jnp.zeros((extra - 2 * local_slices, tile_cols), jnp.float32)], axis=0
        ).astype(jnp.bfloat16)
        around = jnp.concatenate([around, lines], axis=0)
        grads_x = jnp.dot(along_x, around, preferred_element_type=jnp.float32)
        grads_z = jnp.dot(along_z, around, preferred_element_type=jnp.float32)
        cells = slabs[chunk, 1 + which * local_slices : 1 + (which + 1) * local_slices].reshape(group, tile_cols)
        edge_row = iota((SUBLANES, group), 0)
        edges = jnp.where(
            edge_row == 0, edge_in[0, which, chunk], jnp.where(edge_row == 1, edge_in[1, which, chunk], 0.0)
        )
        grads_y = jnp.dot(cells, along_y, preferred_element_type=jnp.float32) + lax.dot_general(
            edges.astype(jnp.bfloat16),
            place,
            (((0,), (0,)), ((), ())),
            preferred_element_type=jnp.float32,
        )
        for z in range(local_slices):
            here = slice(z * rows, (z + 1) * rows)
            gx, gy, gz = fold(grads_x[here]), fold(grads_y[here]), fold(grads_z[here])
            scalar = fold(cells[here].astype(jnp.float32))
            facing = 0.48 * gx + 0.6 * gy + 0.64 * gz
            lighting = 0.55 + 0.45 * facing * lax.rsqrt(gx * gx + gy * gy + gz * gz + 0.25)
            position = jnp.clip((scalar + 4.0) * ((knots - 1) / 8.0), 0.0, knots - 1.0)
            index = position.astype(jnp.int32)
            part = position - index.astype(jnp.float32)
            opacity = 1.0 - jnp.exp(lookup(3, index, part))
            lit = opacity * lighting
            sample = tuple(lit * lookup(c, index, part) for c in range(3)) + (opacity,)
            partial = sample if partial is None else over(partial, sample)
        return partial

    def send_part(step):
        chunk = order(step)
        return remote(
            part_out.at[chunk],
            part_in.at[pair],
            part_send_sem.at[chunk],
            part_recv_sem.at[pair],
            (chunk * PAIR + member, tile),
        )

    def march(step, carry):
        chunk = order(step)
        wait_recv(slot(chunk, mate), recv_sem.at[chunk])
        partial = None
        for which in range(PAIR):
            partial = shade(chunk, which, partial)
        for channel in range(4):
            image = unfold(partial[channel])
            part_own[channel] = image
            part_out[chunk, channel] = image.astype(jnp.bfloat16)

        @pl.when(step < pairs - 1)
        def _():
            send_part(step).start()

        return carry

    lax.fori_loop(0, pairs, march, 0)
    part_in[pair] = part_out[pair]
    for step in range(pairs - 1):
        wait_recv(part_in.at[order(step)], part_recv_sem.at[order(step)])
    total = None
    for source in range(pairs):
        layer = tuple(
            jnp.where(pair == source, part_own[c], part_in[source, c].astype(jnp.float32))
            for c in range(4)
        )
        total = layer if total is None else over(total, layer)
    for channel in range(4):
        out_ref[channel] = total[channel]
    for copy in sends:
        copy.wait_send()
    for step in range(pairs - 1):
        send_part(step).wait_send()

    @pl.when(to_below)
    def _():
        for which in range(PAIR):
            halo(which, -1).wait_send()

    @pl.when(to_above)
    def _():
        for which in range(PAIR):
            halo(which, 1).wait_send()


def render(vorticity, tf_color, tf_extinction):
    depth_count = lax.axis_size("depth")
    tile_count = lax.axis_size("tile")
    local_slices, tile_rows, tile_cols = vorticity.shape
    rows = tile_rows // depth_count
    group = local_slices * rows
    pairs = depth_count // PAIR
    dma = pltpu.SemaphoreType.DMA
    return pl.pallas_call(
        functools.partial(render_kernel, depth_count, tile_count),
        out_shape=pltpu.VMEM((4, rows, tile_cols), jnp.float32),
        in_specs=[
            pl.BlockSpec(memory_space=pltpu.HBM),
            pl.BlockSpec(memory_space=pltpu.HBM),
            pl.BlockSpec(memory_space=pltpu.HBM),
        ],
        out_specs=pl.BlockSpec(memory_space=pltpu.VMEM),
        scratch_shapes=[
            pltpu.SMEM(tf_color.shape, jnp.float32),
            pltpu.SMEM(tf_extinction.shape, jnp.float32),
            pltpu.VMEM((local_slices, pairs, PAIR, rows, tile_cols), jnp.bfloat16),
            pltpu.VMEM((pairs, PAIR * local_slices + 2, rows, tile_cols), jnp.bfloat16),
            pltpu.VMEM((PAIR, pairs, 2 * local_slices, tile_cols), jnp.bfloat16),
            pltpu.VMEM((PAIR, pairs, 2 * local_slices, tile_cols), jnp.bfloat16),
            pltpu.VMEM((2, PAIR, pairs, 1, group), jnp.float32),
            pltpu.VMEM((2, PAIR, pairs, 1, group), jnp.float32),
            pltpu.VMEM((pairs, 4, rows, tile_cols), jnp.bfloat16),
            pltpu.VMEM((pairs, 4, rows, tile_cols), jnp.bfloat16),
            pltpu.VMEM((4, rows, tile_cols), jnp.float32),
            dma,
            dma((2,)),
            dma((pairs,)),
            dma((pairs,)),
            dma((pairs,)),
            dma,
            dma,
            dma((2, PAIR)),
            dma((2, PAIR)),
            dma((PAIR,)),
            dma((2,)),
            dma((pairs,)),
            dma((pairs,)),
        ],
        compiler_params=pltpu.CompilerParams(collective_id=0, has_side_effects=True, vmem_limit_bytes=VMEM_BYTES),
        name="render",
    )(*(pltpu.with_memory_space_constraint(given, pltpu.HBM) for given in (vorticity.reshape(local_slices, pairs, PAIR, rows, tile_cols), tf_color, tf_extinction)))


def fits(vorticity, knots):
    local_slices, tile_rows, tile_cols = vorticity.shape
    depth_count = lax.axis_size("depth")
    rows = tile_rows // depth_count
    return (
        tile_rows % depth_count == 0
        and rows % (2 * SUBLANES) == 0
        and tile_cols % LANES == 0
        and (local_slices * rows) % LANES == 0
        and 2 * local_slices == SUBLANES
        and knots <= LANES
        and depth_count % PAIR == 0
        and depth_count & (depth_count - 1) == 0
        and depth_count <= 16
        and lax.axis_size("tile") > 1
    )


def choose(vorticity, tf_color, tf_extinction):
    if fits(vorticity, tf_extinction.shape[0]):
        return render(vorticity, tf_color, tf_extinction)
    return local(vorticity, tf_color, tf_extinction)


def solution(mesh):
    placed = (P("depth", None, "tile"), P(), P())
    return jax.shard_map(
        choose, mesh=mesh, in_specs=placed, out_specs=P(None, "depth", "tile"), check_vma=False
    )
```

```python
import functools

import jax
import jax.numpy as jnp
from jax import lax
from jax.experimental import pallas as pl
from jax.experimental.pallas import tpu as pltpu
from jax.sharding import PartitionSpec as P


def extended(cells, sides, width):
    for axis, dim in sides:
        count = lax.axis_size(axis)
        ends = count - 1
        head = lax.slice_in_dim(cells, 0, width, axis=dim)
        tail = lax.slice_in_dim(cells, cells.shape[dim] - width, cells.shape[dim], axis=dim)
        cells = jnp.concatenate(
            [
                lax.ppermute(tail, axis, [(i, (i + 1) % count) for i in range(ends)]),
                cells,
                lax.ppermute(head, axis, [((i + 1) % count, i) for i in range(ends)]),
            ],
            axis=dim,
        )
    return cells


def shade_sample(slab_below, slab_here, slab_above, tf_color, tf_extinction, thickness):
    middle = slab_here.astype(jnp.float32)
    grad_z = 0.5 * (
        slab_above[1:-1, 1:-1].astype(jnp.float32) - slab_below[1:-1, 1:-1].astype(jnp.float32)
    )
    grad_x = 0.5 * (middle[2:, 1:-1] - middle[:-2, 1:-1])
    grad_y = 0.5 * (middle[1:-1, 2:] - middle[1:-1, :-2])
    scalar = middle[1:-1, 1:-1]
    facing = 0.48 * grad_x + 0.6 * grad_y + 0.64 * grad_z
    lighting = 0.55 + 0.45 * facing / jnp.sqrt(
        grad_x * grad_x + grad_y * grad_y + grad_z * grad_z + 0.25
    )
    count_knots = tf_extinction.shape[0]
    position = jnp.clip((scalar + 4.0) * ((count_knots - 1) / 8.0), 0.0, count_knots - 1.0)
    knot_points = jnp.arange(count_knots, dtype=jnp.float32)
    weights = jnp.maximum(0.0, 1.0 - jnp.abs(position[None] - knot_points[:, None, None]))
    colour_mix = jnp.einsum("ck,kxy->cxy", tf_color, weights, precision=lax.Precision.HIGHEST)
    extinction = jnp.einsum("k,kxy->xy", tf_extinction, weights, precision=lax.Precision.HIGHEST)
    opacity = 1.0 - jnp.exp(-extinction * thickness)
    return jnp.concatenate([opacity[None] * lighting[None] * colour_mix, opacity[None]], axis=0)


def composite(nearer, farther):
    return nearer + (1.0 - nearer[3:4]) * farther


def local(vorticity, tf_color, tf_extinction):
    depth_count = lax.axis_size("depth")
    local_slices = vorticity.shape[0]
    tile_rows = vorticity.shape[1]
    tile_cols = vorticity.shape[2]
    thickness = 1.0 / (local_slices * depth_count)
    padded = extended(vorticity, (("depth", 0), ("tile", 2)), 1)
    widened = jnp.pad(padded, ((0, 0), (1, 1), (0, 0)))

    def march(slice_index, accumulated):
        slab_below = lax.dynamic_index_in_dim(widened, slice_index, 0, keepdims=False)
        slab_here = lax.dynamic_index_in_dim(widened, slice_index + 1, 0, keepdims=False)
        slab_above = lax.dynamic_index_in_dim(widened, slice_index + 2, 0, keepdims=False)
        sample = shade_sample(slab_below, slab_here, slab_above, tf_color, tf_extinction, thickness)
        return composite(accumulated, sample)

    blank_image = jnp.zeros((4, tile_rows, tile_cols), jnp.float32)
    partial_value = lax.fori_loop(0, local_slices, march, blank_image)
    block_rows = tile_rows // depth_count
    rounds = depth_count.bit_length() - 1
    stacked = partial_value.reshape(4, 1, tile_rows, tile_cols)
    pieces = lax.all_to_all(
        stacked.astype(jnp.bfloat16), "depth", split_axis=2, concat_axis=1, tiled=True
    ).astype(stacked.dtype)
    for halving in range(rounds):
        paired = pieces.reshape(4, pieces.shape[1] // 2, 2, block_rows, tile_cols)
        pieces = composite(paired[:, :, 0], paired[:, :, 1])
    final_image = pieces[:, 0]
    return final_image


MESH = pl.DeviceIdType.MESH
LANES = 128
PAIR = 2
SUBLANES = 8
VMEM_BYTES = 24 * 2**20


def iota(shape, dim):
    return lax.broadcasted_iota(jnp.int32, shape, dim)


def stencil(chosen_up, chosen_down):
    return jnp.where(chosen_up, 0.5, jnp.where(chosen_down, -0.5, 0.0))


def render_kernel(
    depth_count,
    tile_count,
    vort_hbm,
    color_hbm,
    extinction_hbm,
    out_ref,
    color_ref,
    extinction_ref,
    brick,
    slabs,
    row_out,
    row_in,
    edge_out,
    edge_in,
    part_out,
    part_in,
    part_own,
    local_sem,
    table_sem,
    own_sem,
    send_sem,
    recv_sem,
    row_send_sem,
    row_recv_sem,
    edge_send_sem,
    edge_recv_sem,
    halo_send_sem,
    halo_recv_sem,
    part_send_sem,
    part_recv_sem,
    far_sem,
):
    local_slices, pairs, _, rows, tile_cols = vort_hbm.shape
    tile_rows = depth_count * rows
    knots = extinction_hbm.shape[0]
    thickness = 1.0 / (local_slices * depth_count)
    group = local_slices * rows
    pair_slices = PAIR * local_slices
    depth = lax.axis_index("depth")
    tile = lax.axis_index("tile")
    pair = depth // PAIR
    member = depth % PAIR
    mate = 1 - member
    left = tile - 1
    right = tile + 1
    has_below = pair > 0
    has_above = pair < pairs - 1
    has_left = tile > 0
    has_right = tile < tile_count - 1

    whole = pltpu.make_async_copy(vort_hbm, brick, local_sem)
    whole.start()
    loads = [
        pltpu.make_async_copy(color_hbm, color_ref, table_sem.at[0]),
        pltpu.make_async_copy(extinction_hbm, extinction_ref, table_sem.at[1]),
    ]
    for copy in loads:
        copy.start()

    def slot(chunk, which):
        return slabs.at[chunk, pl.ds(1 + which * local_slices, local_slices)]

    own = [
        pltpu.make_async_copy(vort_hbm.at[:, chunk, member], slot(chunk, member), own_sem.at[chunk])
        for chunk in range(pairs)
    ]
    for copy in own:
        copy.start()

    barrier = pltpu.get_barrier_semaphore()

    def greet(there, peers):
        @pl.when(there)
        def _():
            for peer in peers:
                pl.semaphore_signal(barrier, inc=1, device_id=peer, device_id_type=MESH)

    def both(place, column):
        return [(place * PAIR + which, column) for which in range(PAIR)]

    greet(has_left, both(pair, left))
    greet(has_right, both(pair, right))
    greet(has_below, both(pair - 1, tile))
    greet(has_above, both(pair + 1, tile))
    pl.semaphore_signal(barrier, inc=1, device_id=(pair * PAIR + mate, tile), device_id_type=MESH)
    greeted = 1
    for there in (has_left, has_right, has_below, has_above):
        greeted = greeted + PAIR * there.astype(jnp.int32)

    def tell(there, place, sem):
        @pl.when(there)
        def _():
            pl.semaphore_signal(sem, inc=1, device_id=(place * PAIR + member, tile), device_id_type=MESH)

    def hear(there, sem):
        @pl.when(there)
        def _():
            pl.semaphore_wait(sem, 1)


    def remote(src, dst, sent, received, target):
        return pltpu.make_async_remote_copy(
            src_ref=src,
            dst_ref=dst,
            send_sem=sent,
            recv_sem=received,
            device_id=target,
            device_id_type=MESH,
        )

    def order(step, place=None):
        place = pair if place is None else place
        turn = jnp.where(place == 0, 0, jnp.where(place == 1, pairs - 1, place - 1))
        at = step + (step >= turn).astype(jnp.int32)
        chunk = jnp.where(at == 0, 0, jnp.where(at == pairs - 1, 1, at + 1))
        return jnp.where(step == pairs - 1, place, chunk)

    sends = []

    def halo(which, beyond, chunk):
        at = PAIR * local_slices + 1 if beyond < 0 else 0
        return remote(
            vort_hbm.at[0 if beyond < 0 else local_slices - 1, chunk, which],
            slabs.at[chunk, at],
            halo_send_sem.at[which, chunk],
            halo_recv_sem.at[0 if beyond > 0 else 1, chunk],
            ((pair + beyond) * PAIR + which, tile),
        )

    to_below = (member == 0) & (pair > 0)
    to_above = (member == PAIR - 1) & (pair < pairs - 1)

    def push(step):

        @pl.when(to_below)
        def _():
            for which in range(PAIR):
                halo(which, -1, order(step, pair - 1)).start()

        @pl.when(to_above)
        def _():
            for which in range(PAIR):
                halo(which, 1, order(step, pair + 1)).start()

        chunk = order(step)
        copy = remote(
            vort_hbm.at[:, chunk, mate],
            slot(chunk, member),
            send_sem.at[step],
            recv_sem.at[chunk],
            (pair * PAIR + mate, tile),
        )
        copy.start()
        sends.append(copy)

    whole.wait()
    packed = depth_count * 2 * local_slices
    line = iota((packed, 1), 0)
    line_block = line // (2 * local_slices)
    line_slice = (line % (2 * local_slices)) // 2
    line_row = line_block * rows + jnp.where(line % 2 == 0, -1, rows)
    inside = (line_row >= 0) & (line_row < tile_rows)
    wanted = jnp.where(inside, line_slice * tile_rows + line_row, -1)
    pick = jnp.where(iota((packed, local_slices * tile_rows), 1) == wanted, 1.0, 0.0)
    flat = brick[...].reshape(local_slices * tile_rows, tile_cols)
    outside = jnp.dot(pick.astype(jnp.bfloat16), flat, preferred_element_type=jnp.float32)
    for block in range(depth_count):
        first = block * 2 * local_slices
        row_out[block % PAIR, block // PAIR] = outside[first : first + 2 * local_slices].astype(jnp.bfloat16)
    column = iota((SUBLANES, tile_cols), 1)
    ends = iota((SUBLANES, tile_cols), 0)
    pick_ends = ((ends == 0) & (column == 0)) | ((ends == 1) & (column == tile_cols - 1))
    by_block = jnp.concatenate(
        [
            brick[z, block // PAIR, block % PAIR]
            for block in range(depth_count)
            for z in range(local_slices)
        ],
        axis=0,
    )
    columns = lax.dot_general(
        jnp.where(pick_ends, 1.0, 0.0).astype(jnp.bfloat16),
        by_block,
        (((1,), (1,)), ((), ())),
        preferred_element_type=jnp.float32,
    )
    for block in range(depth_count):
        for end in range(2):
            edge_out[end, block % PAIR, block // PAIR] = columns[end : end + 1, block * group : (block + 1) * group]

    blank = jnp.zeros((pairs, 1, rows, tile_cols), jnp.bfloat16)

    @pl.when(pair == 0)
    def _():
        slabs[:, 0:1] = blank

    @pl.when(pair == pairs - 1)
    def _():
        slabs[:, pair_slices + 1 : pair_slices + 2] = blank

    row_in[member] = row_out[member]
    pl.semaphore_wait(barrier, greeted)
    tell(has_below & has_above, pair - 1, far_sem.at[0, 0])
    tell(has_below & has_above, pair + 1, far_sem.at[1, 0])
    copy = remote(
        row_out.at[mate],
        row_in.at[member],
        row_send_sem,
        row_recv_sem,
        (pair * PAIR + mate, tile),
    )
    copy.start()
    sends.append(copy)

    def edge(end, which):
        return remote(
            edge_out.at[end, which],
            edge_in.at[1 - end, member],
            edge_send_sem.at[end, which],
            edge_recv_sem.at[1 - end, member],
            (pair * PAIR + which, (left, right)[end]),
        )

    sides = (has_left, has_right)
    for end in range(2):

        @pl.when(sides[end])
        def _():
            for which in range(PAIR):
                edge(end, which).start()

        @pl.when(jnp.logical_not(sides[end]))
        def _():
            edge_in[end] = jnp.zeros(edge_in.shape[1:], jnp.float32)

    for step in range(pairs):
        push(step)

    spread = (2 + local_slices) * rows
    extra = 2 * SUBLANES
    cell = iota((group, spread + extra), 0)
    source = iota((group, spread + extra), 1)
    cell_row = cell % rows
    in_slabs = source < spread
    up = in_slabs & (source == cell + rows + 1) & (cell_row < rows - 1)
    down = in_slabs & (source == cell + rows - 1) & (cell_row > 0)
    packed_line = spread + 2 * (cell // rows)
    up = up | ((source == packed_line + 1) & (cell_row == rows - 1))
    down = down | ((source == packed_line) & (cell_row == 0))
    along_x = stencil(up, down).astype(jnp.bfloat16)
    along_z = stencil(in_slabs & (source == cell + 2 * rows), in_slabs & (source == cell)).astype(jnp.bfloat16)
    to_col = iota((tile_cols, tile_cols), 1)
    from_col = iota((tile_cols, tile_cols), 0)
    along_y = stencil(from_col == to_col + 1, from_col == to_col - 1).astype(jnp.bfloat16)
    place = jnp.where(
        (ends == 0) & (column == 0),
        -0.5,
        jnp.where((ends == 1) & (column == tile_cols - 1), 0.5, 0.0),
    ).astype(jnp.bfloat16)

    for copy in loads:
        copy.wait()
    folds = rows // SUBLANES
    banks = -(-knots // SUBLANES)
    knot = iota((SUBLANES, LANES), 0)

    def wide(read, count):
        spread_out = []
        for bank in range(banks):
            value = jnp.zeros((SUBLANES, LANES), jnp.float32)
            for k in range(bank * SUBLANES, min(count, (bank + 1) * SUBLANES)):
                value = jnp.where(knot == k - bank * SUBLANES, read(k), value)
            spread_out.append(jnp.concatenate([value] * (folds * tile_cols // LANES), axis=1))
        return spread_out

    def table(read):
        return wide(read, knots), wide(lambda k: read(k + 1) - read(k), knots - 1)

    tables = [table(lambda k, c=c: color_ref[c, k]) for c in range(3)]
    tables.append(table(lambda k: -thickness * extinction_ref[k]))

    def fold(value):
        return jnp.concatenate(
            [value[first : first + SUBLANES] for first in range(0, rows, SUBLANES)], axis=1
        )

    def unfold(value):
        return jnp.concatenate(
            [value[:, first * tile_cols : (first + 1) * tile_cols] for first in range(folds)], axis=0
        )

    def pick_from(choices, index):
        found = None
        for bank, choice in enumerate(choices):
            got = jnp.take_along_axis(choice, index % SUBLANES, axis=0, mode="promise_in_bounds")
            found = got if found is None else jnp.where(index >= bank * SUBLANES, got, found)
        return found

    def lookup(which, index, part):
        value, slope = tables[which]
        return pick_from(value, index) + part * pick_from(slope, index)

    def wait_recv(dst, sem):
        remote(dst, dst, row_send_sem, sem, (depth, tile)).wait_recv()

    for copy in own:
        copy.wait()

    wait_recv(row_in.at[mate], row_recv_sem)
    for end in range(2):

        @pl.when(sides[end])
        def _():
            for which in range(PAIR):
                wait_recv(edge_in.at[end, which], edge_recv_sem.at[end, which])

    hear(pair < pairs - 2, far_sem.at[0, 0])
    hear(pair >= 2, far_sem.at[1, 0])
    for reach in range(1, pairs - 2):
        tell(has_below & (pair < pairs - 1 - reach), pair - 1, far_sem.at[0, reach])
        tell(has_above & (pair > reach), pair + 1, far_sem.at[1, reach])
        hear(pair < pairs - 2 - reach, far_sem.at[0, reach])
        hear(pair >= 2 + reach, far_sem.at[1, reach])

    def over(near, far):
        clear = 1.0 - near[3]
        return tuple(n + clear * f for n, f in zip(near, far))

    def shade(chunk, which, partial):
        around = slabs[chunk, which * local_slices : (which + 1) * local_slices + 2].reshape(spread, tile_cols)
        lines = row_in[which, chunk].astype(jnp.float32)
        lines = jnp.concatenate(
            [lines, jnp.zeros((extra - 2 * local_slices, tile_cols), jnp.float32)], axis=0
        ).astype(jnp.bfloat16)
        around = jnp.concatenate([around, lines], axis=0)
        grads_x = jnp.dot(along_x, around, preferred_element_type=jnp.float32)
        grads_z = jnp.dot(along_z, around, preferred_element_type=jnp.float32)
        cells = slabs[chunk, 1 + which * local_slices : 1 + (which + 1) * local_slices].reshape(group, tile_cols)
        edge_row = iota((SUBLANES, group), 0)
        edges = jnp.where(
            edge_row == 0, edge_in[0, which, chunk], jnp.where(edge_row == 1, edge_in[1, which, chunk], 0.0)
        )
        grads_y = jnp.dot(cells, along_y, preferred_element_type=jnp.float32) + lax.dot_general(
            edges.astype(jnp.bfloat16),
            place,
            (((0,), (0,)), ((), ())),
            preferred_element_type=jnp.float32,
        )
        for z in range(local_slices):
            here = slice(z * rows, (z + 1) * rows)
            gx, gy, gz = fold(grads_x[here]), fold(grads_y[here]), fold(grads_z[here])
            scalar = fold(cells[here].astype(jnp.float32))
            facing = 0.48 * gx + 0.6 * gy + 0.64 * gz
            lighting = 0.55 + 0.45 * facing * lax.rsqrt(gx * gx + gy * gy + gz * gz + 0.25)
            position = jnp.clip((scalar + 4.0) * ((knots - 1) / 8.0), 0.0, knots - 1.0)
            index = position.astype(jnp.int32)
            part = position - index.astype(jnp.float32)
            opacity = 1.0 - jnp.exp(lookup(3, index, part))
            lit = opacity * lighting
            sample = tuple(lit * lookup(c, index, part) for c in range(3)) + (opacity,)
            partial = sample if partial is None else over(partial, sample)
        return partial

    def send_part(step):
        chunk = order(step)
        return remote(
            part_out.at[chunk],
            part_in.at[pair],
            part_send_sem.at[chunk],
            part_recv_sem.at[pair],
            (chunk * PAIR + member, tile),
        )

    def march(step, carry):
        chunk = order(step)
        wait_recv(slot(chunk, mate), recv_sem.at[chunk])

        @pl.when(pair > 0)
        def _():
            wait_recv(slabs.at[chunk, 0], halo_recv_sem.at[0, chunk])

        @pl.when(pair < pairs - 1)
        def _():
            wait_recv(slabs.at[chunk, pair_slices + 1], halo_recv_sem.at[1, chunk])

        partial = None
        for which in range(PAIR):
            partial = shade(chunk, which, partial)
        for channel in range(4):
            image = unfold(partial[channel])
            part_own[channel] = image
            part_out[chunk, channel] = image.astype(jnp.bfloat16)

        @pl.when(step < pairs - 1)
        def _():
            send_part(step).start()

        return carry

    lax.fori_loop(0, pairs, march, 0)
    part_in[pair] = part_out[pair]
    for step in range(pairs - 1):
        wait_recv(part_in.at[order(step)], part_recv_sem.at[order(step)])
    total = None
    for source in range(pairs):
        layer = tuple(
            jnp.where(pair == source, part_own[c], part_in[source, c].astype(jnp.float32))
            for c in range(4)
        )
        total = layer if total is None else over(total, layer)
    for channel in range(4):
        out_ref[channel] = total[channel]
    for copy in sends:
        copy.wait_send()
    for end in range(2):

        @pl.when(sides[end])
        def _():
            for which in range(PAIR):
                edge(end, which).wait_send()

    for step in range(pairs - 1):
        send_part(step).wait_send()

    for chunk in range(pairs):

        @pl.when(to_below)
        def _():
            for which in range(PAIR):
                halo(which, -1, chunk).wait_send()

        @pl.when(to_above)
        def _():
            for which in range(PAIR):
                halo(which, 1, chunk).wait_send()


def render(vorticity, tf_color, tf_extinction):
    depth_count = lax.axis_size("depth")
    tile_count = lax.axis_size("tile")
    local_slices, tile_rows, tile_cols = vorticity.shape
    rows = tile_rows // depth_count
    group = local_slices * rows
    pairs = depth_count // PAIR
    dma = pltpu.SemaphoreType.DMA
    return pl.pallas_call(
        functools.partial(render_kernel, depth_count, tile_count),
        out_shape=pltpu.VMEM((4, rows, tile_cols), jnp.float32),
        in_specs=[
            pl.BlockSpec(memory_space=pltpu.HBM),
            pl.BlockSpec(memory_space=pltpu.HBM),
            pl.BlockSpec(memory_space=pltpu.HBM),
        ],
        out_specs=pl.BlockSpec(memory_space=pltpu.VMEM),
        scratch_shapes=[
            pltpu.SMEM(tf_color.shape, jnp.float32),
            pltpu.SMEM(tf_extinction.shape, jnp.float32),
            pltpu.VMEM((local_slices, pairs, PAIR, rows, tile_cols), jnp.bfloat16),
            pltpu.VMEM((pairs, PAIR * local_slices + 2, rows, tile_cols), jnp.bfloat16),
            pltpu.VMEM((PAIR, pairs, 2 * local_slices, tile_cols), jnp.bfloat16),
            pltpu.VMEM((PAIR, pairs, 2 * local_slices, tile_cols), jnp.bfloat16),
            pltpu.VMEM((2, PAIR, pairs, 1, group), jnp.float32),
            pltpu.VMEM((2, PAIR, pairs, 1, group), jnp.float32),
            pltpu.VMEM((pairs, 4, rows, tile_cols), jnp.bfloat16),
            pltpu.VMEM((pairs, 4, rows, tile_cols), jnp.bfloat16),
            pltpu.VMEM((4, rows, tile_cols), jnp.float32),
            dma,
            dma((2,)),
            dma((pairs,)),
            dma((pairs,)),
            dma((pairs,)),
            dma,
            dma,
            dma((2, PAIR)),
            dma((2, PAIR)),
            dma((PAIR, pairs)),
            dma((2, pairs)),
            dma((pairs,)),
            dma((pairs,)),
            pltpu.SemaphoreType.REGULAR((2, max(pairs - 2, 1))),
        ],
        compiler_params=pltpu.CompilerParams(collective_id=0, has_side_effects=True, vmem_limit_bytes=VMEM_BYTES),
        name="render",
    )(*(pltpu.with_memory_space_constraint(given, pltpu.HBM) for given in (vorticity.reshape(local_slices, pairs, PAIR, rows, tile_cols), tf_color, tf_extinction)))


def fits(vorticity, knots):
    local_slices, tile_rows, tile_cols = vorticity.shape
    depth_count = lax.axis_size("depth")
    rows = tile_rows // depth_count
    return (
        tile_rows % depth_count == 0
        and rows % (2 * SUBLANES) == 0
        and tile_cols % LANES == 0
        and (local_slices * rows) % LANES == 0
        and 2 * local_slices == SUBLANES
        and knots <= LANES
        and depth_count % PAIR == 0
        and depth_count & (depth_count - 1) == 0
        and depth_count <= 16
        and lax.axis_size("tile") > 1
    )


def choose(vorticity, tf_color, tf_extinction):
    if fits(vorticity, tf_extinction.shape[0]):
        return render(vorticity, tf_color, tf_extinction)
    return local(vorticity, tf_color, tf_extinction)


def solution(mesh):
    placed = (P("depth", None, "tile"), P(), P())
    return jax.shard_map(
        choose, mesh=mesh, in_specs=placed, out_specs=P(None, "depth", "tile"), check_vma=False
    )
```

```python
import functools

import jax
import jax.numpy as jnp
from jax import lax
from jax.experimental import pallas as pl
from jax.experimental.pallas import tpu as pltpu
from jax.sharding import PartitionSpec as P


def extended(cells, sides, width):
    for axis, dim in sides:
        count = lax.axis_size(axis)
        ends = count - 1
        head = lax.slice_in_dim(cells, 0, width, axis=dim)
        tail = lax.slice_in_dim(cells, cells.shape[dim] - width, cells.shape[dim], axis=dim)
        cells = jnp.concatenate(
            [
                lax.ppermute(tail, axis, [(i, (i + 1) % count) for i in range(ends)]),
                cells,
                lax.ppermute(head, axis, [((i + 1) % count, i) for i in range(ends)]),
            ],
            axis=dim,
        )
    return cells


def shade_sample(slab_below, slab_here, slab_above, tf_color, tf_extinction, thickness):
    middle = slab_here.astype(jnp.float32)
    grad_z = 0.5 * (
        slab_above[1:-1, 1:-1].astype(jnp.float32) - slab_below[1:-1, 1:-1].astype(jnp.float32)
    )
    grad_x = 0.5 * (middle[2:, 1:-1] - middle[:-2, 1:-1])
    grad_y = 0.5 * (middle[1:-1, 2:] - middle[1:-1, :-2])
    scalar = middle[1:-1, 1:-1]
    facing = 0.48 * grad_x + 0.6 * grad_y + 0.64 * grad_z
    lighting = 0.55 + 0.45 * facing / jnp.sqrt(
        grad_x * grad_x + grad_y * grad_y + grad_z * grad_z + 0.25
    )
    count_knots = tf_extinction.shape[0]
    position = jnp.clip((scalar + 4.0) * ((count_knots - 1) / 8.0), 0.0, count_knots - 1.0)
    knot_points = jnp.arange(count_knots, dtype=jnp.float32)
    weights = jnp.maximum(0.0, 1.0 - jnp.abs(position[None] - knot_points[:, None, None]))
    colour_mix = jnp.einsum("ck,kxy->cxy", tf_color, weights, precision=lax.Precision.HIGHEST)
    extinction = jnp.einsum("k,kxy->xy", tf_extinction, weights, precision=lax.Precision.HIGHEST)
    opacity = 1.0 - jnp.exp(-extinction * thickness)
    return jnp.concatenate([opacity[None] * lighting[None] * colour_mix, opacity[None]], axis=0)


def composite(nearer, farther):
    return nearer + (1.0 - nearer[3:4]) * farther


def local(vorticity, tf_color, tf_extinction):
    depth_count = lax.axis_size("depth")
    local_slices = vorticity.shape[0]
    tile_rows = vorticity.shape[1]
    tile_cols = vorticity.shape[2]
    thickness = 1.0 / (local_slices * depth_count)
    padded = extended(vorticity, (("depth", 0), ("tile", 2)), 1)
    widened = jnp.pad(padded, ((0, 0), (1, 1), (0, 0)))

    def march(slice_index, accumulated):
        slab_below = lax.dynamic_index_in_dim(widened, slice_index, 0, keepdims=False)
        slab_here = lax.dynamic_index_in_dim(widened, slice_index + 1, 0, keepdims=False)
        slab_above = lax.dynamic_index_in_dim(widened, slice_index + 2, 0, keepdims=False)
        sample = shade_sample(slab_below, slab_here, slab_above, tf_color, tf_extinction, thickness)
        return composite(accumulated, sample)

    blank_image = jnp.zeros((4, tile_rows, tile_cols), jnp.float32)
    partial_value = lax.fori_loop(0, local_slices, march, blank_image)
    block_rows = tile_rows // depth_count
    rounds = depth_count.bit_length() - 1
    stacked = partial_value.reshape(4, 1, tile_rows, tile_cols)
    pieces = lax.all_to_all(
        stacked.astype(jnp.bfloat16), "depth", split_axis=2, concat_axis=1, tiled=True
    ).astype(stacked.dtype)
    for halving in range(rounds):
        paired = pieces.reshape(4, pieces.shape[1] // 2, 2, block_rows, tile_cols)
        pieces = composite(paired[:, :, 0], paired[:, :, 1])
    final_image = pieces[:, 0]
    return final_image


MESH = pl.DeviceIdType.MESH
LANES = 128
PAIR = 2
HALVES = 2
SUBLANES = 8
VMEM_BYTES = 24 * 2**20


def iota(shape, dim):
    return lax.broadcasted_iota(jnp.int32, shape, dim)


def stencil(chosen_up, chosen_down):
    return jnp.where(chosen_up, 0.5, jnp.where(chosen_down, -0.5, 0.0))


def render_kernel(
    depth_count,
    tile_count,
    vort_hbm,
    color_hbm,
    extinction_hbm,
    out_ref,
    color_ref,
    extinction_ref,
    brick,
    slabs,
    row_out,
    row_in,
    edge_out,
    edge_in,
    part_out,
    part_in,
    part_own,
    local_sem,
    table_sem,
    own_sem,
    send_sem,
    recv_sem,
    row_send_sem,
    row_recv_sem,
    edge_send_sem,
    edge_recv_sem,
    halo_send_sem,
    halo_recv_sem,
    part_send_sem,
    part_recv_sem,
    far_sem,
):
    local_slices, pairs, _, _, slim, tile_cols = vort_hbm.shape
    rows = HALVES * slim
    tile_rows = depth_count * rows
    knots = extinction_hbm.shape[0]
    thickness = 1.0 / (local_slices * depth_count)
    group = local_slices * rows
    pair_slices = PAIR * local_slices
    depth = lax.axis_index("depth")
    tile = lax.axis_index("tile")
    pair = depth // PAIR
    member = depth % PAIR
    mate = 1 - member
    left = tile - 1
    right = tile + 1
    has_below = pair > 0
    has_above = pair < pairs - 1
    has_left = tile > 0
    has_right = tile < tile_count - 1

    whole = pltpu.make_async_copy(vort_hbm, brick, local_sem)
    whole.start()
    loads = [
        pltpu.make_async_copy(color_hbm, color_ref, table_sem.at[0]),
        pltpu.make_async_copy(extinction_hbm, extinction_ref, table_sem.at[1]),
    ]
    for copy in loads:
        copy.start()

    def slot(chunk, which, half):
        return slabs.at[chunk, half, pl.ds(1 + which * local_slices, local_slices)]

    own = [
        pltpu.make_async_copy(
            vort_hbm.at[:, chunk, member, half], slot(chunk, member, half), own_sem.at[chunk, half]
        )
        for chunk in range(pairs)
        for half in range(HALVES)
    ]
    for copy in own:
        copy.start()

    barrier = pltpu.get_barrier_semaphore()

    def greet(there, peers):
        @pl.when(there)
        def _():
            for peer in peers:
                pl.semaphore_signal(barrier, inc=1, device_id=peer, device_id_type=MESH)

    def both(place, column):
        return [(place * PAIR + which, column) for which in range(PAIR)]

    greet(has_left, both(pair, left))
    greet(has_right, both(pair, right))
    greet(has_below, both(pair - 1, tile))
    greet(has_above, both(pair + 1, tile))
    pl.semaphore_signal(barrier, inc=1, device_id=(pair * PAIR + mate, tile), device_id_type=MESH)
    greeted = 1
    for there in (has_left, has_right, has_below, has_above):
        greeted = greeted + PAIR * there.astype(jnp.int32)

    def tell(there, place, sem):
        @pl.when(there)
        def _():
            pl.semaphore_signal(sem, inc=1, device_id=(place * PAIR + member, tile), device_id_type=MESH)

    def hear(there, sem):
        @pl.when(there)
        def _():
            pl.semaphore_wait(sem, 1)


    def remote(src, dst, sent, received, target):
        return pltpu.make_async_remote_copy(
            src_ref=src,
            dst_ref=dst,
            send_sem=sent,
            recv_sem=received,
            device_id=target,
            device_id_type=MESH,
        )

    def order(step, place=None):
        place = pair if place is None else place
        turn = jnp.where(place == 0, 0, jnp.where(place == 1, pairs - 1, place - 1))
        at = step + (step >= turn).astype(jnp.int32)
        chunk = jnp.where(at == 0, 0, jnp.where(at == pairs - 1, 1, at + 1))
        return jnp.where(step == pairs - 1, place, chunk)

    sends = []

    def halo(which, beyond, chunk):
        at = PAIR * local_slices + 1 if beyond < 0 else 0
        return remote(
            vort_hbm.at[0 if beyond < 0 else local_slices - 1, chunk, which],
            slabs.at[chunk, :, at],
            halo_send_sem.at[which, chunk],
            halo_recv_sem.at[0 if beyond > 0 else 1, chunk],
            ((pair + beyond) * PAIR + which, tile),
        )

    to_below = (member == 0) & (pair > 0)
    to_above = (member == PAIR - 1) & (pair < pairs - 1)

    def push(step):

        @pl.when(to_below)
        def _():
            for which in range(PAIR):
                halo(which, -1, order(step, pair - 1)).start()

        @pl.when(to_above)
        def _():
            for which in range(PAIR):
                halo(which, 1, order(step, pair + 1)).start()

        chunk = order(step)
        copy = remote(
            row_out.at[mate, chunk],
            row_in.at[member, chunk],
            row_send_sem.at[step],
            row_recv_sem.at[chunk],
            (pair * PAIR + mate, tile),
        )
        copy.start()
        sends.append(copy)
        for half in range(HALVES):
            copy = remote(
                vort_hbm.at[:, chunk, mate, half],
                slot(chunk, member, half),
                send_sem.at[step, half],
                recv_sem.at[chunk, half],
                (pair * PAIR + mate, tile),
            )
            copy.start()
            sends.append(copy)

    whole.wait()
    packed = depth_count * HALVES * 2 * local_slices
    line = iota((packed, 1), 0)
    line_block = line // (2 * local_slices)
    line_slice = (line % (2 * local_slices)) // 2
    line_row = line_block * slim + jnp.where(line % 2 == 0, -1, slim)
    inside = (line_row >= 0) & (line_row < tile_rows)
    wanted = jnp.where(inside, line_slice * tile_rows + line_row, -1)
    pick = jnp.where(iota((packed, local_slices * tile_rows), 1) == wanted, 1.0, 0.0)
    flat = brick[...].reshape(local_slices * tile_rows, tile_cols)
    outside = jnp.dot(pick.astype(jnp.bfloat16), flat, preferred_element_type=jnp.float32)
    for block in range(depth_count):
        for half in range(HALVES):
            first = (block * HALVES + half) * 2 * local_slices
            row_out[block % PAIR, block // PAIR, half] = outside[first : first + 2 * local_slices].astype(
                jnp.bfloat16
            )
    column = iota((SUBLANES, tile_cols), 1)
    ends = iota((SUBLANES, tile_cols), 0)
    pick_ends = ((ends == 0) & (column == 0)) | ((ends == 1) & (column == tile_cols - 1))
    by_block = jnp.concatenate(
        [
            brick[z, block // PAIR, block % PAIR, half]
            for block in range(depth_count)
            for half in range(HALVES)
            for z in range(local_slices)
        ],
        axis=0,
    )
    columns = lax.dot_general(
        jnp.where(pick_ends, 1.0, 0.0).astype(jnp.bfloat16),
        by_block,
        (((1,), (1,)), ((), ())),
        preferred_element_type=jnp.float32,
    )
    for block in range(depth_count):
        for end in range(2):
            edge_out[end, block % PAIR, block // PAIR] = columns[end : end + 1, block * group : (block + 1) * group]

    blank = jnp.zeros((pairs, HALVES, 1, slim, tile_cols), jnp.bfloat16)

    @pl.when(pair == 0)
    def _():
        slabs[:, :, 0:1] = blank

    @pl.when(pair == pairs - 1)
    def _():
        slabs[:, :, pair_slices + 1 : pair_slices + 2] = blank

    row_in[member] = row_out[member]
    pl.semaphore_wait(barrier, greeted)
    tell(has_below & has_above, pair - 1, far_sem.at[0, 0])
    tell(has_below & has_above, pair + 1, far_sem.at[1, 0])
    def edge(end, which):
        return remote(
            edge_out.at[end, which],
            edge_in.at[1 - end, member],
            edge_send_sem.at[end, which],
            edge_recv_sem.at[1 - end, member],
            (pair * PAIR + which, (left, right)[end]),
        )

    sides = (has_left, has_right)
    for end in range(2):

        @pl.when(sides[end])
        def _():
            for which in range(PAIR):
                edge(end, which).start()

        @pl.when(jnp.logical_not(sides[end]))
        def _():
            edge_in[end] = jnp.zeros(edge_in.shape[1:], jnp.float32)

    for step in range(pairs):
        push(step)

    stack = pair_slices * slim
    spread = (2 + pair_slices) * slim
    extra = 2 * pair_slices
    cell = iota((stack, spread + extra), 0)
    source = iota((stack, spread + extra), 1)
    cell_row = cell % slim
    in_slabs = source < spread
    up = in_slabs & (source == cell + slim + 1) & (cell_row < slim - 1)
    down = in_slabs & (source == cell + slim - 1) & (cell_row > 0)
    packed_line = spread + 2 * (cell // slim)
    up = up | ((source == packed_line + 1) & (cell_row == slim - 1))
    down = down | ((source == packed_line) & (cell_row == 0))
    along_x = stencil(up, down).astype(jnp.bfloat16)
    along_z = stencil(in_slabs & (source == cell + 2 * slim), in_slabs & (source == cell)).astype(jnp.bfloat16)
    to_col = iota((tile_cols, tile_cols), 1)
    from_col = iota((tile_cols, tile_cols), 0)
    along_y = stencil(from_col == to_col + 1, from_col == to_col - 1).astype(jnp.bfloat16)
    place = jnp.where(
        (ends == 0) & (column == 0),
        -0.5,
        jnp.where((ends == 1) & (column == tile_cols - 1), 0.5, 0.0),
    ).astype(jnp.bfloat16)

    for copy in loads:
        copy.wait()
    folds = slim // SUBLANES
    banks = -(-knots // SUBLANES)
    knot = iota((SUBLANES, LANES), 0)

    def wide(read, count):
        spread_out = []
        for bank in range(banks):
            value = jnp.zeros((SUBLANES, LANES), jnp.float32)
            for k in range(bank * SUBLANES, min(count, (bank + 1) * SUBLANES)):
                value = jnp.where(knot == k - bank * SUBLANES, read(k), value)
            spread_out.append(jnp.concatenate([value] * (folds * tile_cols // LANES), axis=1))
        return spread_out

    def table(read):
        return wide(read, knots), wide(lambda k: read(k + 1) - read(k), knots - 1)

    tables = [table(lambda k, c=c: color_ref[c, k]) for c in range(3)]
    tables.append(table(lambda k: -thickness * extinction_ref[k]))

    def fold(value):
        return jnp.concatenate(
            [value[first : first + SUBLANES] for first in range(0, slim, SUBLANES)], axis=1
        )

    def unfold(value):
        return jnp.concatenate(
            [value[:, first * tile_cols : (first + 1) * tile_cols] for first in range(folds)], axis=0
        )

    def pick_from(choices, index):
        found = None
        for bank, choice in enumerate(choices):
            got = jnp.take_along_axis(choice, index % SUBLANES, axis=0, mode="promise_in_bounds")
            found = got if found is None else jnp.where(index >= bank * SUBLANES, got, found)
        return found

    def lookup(which, index, part):
        value, slope = tables[which]
        return pick_from(value, index) + part * pick_from(slope, index)

    def wait_recv(dst, sem):
        remote(dst, dst, local_sem, sem, (depth, tile)).wait_recv()

    for copy in own:
        copy.wait()

    for end in range(2):

        @pl.when(sides[end])
        def _():
            for which in range(PAIR):
                wait_recv(edge_in.at[end, which], edge_recv_sem.at[end, which])

    hear(pair < pairs - 2, far_sem.at[0, 0])
    hear(pair >= 2, far_sem.at[1, 0])
    for reach in range(1, pairs - 2):
        tell(has_below & (pair < pairs - 1 - reach), pair - 1, far_sem.at[0, reach])
        tell(has_above & (pair > reach), pair + 1, far_sem.at[1, reach])
        hear(pair < pairs - 2 - reach, far_sem.at[0, reach])
        hear(pair >= 2 + reach, far_sem.at[1, reach])

    def over(near, far):
        clear = 1.0 - near[3]
        return tuple(n + clear * f for n, f in zip(near, far))

    def shade(chunk, half):
        cells = slabs[chunk, half, 1 : 1 + pair_slices].reshape(stack, tile_cols)
        lines = jnp.concatenate(
            [row_in[which, chunk, half].astype(jnp.float32) for which in range(PAIR)], axis=0
        ).astype(jnp.bfloat16)
        around = jnp.concatenate([slabs[chunk, half].reshape(spread, tile_cols), lines], axis=0)
        grads_x = jnp.dot(along_x, around, preferred_element_type=jnp.float32)
        grads_z = jnp.dot(along_z, around, preferred_element_type=jnp.float32)
        span = slice(half * local_slices * slim, (half + 1) * local_slices * slim)
        first, second = (
            jnp.concatenate([edge_in[end, which, chunk][:, span] for which in range(PAIR)], axis=1)
            for end in range(2)
        )
        edge_row = iota((SUBLANES, stack), 0)
        edges = jnp.where(edge_row == 0, first, jnp.where(edge_row == 1, second, 0.0))
        grads_y = jnp.dot(cells, along_y, preferred_element_type=jnp.float32) + lax.dot_general(
            edges.astype(jnp.bfloat16),
            place,
            (((0,), (0,)), ((), ())),
            preferred_element_type=jnp.float32,
        )
        partial = None
        for z in range(pair_slices):
            here = slice(z * slim, (z + 1) * slim)
            gx, gy, gz = fold(grads_x[here]), fold(grads_y[here]), fold(grads_z[here])
            scalar = fold(cells[here].astype(jnp.float32))
            facing = 0.48 * gx + 0.6 * gy + 0.64 * gz
            lighting = 0.55 + 0.45 * facing * lax.rsqrt(gx * gx + gy * gy + gz * gz + 0.25)
            position = jnp.clip((scalar + 4.0) * ((knots - 1) / 8.0), 0.0, knots - 1.0)
            index = position.astype(jnp.int32)
            part = position - index.astype(jnp.float32)
            opacity = 1.0 - jnp.exp(lookup(3, index, part))
            lit = opacity * lighting
            sample = tuple(lit * lookup(c, index, part) for c in range(3)) + (opacity,)
            partial = sample if partial is None else over(partial, sample)
        return partial

    def send_part(step, half):
        chunk = order(step)
        return remote(
            part_out.at[chunk, half],
            part_in.at[pair, half],
            part_send_sem.at[chunk, half],
            part_recv_sem.at[pair, half],
            (chunk * PAIR + member, tile),
        )

    def march(step, carry):
        chunk = order(step)

        @pl.when(pair > 0)
        def _():
            wait_recv(slabs.at[chunk, :, 0], halo_recv_sem.at[0, chunk])

        @pl.when(pair < pairs - 1)
        def _():
            wait_recv(slabs.at[chunk, :, pair_slices + 1], halo_recv_sem.at[1, chunk])

        wait_recv(row_in.at[mate, chunk], row_recv_sem.at[chunk])
        for half in range(HALVES):
            wait_recv(slot(chunk, mate, half), recv_sem.at[chunk, half])
            partial = shade(chunk, half)
            for channel in range(4):
                image = unfold(partial[channel])
                part_own[half, channel] = image
                part_out[chunk, half, channel] = image.astype(jnp.bfloat16)

            @pl.when(step < pairs - 1)
            def _():
                send_part(step, half).start()

        return carry

    lax.fori_loop(0, pairs, march, 0)
    part_in[pair] = part_out[pair]
    for half in range(HALVES):
        for step in range(pairs - 1):
            wait_recv(part_in.at[order(step), half], part_recv_sem.at[order(step), half])
        total = None
        for source in range(pairs):
            layer = tuple(
                jnp.where(pair == source, part_own[half, c], part_in[source, half, c].astype(jnp.float32))
                for c in range(4)
            )
            total = layer if total is None else over(total, layer)
        for channel in range(4):
            out_ref[channel, half * slim : (half + 1) * slim] = total[channel]
    for copy in sends:
        copy.wait_send()
    for end in range(2):

        @pl.when(sides[end])
        def _():
            for which in range(PAIR):
                edge(end, which).wait_send()

    for step in range(pairs - 1):
        for half in range(HALVES):
            send_part(step, half).wait_send()

    for chunk in range(pairs):

        @pl.when(to_below)
        def _():
            for which in range(PAIR):
                halo(which, -1, chunk).wait_send()

        @pl.when(to_above)
        def _():
            for which in range(PAIR):
                halo(which, 1, chunk).wait_send()


def render(vorticity, tf_color, tf_extinction):
    depth_count = lax.axis_size("depth")
    tile_count = lax.axis_size("tile")
    local_slices, tile_rows, tile_cols = vorticity.shape
    rows = tile_rows // depth_count
    slim = rows // HALVES
    group = local_slices * rows
    pairs = depth_count // PAIR
    dma = pltpu.SemaphoreType.DMA
    return pl.pallas_call(
        functools.partial(render_kernel, depth_count, tile_count),
        out_shape=pltpu.VMEM((4, rows, tile_cols), jnp.float32),
        in_specs=[
            pl.BlockSpec(memory_space=pltpu.HBM),
            pl.BlockSpec(memory_space=pltpu.HBM),
            pl.BlockSpec(memory_space=pltpu.HBM),
        ],
        out_specs=pl.BlockSpec(memory_space=pltpu.VMEM),
        scratch_shapes=[
            pltpu.SMEM(tf_color.shape, jnp.float32),
            pltpu.SMEM(tf_extinction.shape, jnp.float32),
            pltpu.VMEM((local_slices, pairs, PAIR, HALVES, slim, tile_cols), jnp.bfloat16),
            pltpu.VMEM((pairs, HALVES, PAIR * local_slices + 2, slim, tile_cols), jnp.bfloat16),
            pltpu.VMEM((PAIR, pairs, HALVES, 2 * local_slices, tile_cols), jnp.bfloat16),
            pltpu.VMEM((PAIR, pairs, HALVES, 2 * local_slices, tile_cols), jnp.bfloat16),
            pltpu.VMEM((2, PAIR, pairs, 1, group), jnp.float32),
            pltpu.VMEM((2, PAIR, pairs, 1, group), jnp.float32),
            pltpu.VMEM((pairs, HALVES, 4, slim, tile_cols), jnp.bfloat16),
            pltpu.VMEM((pairs, HALVES, 4, slim, tile_cols), jnp.bfloat16),
            pltpu.VMEM((HALVES, 4, slim, tile_cols), jnp.float32),
            dma,
            dma((2,)),
            dma((pairs, HALVES)),
            dma((pairs, HALVES)),
            dma((pairs, HALVES)),
            dma((pairs,)),
            dma((pairs,)),
            dma((2, PAIR)),
            dma((2, PAIR)),
            dma((PAIR, pairs)),
            dma((2, pairs)),
            dma((pairs, HALVES)),
            dma((pairs, HALVES)),
            pltpu.SemaphoreType.REGULAR((2, max(pairs - 2, 1))),
        ],
        compiler_params=pltpu.CompilerParams(collective_id=0, has_side_effects=True, vmem_limit_bytes=VMEM_BYTES),
        name="render",
    )(*(pltpu.with_memory_space_constraint(given, pltpu.HBM) for given in (vorticity.reshape(local_slices, pairs, PAIR, HALVES, slim, tile_cols), tf_color, tf_extinction)))


def fits(vorticity, knots):
    local_slices, tile_rows, tile_cols = vorticity.shape
    depth_count = lax.axis_size("depth")
    rows = tile_rows // depth_count
    return (
        tile_rows % depth_count == 0
        and rows % (HALVES * 2 * SUBLANES) == 0
        and tile_cols % LANES == 0
        and (local_slices * rows) % LANES == 0
        and 2 * local_slices == SUBLANES
        and knots <= LANES
        and depth_count % PAIR == 0
        and depth_count & (depth_count - 1) == 0
        and depth_count <= 16
        and lax.axis_size("tile") > 1
    )


def choose(vorticity, tf_color, tf_extinction):
    if fits(vorticity, tf_extinction.shape[0]):
        return render(vorticity, tf_color, tf_extinction)
    return local(vorticity, tf_color, tf_extinction)


def solution(mesh):
    placed = (P("depth", None, "tile"), P(), P())
    return jax.shard_map(
        choose, mesh=mesh, in_specs=placed, out_specs=P(None, "depth", "tile"), check_vma=False
    )
```

```python
import functools

import jax
import jax.numpy as jnp
from jax import lax
from jax.experimental import pallas as pl
from jax.experimental.pallas import tpu as pltpu
from jax.sharding import PartitionSpec as P


def extended(cells, sides, width):
    for axis, dim in sides:
        count = lax.axis_size(axis)
        ends = count - 1
        head = lax.slice_in_dim(cells, 0, width, axis=dim)
        tail = lax.slice_in_dim(cells, cells.shape[dim] - width, cells.shape[dim], axis=dim)
        cells = jnp.concatenate(
            [
                lax.ppermute(tail, axis, [(i, (i + 1) % count) for i in range(ends)]),
                cells,
                lax.ppermute(head, axis, [((i + 1) % count, i) for i in range(ends)]),
            ],
            axis=dim,
        )
    return cells


def shade_sample(slab_below, slab_here, slab_above, tf_color, tf_extinction, thickness):
    middle = slab_here.astype(jnp.float32)
    grad_z = 0.5 * (
        slab_above[1:-1, 1:-1].astype(jnp.float32) - slab_below[1:-1, 1:-1].astype(jnp.float32)
    )
    grad_x = 0.5 * (middle[2:, 1:-1] - middle[:-2, 1:-1])
    grad_y = 0.5 * (middle[1:-1, 2:] - middle[1:-1, :-2])
    scalar = middle[1:-1, 1:-1]
    facing = 0.48 * grad_x + 0.6 * grad_y + 0.64 * grad_z
    lighting = 0.55 + 0.45 * facing / jnp.sqrt(
        grad_x * grad_x + grad_y * grad_y + grad_z * grad_z + 0.25
    )
    count_knots = tf_extinction.shape[0]
    position = jnp.clip((scalar + 4.0) * ((count_knots - 1) / 8.0), 0.0, count_knots - 1.0)
    knot_points = jnp.arange(count_knots, dtype=jnp.float32)
    weights = jnp.maximum(0.0, 1.0 - jnp.abs(position[None] - knot_points[:, None, None]))
    colour_mix = jnp.einsum("ck,kxy->cxy", tf_color, weights, precision=lax.Precision.HIGHEST)
    extinction = jnp.einsum("k,kxy->xy", tf_extinction, weights, precision=lax.Precision.HIGHEST)
    opacity = 1.0 - jnp.exp(-extinction * thickness)
    return jnp.concatenate([opacity[None] * lighting[None] * colour_mix, opacity[None]], axis=0)


def composite(nearer, farther):
    return nearer + (1.0 - nearer[3:4]) * farther


def local(vorticity, tf_color, tf_extinction):
    depth_count = lax.axis_size("depth")
    local_slices = vorticity.shape[0]
    tile_rows = vorticity.shape[1]
    tile_cols = vorticity.shape[2]
    thickness = 1.0 / (local_slices * depth_count)
    padded = extended(vorticity, (("depth", 0), ("tile", 2)), 1)
    widened = jnp.pad(padded, ((0, 0), (1, 1), (0, 0)))

    def march(slice_index, accumulated):
        slab_below = lax.dynamic_index_in_dim(widened, slice_index, 0, keepdims=False)
        slab_here = lax.dynamic_index_in_dim(widened, slice_index + 1, 0, keepdims=False)
        slab_above = lax.dynamic_index_in_dim(widened, slice_index + 2, 0, keepdims=False)
        sample = shade_sample(slab_below, slab_here, slab_above, tf_color, tf_extinction, thickness)
        return composite(accumulated, sample)

    blank_image = jnp.zeros((4, tile_rows, tile_cols), jnp.float32)
    partial_value = lax.fori_loop(0, local_slices, march, blank_image)
    block_rows = tile_rows // depth_count
    rounds = depth_count.bit_length() - 1
    stacked = partial_value.reshape(4, 1, tile_rows, tile_cols)
    pieces = lax.all_to_all(
        stacked.astype(jnp.bfloat16), "depth", split_axis=2, concat_axis=1, tiled=True
    ).astype(stacked.dtype)
    for halving in range(rounds):
        paired = pieces.reshape(4, pieces.shape[1] // 2, 2, block_rows, tile_cols)
        pieces = composite(paired[:, :, 0], paired[:, :, 1])
    final_image = pieces[:, 0]
    return final_image


MESH = pl.DeviceIdType.MESH
LANES = 128
PAIR = 2
HALVES = 2
SUBLANES = 8
VMEM_BYTES = 24 * 2**20


def iota(shape, dim):
    return lax.broadcasted_iota(jnp.int32, shape, dim)


def stencil(chosen_up, chosen_down):
    return jnp.where(chosen_up, 0.5, jnp.where(chosen_down, -0.5, 0.0))


def render_kernel(
    depth_count,
    tile_count,
    vort_hbm,
    color_hbm,
    extinction_hbm,
    out_ref,
    color_ref,
    extinction_ref,
    brick,
    slabs,
    row_out,
    row_in,
    row_next,
    edge_out,
    edge_in,
    edge_next,
    part_out,
    part_in,
    part_own,
    local_sem,
    table_sem,
    own_sem,
    send_sem,
    recv_sem,
    row_send_sem,
    row_recv_sem,
    row_next_send_sem,
    row_next_recv_sem,
    edge_send_sem,
    edge_recv_sem,
    edge_next_send_sem,
    edge_next_recv_sem,
    halo_send_sem,
    halo_recv_sem,
    part_send_sem,
    part_recv_sem,
    far_sem,
):
    local_slices, pairs, _, _, slim, tile_cols = vort_hbm.shape
    rows = HALVES * slim
    tile_rows = depth_count * rows
    knots = extinction_hbm.shape[0]
    thickness = 1.0 / (local_slices * depth_count)
    group = local_slices * rows
    pair_slices = PAIR * local_slices
    depth = lax.axis_index("depth")
    tile = lax.axis_index("tile")
    pair = depth // PAIR
    member = depth % PAIR
    mate = 1 - member
    left = tile - 1
    right = tile + 1
    has_below = pair > 0
    has_above = pair < pairs - 1
    has_left = tile > 0
    has_right = tile < tile_count - 1
    towards = pair - 1 + 2 * member
    origin = pair + 1 - 2 * member
    gives = jnp.where(member == 0, pair, pairs - 1 - pair) > 0
    takes = jnp.where(member == 0, pairs - 1 - pair, pair) > 0

    whole = pltpu.make_async_copy(vort_hbm, brick, local_sem)
    whole.start()
    barrier = pltpu.get_barrier_semaphore()

    def greet(there, peers):
        @pl.when(there)
        def _():
            for peer in peers:
                pl.semaphore_signal(barrier, inc=1, device_id=peer, device_id_type=MESH)

    def both(place, column):
        return [(place * PAIR + which, column) for which in range(PAIR)]

    for there, beside in ((has_left, left), (has_right, right)):
        greet(there, both(pair, beside))
        greet(there & takes, [(origin * PAIR + member, beside)])
    greet(has_below, [((pair - 1) * PAIR + member, tile)])
    greet(has_above, [((pair + 1) * PAIR + member, tile)])
    pl.semaphore_signal(barrier, inc=1, device_id=(pair * PAIR + mate, tile), device_id_type=MESH)
    greeted = 1 + has_below.astype(jnp.int32) + has_above.astype(jnp.int32)
    for there in (has_left, has_right):
        greeted = greeted + PAIR * there.astype(jnp.int32) + (there & gives).astype(jnp.int32)

    def tell(there, place, sem):
        @pl.when(there)
        def _():
            pl.semaphore_signal(sem, inc=1, device_id=(place * PAIR + member, tile), device_id_type=MESH)

    def hear(there, sem):
        @pl.when(there)
        def _():
            pl.semaphore_wait(sem, 1)


    def remote(src, dst, sent, received, target):
        return pltpu.make_async_remote_copy(
            src_ref=src,
            dst_ref=dst,
            send_sem=sent,
            recv_sem=received,
            device_id=target,
            device_id_type=MESH,
        )

    def order(step, place=None):
        place = pair if place is None else place
        chunk = place
        for home in range(pairs):
            route = [0] * (home > 0)
            route += list(range(home - 1, 0, -1)) + list(range(pairs - 1, home, -1))
            for turn, reached in enumerate(route):
                chunk = jnp.where((place == home) & (step == turn), reached, chunk)
        return chunk

    sends = []

    def halo(chunk):
        return remote(
            vort_hbm.at[pl.ds((local_slices - 2) * member, 2), chunk, member],
            slabs.at[chunk, pl.ds(pair_slices, 2)],
            halo_send_sem.at[chunk],
            halo_recv_sem.at[chunk],
            (towards * PAIR + member, tile),
        )

    def row_halo(chunk):
        return remote(
            row_out.at[member, chunk],
            row_next.at[chunk],
            row_next_send_sem.at[chunk],
            row_next_recv_sem.at[chunk],
            (towards * PAIR + member, tile),
        )

    def push(step):

        @pl.when(gives)
        def _():
            row_halo(order(step, towards)).start()
            halo(order(step, towards)).start()

        chunk = order(step)
        copy = remote(
            row_out.at[mate, chunk],
            row_in.at[member, chunk],
            row_send_sem.at[step],
            row_recv_sem.at[chunk],
            (pair * PAIR + mate, tile),
        )
        copy.start()
        sends.append(copy)
        for half in range(HALVES):
            copy = remote(
                vort_hbm.at[:, chunk, mate, half],
                slot(chunk, member, half),
                send_sem.at[step, half],
                recv_sem.at[chunk, half],
                (pair * PAIR + mate, tile),
            )
            copy.start()
            sends.append(copy)

    loads = [
        pltpu.make_async_copy(color_hbm, color_ref, table_sem.at[0]),
        pltpu.make_async_copy(extinction_hbm, extinction_ref, table_sem.at[1]),
    ]
    for copy in loads:
        copy.start()

    def slot(chunk, which, half):
        return slabs.at[chunk, pl.ds(which * local_slices, local_slices), half]

    own = [
        pltpu.make_async_copy(
            vort_hbm.at[:, chunk, member, half], slot(chunk, member, half), own_sem.at[chunk, half]
        )
        for chunk in range(pairs)
        for half in range(HALVES)
    ]
    for copy in own:
        copy.start()

    whole.wait()
    packed = depth_count * HALVES * 2 * local_slices
    line = iota((packed, 1), 0)
    line_block = line // (2 * local_slices)
    line_slice = (line % (2 * local_slices)) // 2
    line_row = line_block * slim + jnp.where(line % 2 == 0, -1, slim)
    inside = (line_row >= 0) & (line_row < tile_rows)
    wanted = jnp.where(inside, line_slice * tile_rows + line_row, -1)
    pick = jnp.where(iota((packed, local_slices * tile_rows), 1) == wanted, 1.0, 0.0)
    flat = brick[...].reshape(local_slices * tile_rows, tile_cols)
    outside = jnp.dot(pick.astype(jnp.bfloat16), flat, preferred_element_type=jnp.float32)
    for block in range(depth_count):
        for half in range(HALVES):
            first = (block * HALVES + half) * 2 * local_slices
            row_out[block % PAIR, block // PAIR, half] = outside[first : first + 2 * local_slices].astype(
                jnp.bfloat16
            )
    column = iota((SUBLANES, tile_cols), 1)
    ends = iota((SUBLANES, tile_cols), 0)
    pick_ends = ((ends == 0) & (column == 0)) | ((ends == 1) & (column == tile_cols - 1))
    by_block = jnp.concatenate(
        [
            brick[z, block // PAIR, block % PAIR, half]
            for block in range(depth_count)
            for half in range(HALVES)
            for z in range(local_slices)
        ],
        axis=0,
    )
    columns = lax.dot_general(
        jnp.where(pick_ends, 1.0, 0.0).astype(jnp.bfloat16),
        by_block,
        (((1,), (1,)), ((), ())),
        preferred_element_type=jnp.float32,
    )
    for block in range(depth_count):
        for end in range(2):
            edge_out[end, block % PAIR, block // PAIR] = columns[end : end + 1, block * group : (block + 1) * group]

    @pl.when(jnp.logical_not(takes))
    def _():
        slabs[:, pair_slices:] = jnp.zeros((pairs, 2, HALVES, slim, tile_cols), jnp.bfloat16)
        row_next[...] = jnp.zeros(row_next.shape, jnp.bfloat16)

    row_in[member] = row_out[member]
    pl.semaphore_wait(barrier, greeted)
    tell(has_below & has_above, pair - 1, far_sem.at[0, 0])
    tell(has_below & has_above, pair + 1, far_sem.at[1, 0])
    def edge(end, which):
        return remote(
            edge_out.at[end, which],
            edge_in.at[1 - end, member],
            edge_send_sem.at[end, which],
            edge_recv_sem.at[1 - end, member],
            (pair * PAIR + which, (left, right)[end]),
        )

    def edge_halo(end):
        return remote(
            edge_out.at[end, member],
            edge_next.at[1 - end],
            edge_next_send_sem.at[end],
            edge_next_recv_sem.at[1 - end],
            (towards * PAIR + member, (left, right)[end]),
        )

    sides = (has_left, has_right)
    for end in range(2):

        @pl.when(sides[end])
        def _():
            for which in range(PAIR):
                edge(end, which).start()

        @pl.when(sides[end] & gives)
        def _():
            edge_halo(end).start()

        @pl.when(jnp.logical_not(sides[end]))
        def _():
            edge_in[end] = jnp.zeros(edge_in.shape[1:], jnp.float32)

        @pl.when(jnp.logical_not(sides[end] & takes))
        def _():
            edge_next[end] = jnp.zeros(edge_next.shape[1:], jnp.float32)

    for step in range(pairs):
        push(step)

    stack = (pair_slices + 1) * slim
    spread = (pair_slices + 2) * slim
    lined = 2 * (pair_slices + local_slices)
    extra = -(-lined // (2 * SUBLANES)) * 2 * SUBLANES
    cell = iota((stack, spread + extra), 0)
    source = iota((stack, spread + extra), 1)
    cell_row = cell % slim
    source_row = source % slim
    slot_of = cell // slim
    slice_of = jnp.where(source < spread, source // slim, -2)
    added = slot_of == pair_slices
    last = slot_of == pair_slices - 1
    home = jnp.where(added, pair_slices + member, slot_of)
    up = (slice_of == home) & (source_row == cell_row + 1)
    down = (slice_of == home) & (source_row == cell_row - 1)
    packed_line = spread + 2 * slot_of + jnp.where(added, 2 * (local_slices - 1) * member, 0)
    up = up | ((source == packed_line + 1) & (cell_row == slim - 1))
    down = down | ((source == packed_line) & (cell_row == 0))
    along_x = stencil(up, down).astype(jnp.bfloat16)
    behind = jnp.where(
        added,
        jnp.where(member == 0, pair_slices + 1, 0),
        jnp.where(last & (member == 1), -1, slot_of + 1),
    )
    ahead = jnp.where(
        added,
        jnp.where(member == 0, pair_slices - 1, pair_slices),
        jnp.where((slot_of == 0) & (member == 1), pair_slices + 1, slot_of - 1),
    )
    same_row = source_row == cell_row
    along_z = stencil((slice_of == behind) & same_row, (slice_of == ahead) & same_row).astype(jnp.bfloat16)
    keep_first = ((member == 1) | (pair == 0)).astype(jnp.float32)
    keep_last = ((member == 0) | (pair == pairs - 1)).astype(jnp.float32)
    keep_added = takes.astype(jnp.float32)
    to_col = iota((tile_cols, tile_cols), 1)
    from_col = iota((tile_cols, tile_cols), 0)
    along_y = stencil(from_col == to_col + 1, from_col == to_col - 1).astype(jnp.bfloat16)
    place = jnp.where(
        (ends == 0) & (column == 0),
        -0.5,
        jnp.where((ends == 1) & (column == tile_cols - 1), 0.5, 0.0),
    ).astype(jnp.bfloat16)

    for copy in loads:
        copy.wait()
    folds = slim // SUBLANES
    banks = -(-knots // SUBLANES)
    knot = iota((SUBLANES, LANES), 0)

    def wide(read, count):
        spread_out = []
        for bank in range(banks):
            value = jnp.zeros((SUBLANES, LANES), jnp.float32)
            for k in range(bank * SUBLANES, min(count, (bank + 1) * SUBLANES)):
                value = jnp.where(knot == k - bank * SUBLANES, read(k), value)
            spread_out.append(jnp.concatenate([value] * (folds * tile_cols // LANES), axis=1))
        return spread_out

    def table(read):
        return wide(read, knots), wide(lambda k: read(k + 1) - read(k), knots - 1)

    tables = [table(lambda k, c=c: color_ref[c, k]) for c in range(3)]
    tables.append(table(lambda k: -thickness * extinction_ref[k]))

    def fold(value):
        return jnp.concatenate(
            [value[first : first + SUBLANES] for first in range(0, slim, SUBLANES)], axis=1
        )

    def unfold(value):
        return jnp.concatenate(
            [value[:, first * tile_cols : (first + 1) * tile_cols] for first in range(folds)], axis=0
        )

    def pick_from(choices, index):
        found = None
        for bank, choice in enumerate(choices):
            got = jnp.take_along_axis(choice, index % SUBLANES, axis=0, mode="promise_in_bounds")
            found = got if found is None else jnp.where(index >= bank * SUBLANES, got, found)
        return found

    def lookup(which, index, part):
        value, slope = tables[which]
        return pick_from(value, index) + part * pick_from(slope, index)

    def wait_recv(dst, sem):
        remote(dst, dst, local_sem, sem, (depth, tile)).wait_recv()

    for copy in own:
        copy.wait()

    for end in range(2):

        @pl.when(sides[end])
        def _():
            for which in range(PAIR):
                wait_recv(edge_in.at[end, which], edge_recv_sem.at[end, which])

        @pl.when(sides[end] & takes)
        def _():
            wait_recv(edge_next.at[end], edge_next_recv_sem.at[end])

    hear(pair < pairs - 2, far_sem.at[0, 0])
    hear(pair >= 2, far_sem.at[1, 0])
    for reach in range(1, pairs - 2):
        tell(has_below & (pair < pairs - 1 - reach), pair - 1, far_sem.at[0, reach])
        tell(has_above & (pair > reach), pair + 1, far_sem.at[1, reach])
        hear(pair < pairs - 2 - reach, far_sem.at[0, reach])
        hear(pair >= 2 + reach, far_sem.at[1, reach])

    def over(near, far):
        clear = 1.0 - near[3]
        return tuple(n + clear * f for n, f in zip(near, far))

    def shade(chunk, half):
        filled = slabs[chunk, :, half].reshape(spread, tile_cols)
        cells = jnp.concatenate(
            [filled[: pair_slices * slim], slabs[chunk, pair_slices + member, half]], axis=0
        )
        lines = [row_in[which, chunk, half].astype(jnp.float32) for which in range(PAIR)]
        lines.append(row_next[chunk, half].astype(jnp.float32))
        lines.append(jnp.zeros((extra - lined, tile_cols), jnp.float32))
        around = jnp.concatenate([filled, jnp.concatenate(lines, axis=0).astype(jnp.bfloat16)], axis=0)
        grads_x = jnp.dot(along_x, around, preferred_element_type=jnp.float32)
        grads_z = jnp.dot(along_z, around, preferred_element_type=jnp.float32)
        start = half * local_slices * slim
        stop = start + local_slices * slim
        first, second = (
            jnp.concatenate(
                [edge_in[end, which, chunk][:, start:stop] for which in range(PAIR)]
                + [
                    jnp.where(
                        member == 0,
                        edge_next[end, chunk][:, start : start + slim],
                        edge_next[end, chunk][:, stop - slim : stop],
                    )
                ],
                axis=1,
            )
            for end in range(2)
        )
        edge_row = iota((SUBLANES, stack), 0)
        edges = jnp.where(edge_row == 0, first, jnp.where(edge_row == 1, second, 0.0))
        grads_y = jnp.dot(cells, along_y, preferred_element_type=jnp.float32) + lax.dot_general(
            edges.astype(jnp.bfloat16),
            place,
            (((0,), (0,)), ((), ())),
            preferred_element_type=jnp.float32,
        )
        partial = None
        for z in range(pair_slices + 1):
            here = slice(z * slim, (z + 1) * slim)
            gx, gy, gz = fold(grads_x[here]), fold(grads_y[here]), fold(grads_z[here])
            scalar = fold(cells[here].astype(jnp.float32))
            facing = 0.48 * gx + 0.6 * gy + 0.64 * gz
            lighting = 0.55 + 0.45 * facing * lax.rsqrt(gx * gx + gy * gy + gz * gz + 0.25)
            position = jnp.clip((scalar + 4.0) * ((knots - 1) / 8.0), 0.0, knots - 1.0)
            index = position.astype(jnp.int32)
            part = position - index.astype(jnp.float32)
            opacity = 1.0 - jnp.exp(lookup(3, index, part))
            if z == 0:
                opacity = keep_first * opacity
            if z == pair_slices - 1:
                opacity = keep_last * opacity
            if z == pair_slices:
                opacity = keep_added * opacity
            lit = opacity * lighting
            sample = tuple(lit * lookup(c, index, part) for c in range(3)) + (opacity,)
            if z == pair_slices:
                near = tuple(jnp.where(member == 0, p, t) for p, t in zip(partial, sample))
                sample = tuple(jnp.where(member == 0, t, p) for p, t in zip(partial, sample))
                partial = near
            partial = sample if partial is None else over(partial, sample)
        return partial

    def send_part(step, half):
        chunk = order(step)
        return remote(
            part_out.at[chunk, half],
            part_in.at[pair, half],
            part_send_sem.at[chunk, half],
            part_recv_sem.at[pair, half],
            (chunk * PAIR + member, tile),
        )

    def march(step, carry):
        chunk = order(step)

        @pl.when(takes)
        def _():
            wait_recv(row_next.at[chunk], row_next_recv_sem.at[chunk])
            wait_recv(slabs.at[chunk, pl.ds(pair_slices, 2)], halo_recv_sem.at[chunk])

        wait_recv(row_in.at[mate, chunk], row_recv_sem.at[chunk])
        for half in range(HALVES):
            wait_recv(slot(chunk, mate, half), recv_sem.at[chunk, half])
            partial = shade(chunk, half)
            for channel in range(4):
                image = unfold(partial[channel])
                part_own[half, channel] = image
                part_out[chunk, half, channel] = image.astype(jnp.bfloat16)

            @pl.when(step < pairs - 1)
            def _():
                send_part(step, half).start()

        return carry

    lax.fori_loop(0, pairs, march, 0)
    part_in[pair] = part_out[pair]
    for copy in sends:
        copy.wait_send()
    for end in range(2):

        @pl.when(sides[end])
        def _():
            for which in range(PAIR):
                edge(end, which).wait_send()

        @pl.when(sides[end] & gives)
        def _():
            edge_halo(end).wait_send()

    for step in range(pairs - 1):
        for half in range(HALVES):
            send_part(step, half).wait_send()

    @pl.when(gives)
    def _():
        for chunk in range(pairs):
            halo(chunk).wait_send()
            row_halo(chunk).wait_send()

    for half in range(HALVES):
        for step in range(pairs - 1):
            wait_recv(part_in.at[order(step), half], part_recv_sem.at[order(step), half])
        total = None
        for source in range(pairs):
            layer = tuple(
                jnp.where(pair == source, part_own[half, c], part_in[source, half, c].astype(jnp.float32))
                for c in range(4)
            )
            total = layer if total is None else over(total, layer)
        for channel in range(4):
            out_ref[channel, half * slim : (half + 1) * slim] = total[channel]


def render(vorticity, tf_color, tf_extinction):
    depth_count = lax.axis_size("depth")
    tile_count = lax.axis_size("tile")
    local_slices, tile_rows, tile_cols = vorticity.shape
    rows = tile_rows // depth_count
    slim = rows // HALVES
    group = local_slices * rows
    pairs = depth_count // PAIR
    dma = pltpu.SemaphoreType.DMA
    return pl.pallas_call(
        functools.partial(render_kernel, depth_count, tile_count),
        out_shape=pltpu.VMEM((4, rows, tile_cols), jnp.float32),
        in_specs=[
            pl.BlockSpec(memory_space=pltpu.HBM),
            pl.BlockSpec(memory_space=pltpu.HBM),
            pl.BlockSpec(memory_space=pltpu.HBM),
        ],
        out_specs=pl.BlockSpec(memory_space=pltpu.VMEM),
        scratch_shapes=[
            pltpu.SMEM(tf_color.shape, jnp.float32),
            pltpu.SMEM(tf_extinction.shape, jnp.float32),
            pltpu.VMEM((local_slices, pairs, PAIR, HALVES, slim, tile_cols), jnp.bfloat16),
            pltpu.VMEM((pairs, PAIR * local_slices + 2, HALVES, slim, tile_cols), jnp.bfloat16),
            pltpu.VMEM((PAIR, pairs, HALVES, 2 * local_slices, tile_cols), jnp.bfloat16),
            pltpu.VMEM((PAIR, pairs, HALVES, 2 * local_slices, tile_cols), jnp.bfloat16),
            pltpu.VMEM((pairs, HALVES, 2 * local_slices, tile_cols), jnp.bfloat16),
            pltpu.VMEM((2, PAIR, pairs, 1, group), jnp.float32),
            pltpu.VMEM((2, PAIR, pairs, 1, group), jnp.float32),
            pltpu.VMEM((2, pairs, 1, group), jnp.float32),
            pltpu.VMEM((pairs, HALVES, 4, slim, tile_cols), jnp.bfloat16),
            pltpu.VMEM((pairs, HALVES, 4, slim, tile_cols), jnp.bfloat16),
            pltpu.VMEM((HALVES, 4, slim, tile_cols), jnp.float32),
            dma,
            dma((2,)),
            dma((pairs, HALVES)),
            dma((pairs, HALVES)),
            dma((pairs, HALVES)),
            dma((pairs,)),
            dma((pairs,)),
            dma((pairs,)),
            dma((pairs,)),
            dma((2, PAIR)),
            dma((2, PAIR)),
            dma((2,)),
            dma((2,)),
            dma((pairs,)),
            dma((pairs,)),
            dma((pairs, HALVES)),
            dma((pairs, HALVES)),
            pltpu.SemaphoreType.REGULAR((2, max(pairs - 2, 1))),
        ],
        compiler_params=pltpu.CompilerParams(collective_id=0, has_side_effects=True, vmem_limit_bytes=VMEM_BYTES),
        name="render",
    )(*(pltpu.with_memory_space_constraint(given, pltpu.HBM) for given in (vorticity.reshape(local_slices, pairs, PAIR, HALVES, slim, tile_cols), tf_color, tf_extinction)))


def fits(vorticity, knots):
    local_slices, tile_rows, tile_cols = vorticity.shape
    depth_count = lax.axis_size("depth")
    rows = tile_rows // depth_count
    return (
        tile_rows % depth_count == 0
        and rows % (HALVES * 2 * SUBLANES) == 0
        and tile_cols % LANES == 0
        and (local_slices * rows) % LANES == 0
        and 2 * local_slices == SUBLANES
        and knots <= LANES
        and depth_count % PAIR == 0
        and depth_count & (depth_count - 1) == 0
        and depth_count <= 16
        and lax.axis_size("tile") > 1
    )


def choose(vorticity, tf_color, tf_extinction):
    if fits(vorticity, tf_extinction.shape[0]):
        return render(vorticity, tf_color, tf_extinction)
    return local(vorticity, tf_color, tf_extinction)


def solution(mesh):
    placed = (P("depth", None, "tile"), P(), P())
    return jax.shard_map(
        choose, mesh=mesh, in_specs=placed, out_specs=P(None, "depth", "tile"), check_vma=False
    )
```

```python
import functools

import jax
import jax.numpy as jnp
from jax import lax
from jax.experimental import pallas as pl
from jax.experimental.pallas import tpu as pltpu
from jax.sharding import PartitionSpec as P


def extended(cells, sides, width):
    for axis, dim in sides:
        count = lax.axis_size(axis)
        ends = count - 1
        head = lax.slice_in_dim(cells, 0, width, axis=dim)
        tail = lax.slice_in_dim(cells, cells.shape[dim] - width, cells.shape[dim], axis=dim)
        cells = jnp.concatenate(
            [
                lax.ppermute(tail, axis, [(i, (i + 1) % count) for i in range(ends)]),
                cells,
                lax.ppermute(head, axis, [((i + 1) % count, i) for i in range(ends)]),
            ],
            axis=dim,
        )
    return cells


def shade_sample(slab_below, slab_here, slab_above, tf_color, tf_extinction, thickness):
    middle = slab_here.astype(jnp.float32)
    grad_z = 0.5 * (
        slab_above[1:-1, 1:-1].astype(jnp.float32) - slab_below[1:-1, 1:-1].astype(jnp.float32)
    )
    grad_x = 0.5 * (middle[2:, 1:-1] - middle[:-2, 1:-1])
    grad_y = 0.5 * (middle[1:-1, 2:] - middle[1:-1, :-2])
    scalar = middle[1:-1, 1:-1]
    facing = 0.48 * grad_x + 0.6 * grad_y + 0.64 * grad_z
    lighting = 0.55 + 0.45 * facing / jnp.sqrt(
        grad_x * grad_x + grad_y * grad_y + grad_z * grad_z + 0.25
    )
    count_knots = tf_extinction.shape[0]
    position = jnp.clip((scalar + 4.0) * ((count_knots - 1) / 8.0), 0.0, count_knots - 1.0)
    knot_points = jnp.arange(count_knots, dtype=jnp.float32)
    weights = jnp.maximum(0.0, 1.0 - jnp.abs(position[None] - knot_points[:, None, None]))
    colour_mix = jnp.einsum("ck,kxy->cxy", tf_color, weights, precision=lax.Precision.HIGHEST)
    extinction = jnp.einsum("k,kxy->xy", tf_extinction, weights, precision=lax.Precision.HIGHEST)
    opacity = 1.0 - jnp.exp(-extinction * thickness)
    return jnp.concatenate([opacity[None] * lighting[None] * colour_mix, opacity[None]], axis=0)


def composite(nearer, farther):
    return nearer + (1.0 - nearer[3:4]) * farther


def local(vorticity, tf_color, tf_extinction):
    depth_count = lax.axis_size("depth")
    local_slices = vorticity.shape[0]
    tile_rows = vorticity.shape[1]
    tile_cols = vorticity.shape[2]
    thickness = 1.0 / (local_slices * depth_count)
    padded = extended(vorticity, (("depth", 0), ("tile", 2)), 1)
    widened = jnp.pad(padded, ((0, 0), (1, 1), (0, 0)))

    def march(slice_index, accumulated):
        slab_below = lax.dynamic_index_in_dim(widened, slice_index, 0, keepdims=False)
        slab_here = lax.dynamic_index_in_dim(widened, slice_index + 1, 0, keepdims=False)
        slab_above = lax.dynamic_index_in_dim(widened, slice_index + 2, 0, keepdims=False)
        sample = shade_sample(slab_below, slab_here, slab_above, tf_color, tf_extinction, thickness)
        return composite(accumulated, sample)

    blank_image = jnp.zeros((4, tile_rows, tile_cols), jnp.float32)
    partial_value = lax.fori_loop(0, local_slices, march, blank_image)
    block_rows = tile_rows // depth_count
    rounds = depth_count.bit_length() - 1
    stacked = partial_value.reshape(4, 1, tile_rows, tile_cols)
    pieces = lax.all_to_all(
        stacked.astype(jnp.bfloat16), "depth", split_axis=2, concat_axis=1, tiled=True
    ).astype(stacked.dtype)
    for halving in range(rounds):
        paired = pieces.reshape(4, pieces.shape[1] // 2, 2, block_rows, tile_cols)
        pieces = composite(paired[:, :, 0], paired[:, :, 1])
    final_image = pieces[:, 0]
    return final_image


MESH = pl.DeviceIdType.MESH
LANES = 128
PAIR = 2
HALVES = 2
SUBLANES = 8
VMEM_BYTES = 24 * 2**20


def iota(shape, dim):
    return lax.broadcasted_iota(jnp.int32, shape, dim)


def stencil(chosen_up, chosen_down):
    return jnp.where(chosen_up, 0.5, jnp.where(chosen_down, -0.5, 0.0))


def render_kernel(
    depth_count,
    tile_count,
    vort_hbm,
    color_hbm,
    extinction_hbm,
    out_ref,
    color_ref,
    extinction_ref,
    brick,
    slabs,
    row_out,
    row_in,
    row_next,
    edge_out,
    edge_in,
    edge_next,
    part_out,
    part_in,
    part_own,
    local_sem,
    table_sem,
    own_sem,
    send_sem,
    recv_sem,
    row_send_sem,
    row_recv_sem,
    row_next_send_sem,
    row_next_recv_sem,
    edge_send_sem,
    edge_recv_sem,
    edge_next_send_sem,
    edge_next_recv_sem,
    halo_send_sem,
    halo_recv_sem,
    part_send_sem,
    part_recv_sem,
    far_sem,
    side_sem,
):
    local_slices, pairs, _, _, slim, tile_cols = vort_hbm.shape
    rows = HALVES * slim
    tile_rows = depth_count * rows
    knots = extinction_hbm.shape[0]
    thickness = 1.0 / (local_slices * depth_count)
    group = local_slices * rows
    pair_slices = PAIR * local_slices
    depth = lax.axis_index("depth")
    tile = lax.axis_index("tile")
    pair = depth // PAIR
    member = depth % PAIR
    mate = 1 - member
    left = tile - 1
    right = tile + 1
    has_below = pair > 0
    has_above = pair < pairs - 1
    has_left = tile > 0
    has_right = tile < tile_count - 1
    towards = pair - 1 + 2 * member
    origin = pair + 1 - 2 * member
    gives = jnp.where(member == 0, pair, pairs - 1 - pair) > 0
    takes = jnp.where(member == 0, pairs - 1 - pair, pair) > 0

    whole = pltpu.make_async_copy(vort_hbm, brick, local_sem)
    whole.start()
    barrier = pltpu.get_barrier_semaphore()

    def greet(there, peers):
        @pl.when(there)
        def _():
            for peer in peers:
                pl.semaphore_signal(barrier, inc=1, device_id=peer, device_id_type=MESH)

    close = (tile % 2 == 1, tile % 2 == 0)
    for there, at_hand, beside in ((has_left, close[0], left), (has_right, close[1], right)):
        greet(there, [(pair * PAIR + member, beside)])
        greet(there & at_hand, [(pair * PAIR + mate, beside)])
        greet(there & at_hand & takes, [(origin * PAIR + member, beside)])
    greet(has_below, [((pair - 1) * PAIR + member, tile)])
    greet(has_above, [((pair + 1) * PAIR + member, tile)])
    pl.semaphore_signal(barrier, inc=1, device_id=(pair * PAIR + mate, tile), device_id_type=MESH)
    greeted = 1 + has_below.astype(jnp.int32) + has_above.astype(jnp.int32)
    for there, at_hand in ((has_left, close[0]), (has_right, close[1])):
        for known in (there, there & at_hand, there & at_hand & gives):
            greeted = greeted + known.astype(jnp.int32)

    def tell(there, place, sem):
        @pl.when(there)
        def _():
            pl.semaphore_signal(sem, inc=1, device_id=(place * PAIR + member, tile), device_id_type=MESH)

    def hear(there, sem):
        @pl.when(there)
        def _():
            pl.semaphore_wait(sem, 1)


    def remote(src, dst, sent, received, target):
        return pltpu.make_async_remote_copy(
            src_ref=src,
            dst_ref=dst,
            send_sem=sent,
            recv_sem=received,
            device_id=target,
            device_id_type=MESH,
        )

    def order(step, place=None):
        place = pair if place is None else place
        chunk = place
        for home in range(pairs):
            route = [0] * (home > 0)
            route += list(range(home - 1, 0, -1)) + list(range(pairs - 1, home, -1))
            for turn, reached in enumerate(route):
                chunk = jnp.where((place == home) & (step == turn), reached, chunk)
        return chunk

    sends = []

    def halo(chunk):
        return remote(
            vort_hbm.at[pl.ds((local_slices - 2) * member, 2), chunk, member],
            slabs.at[chunk, pl.ds(pair_slices, 2)],
            halo_send_sem.at[chunk],
            halo_recv_sem.at[chunk],
            (towards * PAIR + member, tile),
        )

    def row_halo(chunk):
        return remote(
            row_out.at[member, chunk],
            row_next.at[chunk],
            row_next_send_sem.at[chunk],
            row_next_recv_sem.at[chunk],
            (towards * PAIR + member, tile),
        )

    def push(step, between=None):

        @pl.when(gives)
        def _():
            row_halo(order(step, towards)).start()
            halo(order(step, towards)).start()

        chunk = order(step)
        copy = remote(
            row_out.at[mate, chunk],
            row_in.at[member, chunk],
            row_send_sem.at[step],
            row_recv_sem.at[chunk],
            (pair * PAIR + mate, tile),
        )
        copy.start()
        sends.append(copy)
        for half in range(HALVES):
            if half == 1 and between is not None:
                between()
            copy = remote(
                vort_hbm.at[:, chunk, mate, half],
                slot(chunk, member, half),
                send_sem.at[step, half],
                recv_sem.at[chunk, half],
                (pair * PAIR + mate, tile),
            )
            copy.start()
            sends.append(copy)

    loads = [
        pltpu.make_async_copy(color_hbm, color_ref, table_sem.at[0]),
        pltpu.make_async_copy(extinction_hbm, extinction_ref, table_sem.at[1]),
    ]
    for copy in loads:
        copy.start()

    def slot(chunk, which, half):
        return slabs.at[chunk, pl.ds(which * local_slices, local_slices), half]

    own = [
        pltpu.make_async_copy(
            vort_hbm.at[:, chunk, member, half], slot(chunk, member, half), own_sem.at[chunk, half]
        )
        for chunk in range(pairs)
        for half in range(HALVES)
    ]
    for copy in own:
        copy.start()

    whole.wait()
    packed = depth_count * HALVES * 2 * local_slices
    line = iota((packed, 1), 0)
    line_block = line // (2 * local_slices)
    line_slice = (line % (2 * local_slices)) // 2
    line_row = line_block * slim + jnp.where(line % 2 == 0, -1, slim)
    inside = (line_row >= 0) & (line_row < tile_rows)
    wanted = jnp.where(inside, line_slice * tile_rows + line_row, -1)
    pick = jnp.where(iota((packed, local_slices * tile_rows), 1) == wanted, 1.0, 0.0)
    flat = brick[...].reshape(local_slices * tile_rows, tile_cols)
    outside = jnp.dot(pick.astype(jnp.bfloat16), flat, preferred_element_type=jnp.float32)
    for block in range(depth_count):
        for half in range(HALVES):
            first = (block * HALVES + half) * 2 * local_slices
            row_out[block % PAIR, block // PAIR, half] = outside[first : first + 2 * local_slices].astype(
                jnp.bfloat16
            )
    column = iota((SUBLANES, tile_cols), 1)
    ends = iota((SUBLANES, tile_cols), 0)
    pick_ends = ((ends == 0) & (column == 0)) | ((ends == 1) & (column == tile_cols - 1))
    by_block = jnp.concatenate(
        [
            brick[z, block // PAIR, block % PAIR, half]
            for block in range(depth_count)
            for half in range(HALVES)
            for z in range(local_slices)
        ],
        axis=0,
    )
    columns = lax.dot_general(
        jnp.where(pick_ends, 1.0, 0.0).astype(jnp.bfloat16),
        by_block,
        (((1,), (1,)), ((), ())),
        preferred_element_type=jnp.float32,
    )
    for block in range(depth_count):
        for end in range(2):
            edge_out[end, block % PAIR, block // PAIR] = columns[end : end + 1, block * group : (block + 1) * group]

    @pl.when(jnp.logical_not(takes))
    def _():
        slabs[:, pair_slices:] = jnp.zeros((pairs, 2, HALVES, slim, tile_cols), jnp.bfloat16)
        row_next[...] = jnp.zeros(row_next.shape, jnp.bfloat16)

    row_in[member] = row_out[member]
    pl.semaphore_wait(barrier, greeted)
    tell(has_below & has_above, pair - 1, far_sem.at[0, 0])
    tell(has_below & has_above, pair + 1, far_sem.at[1, 0])
    sides = (has_left, has_right)
    distant = [there & jnp.logical_not(at_hand) for there, at_hand in zip(sides, close)]
    for end in range(2):

        @pl.when(distant[end])
        def _():
            pl.semaphore_signal(
                side_sem.at[1 - end],
                inc=1,
                device_id=(pair * PAIR + member, (left, right)[end]),
                device_id_type=MESH,
            )

    def edge(end, which):
        return remote(
            edge_out.at[end, which],
            edge_in.at[1 - end, member],
            edge_send_sem.at[end, which],
            edge_recv_sem.at[1 - end, member],
            (pair * PAIR + which, (left, right)[end]),
        )

    def edge_halo(end):
        return remote(
            edge_out.at[end, member],
            edge_next.at[1 - end],
            edge_next_send_sem.at[end],
            edge_next_recv_sem.at[1 - end],
            (towards * PAIR + member, (left, right)[end]),
        )

    for end in range(2):

        @pl.when(sides[end])
        def _():
            edge(end, member).start()

        @pl.when(sides[end] & close[end])
        def _():
            edge(end, mate).start()

        @pl.when(sides[end] & close[end] & gives)
        def _():
            edge_halo(end).start()

        @pl.when(jnp.logical_not(sides[end]))
        def _():
            edge_in[end] = jnp.zeros(edge_in.shape[1:], jnp.float32)

        @pl.when(jnp.logical_not(sides[end] & takes))
        def _():
            edge_next[end] = jnp.zeros(edge_next.shape[1:], jnp.float32)

    def far_edges():
        for end in range(2):
            hear(distant[end], side_sem.at[end])

            @pl.when(distant[end])
            def _():
                edge(end, mate).start()

            @pl.when(distant[end] & gives)
            def _():
                edge_halo(end).start()

    push(0, far_edges)
    for step in range(1, pairs):
        push(step)

    stack = (pair_slices + 1) * slim
    spread = (pair_slices + 2) * slim
    lined = 2 * (pair_slices + local_slices)
    extra = -(-lined // (2 * SUBLANES)) * 2 * SUBLANES
    cell = iota((stack, spread + extra), 0)
    source = iota((stack, spread + extra), 1)
    cell_row = cell % slim
    source_row = source % slim
    slot_of = cell // slim
    slice_of = jnp.where(source < spread, source // slim, -2)
    added = slot_of == pair_slices
    last = slot_of == pair_slices - 1
    home = jnp.where(added, pair_slices + member, slot_of)
    up = (slice_of == home) & (source_row == cell_row + 1)
    down = (slice_of == home) & (source_row == cell_row - 1)
    packed_line = spread + 2 * slot_of + jnp.where(added, 2 * (local_slices - 1) * member, 0)
    up = up | ((source == packed_line + 1) & (cell_row == slim - 1))
    down = down | ((source == packed_line) & (cell_row == 0))
    along_x = stencil(up, down).astype(jnp.bfloat16)
    behind = jnp.where(
        added,
        jnp.where(member == 0, pair_slices + 1, 0),
        jnp.where(last & (member == 1), -1, slot_of + 1),
    )
    ahead = jnp.where(
        added,
        jnp.where(member == 0, pair_slices - 1, pair_slices),
        jnp.where((slot_of == 0) & (member == 1), pair_slices + 1, slot_of - 1),
    )
    same_row = source_row == cell_row
    along_z = stencil((slice_of == behind) & same_row, (slice_of == ahead) & same_row).astype(jnp.bfloat16)
    keep_first = ((member == 1) | (pair == 0)).astype(jnp.float32)
    keep_last = ((member == 0) | (pair == pairs - 1)).astype(jnp.float32)
    keep_added = takes.astype(jnp.float32)
    to_col = iota((tile_cols, tile_cols), 1)
    from_col = iota((tile_cols, tile_cols), 0)
    along_y = stencil(from_col == to_col + 1, from_col == to_col - 1).astype(jnp.bfloat16)
    place = jnp.where(
        (ends == 0) & (column == 0),
        -0.5,
        jnp.where((ends == 1) & (column == tile_cols - 1), 0.5, 0.0),
    ).astype(jnp.bfloat16)

    for copy in loads:
        copy.wait()
    folds = slim // SUBLANES
    banks = -(-knots // SUBLANES)
    knot = iota((SUBLANES, LANES), 0)

    def wide(read, count):
        spread_out = []
        for bank in range(banks):
            value = jnp.zeros((SUBLANES, LANES), jnp.float32)
            for k in range(bank * SUBLANES, min(count, (bank + 1) * SUBLANES)):
                value = jnp.where(knot == k - bank * SUBLANES, read(k), value)
            spread_out.append(jnp.concatenate([value] * (folds * tile_cols // LANES), axis=1))
        return spread_out

    def table(read):
        return wide(read, knots), wide(lambda k: read(k + 1) - read(k), knots - 1)

    tables = [table(lambda k, c=c: color_ref[c, k]) for c in range(3)]
    tables.append(table(lambda k: -thickness * extinction_ref[k]))

    def fold(value):
        return jnp.concatenate(
            [value[first : first + SUBLANES] for first in range(0, slim, SUBLANES)], axis=1
        )

    def unfold(value):
        return jnp.concatenate(
            [value[:, first * tile_cols : (first + 1) * tile_cols] for first in range(folds)], axis=0
        )

    def pick_from(choices, index):
        found = None
        for bank, choice in enumerate(choices):
            got = jnp.take_along_axis(choice, index % SUBLANES, axis=0, mode="promise_in_bounds")
            found = got if found is None else jnp.where(index >= bank * SUBLANES, got, found)
        return found

    def lookup(which, index, part):
        value, slope = tables[which]
        return pick_from(value, index) + part * pick_from(slope, index)

    def wait_recv(dst, sem):
        remote(dst, dst, local_sem, sem, (depth, tile)).wait_recv()

    for copy in own:
        copy.wait()

    for end in range(2):

        @pl.when(sides[end])
        def _():
            for which in range(PAIR):
                wait_recv(edge_in.at[end, which], edge_recv_sem.at[end, which])

        @pl.when(sides[end] & takes)
        def _():
            wait_recv(edge_next.at[end], edge_next_recv_sem.at[end])

    hear(pair < pairs - 2, far_sem.at[0, 0])
    hear(pair >= 2, far_sem.at[1, 0])
    for reach in range(1, pairs - 2):
        tell(has_below & (pair < pairs - 1 - reach), pair - 1, far_sem.at[0, reach])
        tell(has_above & (pair > reach), pair + 1, far_sem.at[1, reach])
        hear(pair < pairs - 2 - reach, far_sem.at[0, reach])
        hear(pair >= 2 + reach, far_sem.at[1, reach])

    def over(near, far):
        clear = 1.0 - near[3]
        return tuple(n + clear * f for n, f in zip(near, far))

    def shade(chunk, half):
        filled = slabs[chunk, :, half].reshape(spread, tile_cols)
        cells = jnp.concatenate(
            [filled[: pair_slices * slim], slabs[chunk, pair_slices + member, half]], axis=0
        )
        lines = [row_in[which, chunk, half].astype(jnp.float32) for which in range(PAIR)]
        lines.append(row_next[chunk, half].astype(jnp.float32))
        lines.append(jnp.zeros((extra - lined, tile_cols), jnp.float32))
        around = jnp.concatenate([filled, jnp.concatenate(lines, axis=0).astype(jnp.bfloat16)], axis=0)
        grads_x = jnp.dot(along_x, around, preferred_element_type=jnp.float32)
        grads_z = jnp.dot(along_z, around, preferred_element_type=jnp.float32)
        start = half * local_slices * slim
        stop = start + local_slices * slim
        first, second = (
            jnp.concatenate(
                [edge_in[end, which, chunk][:, start:stop] for which in range(PAIR)]
                + [
                    jnp.where(
                        member == 0,
                        edge_next[end, chunk][:, start : start + slim],
                        edge_next[end, chunk][:, stop - slim : stop],
                    )
                ],
                axis=1,
            )
            for end in range(2)
        )
        edge_row = iota((SUBLANES, stack), 0)
        edges = jnp.where(edge_row == 0, first, jnp.where(edge_row == 1, second, 0.0))
        grads_y = jnp.dot(cells, along_y, preferred_element_type=jnp.float32) + lax.dot_general(
            edges.astype(jnp.bfloat16),
            place,
            (((0,), (0,)), ((), ())),
            preferred_element_type=jnp.float32,
        )
        partial = None
        for z in range(pair_slices + 1):
            here = slice(z * slim, (z + 1) * slim)
            gx, gy, gz = fold(grads_x[here]), fold(grads_y[here]), fold(grads_z[here])
            scalar = fold(cells[here].astype(jnp.float32))
            facing = 0.48 * gx + 0.6 * gy + 0.64 * gz
            lighting = 0.55 + 0.45 * facing * lax.rsqrt(gx * gx + gy * gy + gz * gz + 0.25)
            position = jnp.clip((scalar + 4.0) * ((knots - 1) / 8.0), 0.0, knots - 1.0)
            index = position.astype(jnp.int32)
            part = position - index.astype(jnp.float32)
            opacity = 1.0 - jnp.exp(lookup(3, index, part))
            if z == 0:
                opacity = keep_first * opacity
            if z == pair_slices - 1:
                opacity = keep_last * opacity
            if z == pair_slices:
                opacity = keep_added * opacity
            lit = opacity * lighting
            sample = tuple(lit * lookup(c, index, part) for c in range(3)) + (opacity,)
            if z == pair_slices:
                near = tuple(jnp.where(member == 0, p, t) for p, t in zip(partial, sample))
                sample = tuple(jnp.where(member == 0, t, p) for p, t in zip(partial, sample))
                partial = near
            partial = sample if partial is None else over(partial, sample)
        return partial

    def send_part(step, half):
        chunk = order(step)
        return remote(
            part_out.at[chunk, half],
            part_in.at[pair, half],
            part_send_sem.at[chunk, half],
            part_recv_sem.at[pair, half],
            (chunk * PAIR + member, tile),
        )

    def march(step, carry):
        chunk = order(step)

        @pl.when(takes)
        def _():
            wait_recv(row_next.at[chunk], row_next_recv_sem.at[chunk])
            wait_recv(slabs.at[chunk, pl.ds(pair_slices, 2)], halo_recv_sem.at[chunk])

        wait_recv(row_in.at[mate, chunk], row_recv_sem.at[chunk])
        for half in range(HALVES):
            wait_recv(slot(chunk, mate, half), recv_sem.at[chunk, half])
            partial = shade(chunk, half)
            for channel in range(4):
                image = unfold(partial[channel])
                part_own[half, channel] = image
                part_out[chunk, half, channel] = image.astype(jnp.bfloat16)

            @pl.when(step < pairs - 1)
            def _():
                send_part(step, half).start()

        return carry

    lax.fori_loop(0, pairs, march, 0)
    part_in[pair] = part_out[pair]
    for copy in sends:
        copy.wait_send()
    for end in range(2):

        @pl.when(sides[end])
        def _():
            for which in range(PAIR):
                edge(end, which).wait_send()

        @pl.when(sides[end] & gives)
        def _():
            edge_halo(end).wait_send()

    for step in range(pairs - 1):
        for half in range(HALVES):
            send_part(step, half).wait_send()

    @pl.when(gives)
    def _():
        for chunk in range(pairs):
            halo(chunk).wait_send()
            row_halo(chunk).wait_send()

    for half in range(HALVES):
        for step in range(pairs - 1):
            wait_recv(part_in.at[order(step), half], part_recv_sem.at[order(step), half])
        total = None
        for source in range(pairs):
            layer = tuple(
                jnp.where(pair == source, part_own[half, c], part_in[source, half, c].astype(jnp.float32))
                for c in range(4)
            )
            total = layer if total is None else over(total, layer)
        for channel in range(4):
            out_ref[channel, half * slim : (half + 1) * slim] = total[channel]


def render(vorticity, tf_color, tf_extinction):
    depth_count = lax.axis_size("depth")
    tile_count = lax.axis_size("tile")
    local_slices, tile_rows, tile_cols = vorticity.shape
    rows = tile_rows // depth_count
    slim = rows // HALVES
    group = local_slices * rows
    pairs = depth_count // PAIR
    dma = pltpu.SemaphoreType.DMA
    return pl.pallas_call(
        functools.partial(render_kernel, depth_count, tile_count),
        out_shape=pltpu.VMEM((4, rows, tile_cols), jnp.float32),
        in_specs=[
            pl.BlockSpec(memory_space=pltpu.HBM),
            pl.BlockSpec(memory_space=pltpu.HBM),
            pl.BlockSpec(memory_space=pltpu.HBM),
        ],
        out_specs=pl.BlockSpec(memory_space=pltpu.VMEM),
        scratch_shapes=[
            pltpu.SMEM(tf_color.shape, jnp.float32),
            pltpu.SMEM(tf_extinction.shape, jnp.float32),
            pltpu.VMEM((local_slices, pairs, PAIR, HALVES, slim, tile_cols), jnp.bfloat16),
            pltpu.VMEM((pairs, PAIR * local_slices + 2, HALVES, slim, tile_cols), jnp.bfloat16),
            pltpu.VMEM((PAIR, pairs, HALVES, 2 * local_slices, tile_cols), jnp.bfloat16),
            pltpu.VMEM((PAIR, pairs, HALVES, 2 * local_slices, tile_cols), jnp.bfloat16),
            pltpu.VMEM((pairs, HALVES, 2 * local_slices, tile_cols), jnp.bfloat16),
            pltpu.VMEM((2, PAIR, pairs, 1, group), jnp.float32),
            pltpu.VMEM((2, PAIR, pairs, 1, group), jnp.float32),
            pltpu.VMEM((2, pairs, 1, group), jnp.float32),
            pltpu.VMEM((pairs, HALVES, 4, slim, tile_cols), jnp.bfloat16),
            pltpu.VMEM((pairs, HALVES, 4, slim, tile_cols), jnp.bfloat16),
            pltpu.VMEM((HALVES, 4, slim, tile_cols), jnp.float32),
            dma,
            dma((2,)),
            dma((pairs, HALVES)),
            dma((pairs, HALVES)),
            dma((pairs, HALVES)),
            dma((pairs,)),
            dma((pairs,)),
            dma((pairs,)),
            dma((pairs,)),
            dma((2, PAIR)),
            dma((2, PAIR)),
            dma((2,)),
            dma((2,)),
            dma((pairs,)),
            dma((pairs,)),
            dma((pairs, HALVES)),
            dma((pairs, HALVES)),
            pltpu.SemaphoreType.REGULAR((2, max(pairs - 2, 1))),
            pltpu.SemaphoreType.REGULAR((2,)),
        ],
        compiler_params=pltpu.CompilerParams(collective_id=0, has_side_effects=True, vmem_limit_bytes=VMEM_BYTES),
        name="render",
    )(*(pltpu.with_memory_space_constraint(given, pltpu.HBM) for given in (vorticity.reshape(local_slices, pairs, PAIR, HALVES, slim, tile_cols), tf_color, tf_extinction)))


def fits(vorticity, knots):
    local_slices, tile_rows, tile_cols = vorticity.shape
    depth_count = lax.axis_size("depth")
    rows = tile_rows // depth_count
    return (
        tile_rows % depth_count == 0
        and rows % (HALVES * 2 * SUBLANES) == 0
        and tile_cols % LANES == 0
        and (local_slices * rows) % LANES == 0
        and 2 * local_slices == SUBLANES
        and knots <= LANES
        and depth_count % PAIR == 0
        and depth_count & (depth_count - 1) == 0
        and depth_count <= 16
        and lax.axis_size("tile") > 1
    )


def choose(vorticity, tf_color, tf_extinction):
    if fits(vorticity, tf_extinction.shape[0]):
        return render(vorticity, tf_color, tf_extinction)
    return local(vorticity, tf_color, tf_extinction)


def solution(mesh):
    placed = (P("depth", None, "tile"), P(), P())
    return jax.shard_map(
        choose, mesh=mesh, in_specs=placed, out_specs=P(None, "depth", "tile"), check_vma=False
    )
```

```python
import functools

import jax
import jax.numpy as jnp
from jax import lax
from jax.experimental import pallas as pl
from jax.experimental.pallas import tpu as pltpu
from jax.sharding import PartitionSpec as P


def extended(cells, sides, width):
    for axis, dim in sides:
        count = lax.axis_size(axis)
        ends = count - 1
        head = lax.slice_in_dim(cells, 0, width, axis=dim)
        tail = lax.slice_in_dim(cells, cells.shape[dim] - width, cells.shape[dim], axis=dim)
        cells = jnp.concatenate(
            [
                lax.ppermute(tail, axis, [(i, (i + 1) % count) for i in range(ends)]),
                cells,
                lax.ppermute(head, axis, [((i + 1) % count, i) for i in range(ends)]),
            ],
            axis=dim,
        )
    return cells


def shade_sample(slab_below, slab_here, slab_above, tf_color, tf_extinction, thickness):
    middle = slab_here.astype(jnp.float32)
    grad_z = 0.5 * (
        slab_above[1:-1, 1:-1].astype(jnp.float32) - slab_below[1:-1, 1:-1].astype(jnp.float32)
    )
    grad_x = 0.5 * (middle[2:, 1:-1] - middle[:-2, 1:-1])
    grad_y = 0.5 * (middle[1:-1, 2:] - middle[1:-1, :-2])
    scalar = middle[1:-1, 1:-1]
    facing = 0.48 * grad_x + 0.6 * grad_y + 0.64 * grad_z
    lighting = 0.55 + 0.45 * facing / jnp.sqrt(
        grad_x * grad_x + grad_y * grad_y + grad_z * grad_z + 0.25
    )
    count_knots = tf_extinction.shape[0]
    position = jnp.clip((scalar + 4.0) * ((count_knots - 1) / 8.0), 0.0, count_knots - 1.0)
    knot_points = jnp.arange(count_knots, dtype=jnp.float32)
    weights = jnp.maximum(0.0, 1.0 - jnp.abs(position[None] - knot_points[:, None, None]))
    colour_mix = jnp.einsum("ck,kxy->cxy", tf_color, weights, precision=lax.Precision.HIGHEST)
    extinction = jnp.einsum("k,kxy->xy", tf_extinction, weights, precision=lax.Precision.HIGHEST)
    opacity = 1.0 - jnp.exp(-extinction * thickness)
    return jnp.concatenate([opacity[None] * lighting[None] * colour_mix, opacity[None]], axis=0)


def composite(nearer, farther):
    return nearer + (1.0 - nearer[3:4]) * farther


def local(vorticity, tf_color, tf_extinction):
    depth_count = lax.axis_size("depth")
    local_slices = vorticity.shape[0]
    tile_rows = vorticity.shape[1]
    tile_cols = vorticity.shape[2]
    thickness = 1.0 / (local_slices * depth_count)
    padded = extended(vorticity, (("depth", 0), ("tile", 2)), 1)
    widened = jnp.pad(padded, ((0, 0), (1, 1), (0, 0)))

    def march(slice_index, accumulated):
        slab_below = lax.dynamic_index_in_dim(widened, slice_index, 0, keepdims=False)
        slab_here = lax.dynamic_index_in_dim(widened, slice_index + 1, 0, keepdims=False)
        slab_above = lax.dynamic_index_in_dim(widened, slice_index + 2, 0, keepdims=False)
        sample = shade_sample(slab_below, slab_here, slab_above, tf_color, tf_extinction, thickness)
        return composite(accumulated, sample)

    blank_image = jnp.zeros((4, tile_rows, tile_cols), jnp.float32)
    partial_value = lax.fori_loop(0, local_slices, march, blank_image)
    block_rows = tile_rows // depth_count
    rounds = depth_count.bit_length() - 1
    stacked = partial_value.reshape(4, 1, tile_rows, tile_cols)
    pieces = lax.all_to_all(
        stacked.astype(jnp.bfloat16), "depth", split_axis=2, concat_axis=1, tiled=True
    ).astype(stacked.dtype)
    for halving in range(rounds):
        paired = pieces.reshape(4, pieces.shape[1] // 2, 2, block_rows, tile_cols)
        pieces = composite(paired[:, :, 0], paired[:, :, 1])
    final_image = pieces[:, 0]
    return final_image


MESH = pl.DeviceIdType.MESH
LANES = 128
PAIR = 2
HALVES = 2
SUBLANES = 8
VMEM_BYTES = 24 * 2**20


def iota(shape, dim):
    return lax.broadcasted_iota(jnp.int32, shape, dim)


def stencil(chosen_up, chosen_down):
    return jnp.where(chosen_up, 0.5, jnp.where(chosen_down, -0.5, 0.0))


def render_kernel(
    depth_count,
    tile_count,
    vort_hbm,
    color_hbm,
    extinction_hbm,
    out_ref,
    color_ref,
    extinction_ref,
    brick,
    slabs,
    row_out,
    row_in,
    row_next,
    edge_out,
    edge_in,
    edge_next,
    part_out,
    part_in,
    part_own,
    local_sem,
    table_sem,
    own_sem,
    send_sem,
    recv_sem,
    row_send_sem,
    row_recv_sem,
    row_next_send_sem,
    row_next_recv_sem,
    edge_send_sem,
    edge_recv_sem,
    edge_next_send_sem,
    edge_next_recv_sem,
    halo_send_sem,
    halo_recv_sem,
    part_send_sem,
    part_recv_sem,
    far_sem,
    side_sem,
):
    local_slices, pairs, _, _, slim, tile_cols = vort_hbm.shape
    rows = HALVES * slim
    tile_rows = depth_count * rows
    knots = extinction_hbm.shape[0]
    thickness = 1.0 / (local_slices * depth_count)
    group = local_slices * rows
    pair_slices = PAIR * local_slices
    depth = lax.axis_index("depth")
    tile = lax.axis_index("tile")
    pair = depth // PAIR
    member = depth % PAIR
    mate = 1 - member
    left = tile - 1
    right = tile + 1
    has_below = pair > 0
    has_above = pair < pairs - 1
    has_left = tile > 0
    has_right = tile < tile_count - 1
    towards = pair - 1 + 2 * member
    origin = pair + 1 - 2 * member
    gives = jnp.where(member == 0, pair, pairs - 1 - pair) > 0
    takes = jnp.where(member == 0, pairs - 1 - pair, pair) > 0

    whole = pltpu.make_async_copy(vort_hbm, brick, local_sem)
    whole.start()
    barrier = pltpu.get_barrier_semaphore()

    def greet(there, peers):
        @pl.when(there)
        def _():
            for peer in peers:
                pl.semaphore_signal(barrier, inc=1, device_id=peer, device_id_type=MESH)

    close = (tile % 2 == 1, tile % 2 == 0)
    for there, at_hand, beside in ((has_left, close[0], left), (has_right, close[1], right)):
        greet(there, [(pair * PAIR + member, beside)])
        greet(there & at_hand, [(pair * PAIR + mate, beside)])
        greet(there & at_hand & takes, [(origin * PAIR + member, beside)])
    greet(has_below, [((pair - 1) * PAIR + member, tile)])
    greet(has_above, [((pair + 1) * PAIR + member, tile)])
    pl.semaphore_signal(barrier, inc=1, device_id=(pair * PAIR + mate, tile), device_id_type=MESH)
    greeted = 1 + has_below.astype(jnp.int32) + has_above.astype(jnp.int32)
    for there, at_hand in ((has_left, close[0]), (has_right, close[1])):
        for known in (there, there & at_hand, there & at_hand & gives):
            greeted = greeted + known.astype(jnp.int32)

    def tell(there, place, sem):
        @pl.when(there)
        def _():
            pl.semaphore_signal(sem, inc=1, device_id=(place * PAIR + member, tile), device_id_type=MESH)

    def hear(there, sem):
        @pl.when(there)
        def _():
            pl.semaphore_wait(sem, 1)


    def remote(src, dst, sent, received, target):
        return pltpu.make_async_remote_copy(
            src_ref=src,
            dst_ref=dst,
            send_sem=sent,
            recv_sem=received,
            device_id=target,
            device_id_type=MESH,
        )

    def order(step, place=None):
        place = pair if place is None else place
        chunk = place
        for home in range(pairs):
            route = [0] * (home > 0)
            route += list(range(home - 1, 0, -1)) + list(range(pairs - 1, home, -1))
            for turn, reached in enumerate(route):
                chunk = jnp.where((place == home) & (step == turn), reached, chunk)
        return chunk

    sends = []

    def halo(chunk):
        return remote(
            vort_hbm.at[pl.ds((local_slices - 2) * member, 2), chunk, member],
            slabs.at[chunk, pl.ds(pair_slices, 2)],
            halo_send_sem.at[chunk],
            halo_recv_sem.at[chunk],
            (towards * PAIR + member, tile),
        )

    def row_halo(chunk):
        return remote(
            row_out.at[member, chunk],
            row_next.at[chunk],
            row_next_send_sem.at[chunk],
            row_next_recv_sem.at[chunk],
            (towards * PAIR + member, tile),
        )

    def push(step, between=None):

        @pl.when(gives)
        def _():
            row_halo(order(step, towards)).start()
            halo(order(step, towards)).start()

        chunk = order(step)
        copy = remote(
            row_out.at[mate, chunk],
            row_in.at[member, chunk],
            row_send_sem.at[step],
            row_recv_sem.at[chunk],
            (pair * PAIR + mate, tile),
        )
        copy.start()
        sends.append(copy)
        for half in range(HALVES):
            if half == 1 and between is not None:
                between()
            copy = remote(
                vort_hbm.at[:, chunk, mate, half],
                slot(chunk, member, half),
                send_sem.at[step, half],
                recv_sem.at[chunk, half],
                (pair * PAIR + mate, tile),
            )
            copy.start()
            sends.append(copy)

    loads = [
        pltpu.make_async_copy(color_hbm, color_ref, table_sem.at[0]),
        pltpu.make_async_copy(extinction_hbm, extinction_ref, table_sem.at[1]),
    ]
    for copy in loads:
        copy.start()

    def slot(chunk, which, half):
        return slabs.at[chunk, pl.ds(which * local_slices, local_slices), half]

    own = [
        pltpu.make_async_copy(
            vort_hbm.at[:, chunk, member, half], slot(chunk, member, half), own_sem.at[chunk, half]
        )
        for chunk in range(pairs)
        for half in range(HALVES)
    ]
    for copy in own:
        copy.start()

    whole.wait()
    packed = depth_count * HALVES * 2 * local_slices
    line = iota((packed, 1), 0)
    line_block = line // (2 * local_slices)
    line_slice = (line % (2 * local_slices)) // 2
    line_row = line_block * slim + jnp.where(line % 2 == 0, -1, slim)
    inside = (line_row >= 0) & (line_row < tile_rows)
    wanted = jnp.where(inside, line_slice * tile_rows + line_row, -1)
    pick = jnp.where(iota((packed, local_slices * tile_rows), 1) == wanted, 1.0, 0.0)
    flat = brick[...].reshape(local_slices * tile_rows, tile_cols)
    outside = jnp.dot(pick.astype(jnp.bfloat16), flat, preferred_element_type=jnp.float32)
    for block in range(depth_count):
        for half in range(HALVES):
            first = (block * HALVES + half) * 2 * local_slices
            row_out[block % PAIR, block // PAIR, half] = outside[first : first + 2 * local_slices].astype(
                jnp.bfloat16
            )
    column = iota((SUBLANES, tile_cols), 1)
    ends = iota((SUBLANES, tile_cols), 0)
    pick_ends = ((ends == 0) & (column == 0)) | ((ends == 1) & (column == tile_cols - 1))
    by_block = jnp.concatenate(
        [
            brick[z, block // PAIR, block % PAIR, half]
            for block in range(depth_count)
            for half in range(HALVES)
            for z in range(local_slices)
        ],
        axis=0,
    )
    columns = lax.dot_general(
        jnp.where(pick_ends, 1.0, 0.0).astype(jnp.bfloat16),
        by_block,
        (((1,), (1,)), ((), ())),
        preferred_element_type=jnp.float32,
    )
    for block in range(depth_count):
        for end in range(2):
            edge_out[end, block % PAIR, block // PAIR] = columns[end : end + 1, block * group : (block + 1) * group]

    @pl.when(jnp.logical_not(takes))
    def _():
        slabs[:, pair_slices:] = jnp.zeros((pairs, 2, HALVES, slim, tile_cols), jnp.bfloat16)
        row_next[...] = jnp.zeros(row_next.shape, jnp.bfloat16)

    row_in[member] = row_out[member]
    pl.semaphore_wait(barrier, greeted)
    tell(has_below & has_above, pair - 1, far_sem.at[0, 0])
    tell(has_below & has_above, pair + 1, far_sem.at[1, 0])
    sides = (has_left, has_right)
    distant = [there & jnp.logical_not(at_hand) for there, at_hand in zip(sides, close)]
    for end in range(2):

        @pl.when(distant[end])
        def _():
            pl.semaphore_signal(
                side_sem.at[1 - end],
                inc=1,
                device_id=(pair * PAIR + member, (left, right)[end]),
                device_id_type=MESH,
            )

    def edge(end, which):
        return remote(
            edge_out.at[end, which],
            edge_in.at[1 - end, member],
            edge_send_sem.at[end, which],
            edge_recv_sem.at[1 - end, member],
            (pair * PAIR + which, (left, right)[end]),
        )

    def edge_halo(end):
        return remote(
            edge_out.at[end, member],
            edge_next.at[1 - end],
            edge_next_send_sem.at[end],
            edge_next_recv_sem.at[1 - end],
            (towards * PAIR + member, (left, right)[end]),
        )

    for end in range(2):

        @pl.when(sides[end])
        def _():
            edge(end, member).start()

        @pl.when(sides[end] & close[end])
        def _():
            edge(end, mate).start()

        @pl.when(sides[end] & close[end] & gives)
        def _():
            edge_halo(end).start()

        @pl.when(jnp.logical_not(sides[end]))
        def _():
            edge_in[end] = jnp.zeros(edge_in.shape[1:], jnp.float32)

        @pl.when(jnp.logical_not(sides[end] & takes))
        def _():
            edge_next[end] = jnp.zeros(edge_next.shape[1:], jnp.float32)

    def far_edges():
        for end in range(2):
            hear(distant[end], side_sem.at[end])

            @pl.when(distant[end])
            def _():
                edge(end, mate).start()

            @pl.when(distant[end] & gives)
            def _():
                edge_halo(end).start()

    push(0, far_edges)
    for step in range(1, pairs):
        push(step)

    stack = (pair_slices + 1) * slim
    spread = (pair_slices + 2) * slim
    lined = 2 * (pair_slices + local_slices)
    extra = -(-lined // (2 * SUBLANES)) * 2 * SUBLANES
    cell = iota((stack, spread + extra), 0)
    source = iota((stack, spread + extra), 1)
    cell_row = cell % slim
    source_row = source % slim
    slot_of = cell // slim
    slice_of = jnp.where(source < spread, source // slim, -2)
    added = slot_of == pair_slices
    last = slot_of == pair_slices - 1
    home = jnp.where(added, pair_slices + member, slot_of)
    up = (slice_of == home) & (source_row == cell_row + 1)
    down = (slice_of == home) & (source_row == cell_row - 1)
    packed_line = spread + 2 * slot_of + jnp.where(added, 2 * (local_slices - 1) * member, 0)
    up = up | ((source == packed_line + 1) & (cell_row == slim - 1))
    down = down | ((source == packed_line) & (cell_row == 0))
    along_x = stencil(up, down).astype(jnp.bfloat16)
    behind = jnp.where(
        added,
        jnp.where(member == 0, pair_slices + 1, 0),
        jnp.where(last & (member == 1), -1, slot_of + 1),
    )
    ahead = jnp.where(
        added,
        jnp.where(member == 0, pair_slices - 1, pair_slices),
        jnp.where((slot_of == 0) & (member == 1), pair_slices + 1, slot_of - 1),
    )
    same_row = source_row == cell_row
    along_z = stencil((slice_of == behind) & same_row, (slice_of == ahead) & same_row).astype(jnp.bfloat16)
    along_both = jnp.concatenate([along_x, along_z], axis=0)
    keep_first = ((member == 1) | (pair == 0)).astype(jnp.float32)
    keep_last = ((member == 0) | (pair == pairs - 1)).astype(jnp.float32)
    keep_added = takes.astype(jnp.float32)
    to_col = iota((tile_cols, tile_cols), 1)
    from_col = iota((tile_cols, tile_cols), 0)
    along_y = stencil(from_col == to_col + 1, from_col == to_col - 1).astype(jnp.bfloat16)
    place = jnp.where(
        (ends == 0) & (column == 0),
        -0.5,
        jnp.where((ends == 1) & (column == tile_cols - 1), 0.5, 0.0),
    ).astype(jnp.bfloat16)

    for copy in loads:
        copy.wait()
    folds = slim // SUBLANES
    banks = -(-knots // SUBLANES)
    knot = iota((SUBLANES, LANES), 0)

    def wide(read, count):
        spread_out = []
        for bank in range(banks):
            value = jnp.zeros((SUBLANES, LANES), jnp.float32)
            for k in range(bank * SUBLANES, min(count, (bank + 1) * SUBLANES)):
                value = jnp.where(knot == k - bank * SUBLANES, read(k), value)
            spread_out.append(jnp.concatenate([value] * (folds * tile_cols // LANES), axis=1))
        return spread_out

    def table(read):
        return wide(read, knots), wide(lambda k: read(k + 1) - read(k), knots - 1)

    tables = [table(lambda k, c=c: color_ref[c, k]) for c in range(3)]
    tables.append(table(lambda k: -thickness * extinction_ref[k]))

    def fold(value):
        return jnp.concatenate(
            [value[first : first + SUBLANES] for first in range(0, slim, SUBLANES)], axis=1
        )

    def unfold(value):
        return jnp.concatenate(
            [value[:, first * tile_cols : (first + 1) * tile_cols] for first in range(folds)], axis=0
        )

    def pick_from(choices, index):
        found = None
        for bank, choice in enumerate(choices):
            got = jnp.take_along_axis(choice, index % SUBLANES, axis=0, mode="promise_in_bounds")
            found = got if found is None else jnp.where(index >= bank * SUBLANES, got, found)
        return found

    def lookup(which, index, part):
        value, slope = tables[which]
        return pick_from(value, index) + part * pick_from(slope, index)

    def wait_recv(dst, sem):
        remote(dst, dst, local_sem, sem, (depth, tile)).wait_recv()

    for copy in own:
        copy.wait()

    for end in range(2):

        @pl.when(sides[end])
        def _():
            for which in range(PAIR):
                wait_recv(edge_in.at[end, which], edge_recv_sem.at[end, which])

        @pl.when(sides[end] & takes)
        def _():
            wait_recv(edge_next.at[end], edge_next_recv_sem.at[end])

    hear(pair < pairs - 2, far_sem.at[0, 0])
    hear(pair >= 2, far_sem.at[1, 0])
    for reach in range(1, pairs - 2):
        tell(has_below & (pair < pairs - 1 - reach), pair - 1, far_sem.at[0, reach])
        tell(has_above & (pair > reach), pair + 1, far_sem.at[1, reach])
        hear(pair < pairs - 2 - reach, far_sem.at[0, reach])
        hear(pair >= 2 + reach, far_sem.at[1, reach])

    def over(near, far):
        clear = 1.0 - near[3]
        return tuple(n + clear * f for n, f in zip(near, far))

    def shade(chunk, half):
        filled = slabs[chunk, :, half].reshape(spread, tile_cols)
        cells = jnp.concatenate(
            [filled[: pair_slices * slim], slabs[chunk, pair_slices + member, half]], axis=0
        )
        lines = [row_in[which, chunk, half].astype(jnp.float32) for which in range(PAIR)]
        lines.append(row_next[chunk, half].astype(jnp.float32))
        lines.append(jnp.zeros((extra - lined, tile_cols), jnp.float32))
        around = jnp.concatenate([filled, jnp.concatenate(lines, axis=0).astype(jnp.bfloat16)], axis=0)
        grads = jnp.dot(along_both, around, preferred_element_type=jnp.float32)
        grads_x, grads_z = grads[:stack], grads[stack:]
        start = half * local_slices * slim
        stop = start + local_slices * slim
        first, second = (
            jnp.concatenate(
                [edge_in[end, which, chunk][:, start:stop] for which in range(PAIR)]
                + [
                    jnp.where(
                        member == 0,
                        edge_next[end, chunk][:, start : start + slim],
                        edge_next[end, chunk][:, stop - slim : stop],
                    )
                ],
                axis=1,
            )
            for end in range(2)
        )
        edge_row = iota((SUBLANES, stack), 0)
        edges = jnp.where(edge_row == 0, first, jnp.where(edge_row == 1, second, 0.0))
        grads_y = jnp.dot(cells, along_y, preferred_element_type=jnp.float32) + lax.dot_general(
            edges.astype(jnp.bfloat16),
            place,
            (((0,), (0,)), ((), ())),
            preferred_element_type=jnp.float32,
        )
        partial = None
        for z in range(pair_slices + 1):
            here = slice(z * slim, (z + 1) * slim)
            gx, gy, gz = fold(grads_x[here]), fold(grads_y[here]), fold(grads_z[here])
            scalar = fold(cells[here].astype(jnp.float32))
            facing = 0.48 * gx + 0.6 * gy + 0.64 * gz
            lighting = 0.55 + 0.45 * facing * lax.rsqrt(gx * gx + gy * gy + gz * gz + 0.25)
            position = jnp.clip((scalar + 4.0) * ((knots - 1) / 8.0), 0.0, knots - 1.0)
            index = position.astype(jnp.int32)
            part = position - index.astype(jnp.float32)
            opacity = 1.0 - jnp.exp(lookup(3, index, part))
            if z == 0:
                opacity = keep_first * opacity
            if z == pair_slices - 1:
                opacity = keep_last * opacity
            if z == pair_slices:
                opacity = keep_added * opacity
            lit = opacity * lighting
            sample = tuple(lit * lookup(c, index, part) for c in range(3)) + (opacity,)
            if z == pair_slices:
                near = tuple(jnp.where(member == 0, p, t) for p, t in zip(partial, sample))
                sample = tuple(jnp.where(member == 0, t, p) for p, t in zip(partial, sample))
                partial = near
            partial = sample if partial is None else over(partial, sample)
        return partial

    def send_part(step, half):
        chunk = order(step)
        return remote(
            part_out.at[chunk, half],
            part_in.at[pair, half],
            part_send_sem.at[chunk, half],
            part_recv_sem.at[pair, half],
            (chunk * PAIR + member, tile),
        )

    def march(step, carry):
        chunk = order(step)

        @pl.when(takes)
        def _():
            wait_recv(row_next.at[chunk], row_next_recv_sem.at[chunk])
            wait_recv(slabs.at[chunk, pl.ds(pair_slices, 2)], halo_recv_sem.at[chunk])

        wait_recv(row_in.at[mate, chunk], row_recv_sem.at[chunk])
        for half in range(HALVES):
            wait_recv(slot(chunk, mate, half), recv_sem.at[chunk, half])
            partial = shade(chunk, half)
            for channel in range(4):
                image = unfold(partial[channel])
                part_own[half, channel] = image
                part_out[chunk, half, channel] = image.astype(jnp.bfloat16)

            @pl.when(step < pairs - 1)
            def _():
                send_part(step, half).start()

        return carry

    lax.fori_loop(0, pairs, march, 0)
    part_in[pair] = part_out[pair]
    for copy in sends:
        copy.wait_send()
    for end in range(2):

        @pl.when(sides[end])
        def _():
            for which in range(PAIR):
                edge(end, which).wait_send()

        @pl.when(sides[end] & gives)
        def _():
            edge_halo(end).wait_send()

    for step in range(pairs - 1):
        for half in range(HALVES):
            send_part(step, half).wait_send()

    @pl.when(gives)
    def _():
        for chunk in range(pairs):
            halo(chunk).wait_send()
            row_halo(chunk).wait_send()

    for half in range(HALVES):
        for step in range(pairs - 1):
            wait_recv(part_in.at[order(step), half], part_recv_sem.at[order(step), half])
        total = None
        for source in range(pairs):
            layer = tuple(
                jnp.where(pair == source, part_own[half, c], part_in[source, half, c].astype(jnp.float32))
                for c in range(4)
            )
            total = layer if total is None else over(total, layer)
        for channel in range(4):
            out_ref[channel, half * slim : (half + 1) * slim] = total[channel]


def render(vorticity, tf_color, tf_extinction):
    depth_count = lax.axis_size("depth")
    tile_count = lax.axis_size("tile")
    local_slices, tile_rows, tile_cols = vorticity.shape
    rows = tile_rows // depth_count
    slim = rows // HALVES
    group = local_slices * rows
    pairs = depth_count // PAIR
    dma = pltpu.SemaphoreType.DMA
    return pl.pallas_call(
        functools.partial(render_kernel, depth_count, tile_count),
        out_shape=pltpu.VMEM((4, rows, tile_cols), jnp.float32),
        in_specs=[
            pl.BlockSpec(memory_space=pltpu.HBM),
            pl.BlockSpec(memory_space=pltpu.HBM),
            pl.BlockSpec(memory_space=pltpu.HBM),
        ],
        out_specs=pl.BlockSpec(memory_space=pltpu.VMEM),
        scratch_shapes=[
            pltpu.SMEM(tf_color.shape, jnp.float32),
            pltpu.SMEM(tf_extinction.shape, jnp.float32),
            pltpu.VMEM((local_slices, pairs, PAIR, HALVES, slim, tile_cols), jnp.bfloat16),
            pltpu.VMEM((pairs, PAIR * local_slices + 2, HALVES, slim, tile_cols), jnp.bfloat16),
            pltpu.VMEM((PAIR, pairs, HALVES, 2 * local_slices, tile_cols), jnp.bfloat16),
            pltpu.VMEM((PAIR, pairs, HALVES, 2 * local_slices, tile_cols), jnp.bfloat16),
            pltpu.VMEM((pairs, HALVES, 2 * local_slices, tile_cols), jnp.bfloat16),
            pltpu.VMEM((2, PAIR, pairs, 1, group), jnp.float32),
            pltpu.VMEM((2, PAIR, pairs, 1, group), jnp.float32),
            pltpu.VMEM((2, pairs, 1, group), jnp.float32),
            pltpu.VMEM((pairs, HALVES, 4, slim, tile_cols), jnp.bfloat16),
            pltpu.VMEM((pairs, HALVES, 4, slim, tile_cols), jnp.bfloat16),
            pltpu.VMEM((HALVES, 4, slim, tile_cols), jnp.float32),
            dma,
            dma((2,)),
            dma((pairs, HALVES)),
            dma((pairs, HALVES)),
            dma((pairs, HALVES)),
            dma((pairs,)),
            dma((pairs,)),
            dma((pairs,)),
            dma((pairs,)),
            dma((2, PAIR)),
            dma((2, PAIR)),
            dma((2,)),
            dma((2,)),
            dma((pairs,)),
            dma((pairs,)),
            dma((pairs, HALVES)),
            dma((pairs, HALVES)),
            pltpu.SemaphoreType.REGULAR((2, max(pairs - 2, 1))),
            pltpu.SemaphoreType.REGULAR((2,)),
        ],
        compiler_params=pltpu.CompilerParams(collective_id=0, has_side_effects=True, vmem_limit_bytes=VMEM_BYTES),
        name="render",
    )(*(pltpu.with_memory_space_constraint(given, pltpu.HBM) for given in (vorticity.reshape(local_slices, pairs, PAIR, HALVES, slim, tile_cols), tf_color, tf_extinction)))


def fits(vorticity, knots):
    local_slices, tile_rows, tile_cols = vorticity.shape
    depth_count = lax.axis_size("depth")
    rows = tile_rows // depth_count
    return (
        tile_rows % depth_count == 0
        and rows % (HALVES * 2 * SUBLANES) == 0
        and tile_cols % LANES == 0
        and (local_slices * rows) % LANES == 0
        and 2 * local_slices == SUBLANES
        and knots <= LANES
        and depth_count % PAIR == 0
        and depth_count & (depth_count - 1) == 0
        and depth_count <= 16
        and lax.axis_size("tile") > 1
    )


def choose(vorticity, tf_color, tf_extinction):
    if fits(vorticity, tf_extinction.shape[0]):
        return render(vorticity, tf_color, tf_extinction)
    return local(vorticity, tf_color, tf_extinction)


def solution(mesh):
    placed = (P("depth", None, "tile"), P(), P())
    return jax.shard_map(
        choose, mesh=mesh, in_specs=placed, out_specs=P(None, "depth", "tile"), check_vma=False
    )
```

```python
import functools

import jax
import jax.numpy as jnp
from jax import lax
from jax.experimental import pallas as pl
from jax.experimental.pallas import tpu as pltpu
from jax.sharding import PartitionSpec as P


def extended(cells, sides, width):
    for axis, dim in sides:
        count = lax.axis_size(axis)
        ends = count - 1
        head = lax.slice_in_dim(cells, 0, width, axis=dim)
        tail = lax.slice_in_dim(cells, cells.shape[dim] - width, cells.shape[dim], axis=dim)
        cells = jnp.concatenate(
            [
                lax.ppermute(tail, axis, [(i, (i + 1) % count) for i in range(ends)]),
                cells,
                lax.ppermute(head, axis, [((i + 1) % count, i) for i in range(ends)]),
            ],
            axis=dim,
        )
    return cells


def shade_sample(slab_below, slab_here, slab_above, tf_color, tf_extinction, thickness):
    middle = slab_here.astype(jnp.float32)
    grad_z = 0.5 * (
        slab_above[1:-1, 1:-1].astype(jnp.float32) - slab_below[1:-1, 1:-1].astype(jnp.float32)
    )
    grad_x = 0.5 * (middle[2:, 1:-1] - middle[:-2, 1:-1])
    grad_y = 0.5 * (middle[1:-1, 2:] - middle[1:-1, :-2])
    scalar = middle[1:-1, 1:-1]
    facing = 0.48 * grad_x + 0.6 * grad_y + 0.64 * grad_z
    lighting = 0.55 + 0.45 * facing / jnp.sqrt(
        grad_x * grad_x + grad_y * grad_y + grad_z * grad_z + 0.25
    )
    count_knots = tf_extinction.shape[0]
    position = jnp.clip((scalar + 4.0) * ((count_knots - 1) / 8.0), 0.0, count_knots - 1.0)
    knot_points = jnp.arange(count_knots, dtype=jnp.float32)
    weights = jnp.maximum(0.0, 1.0 - jnp.abs(position[None] - knot_points[:, None, None]))
    colour_mix = jnp.einsum("ck,kxy->cxy", tf_color, weights, precision=lax.Precision.HIGHEST)
    extinction = jnp.einsum("k,kxy->xy", tf_extinction, weights, precision=lax.Precision.HIGHEST)
    opacity = 1.0 - jnp.exp(-extinction * thickness)
    return jnp.concatenate([opacity[None] * lighting[None] * colour_mix, opacity[None]], axis=0)


def composite(nearer, farther):
    return nearer + (1.0 - nearer[3:4]) * farther


def local(vorticity, tf_color, tf_extinction):
    depth_count = lax.axis_size("depth")
    local_slices = vorticity.shape[0]
    tile_rows = vorticity.shape[1]
    tile_cols = vorticity.shape[2]
    thickness = 1.0 / (local_slices * depth_count)
    padded = extended(vorticity, (("depth", 0), ("tile", 2)), 1)
    widened = jnp.pad(padded, ((0, 0), (1, 1), (0, 0)))

    def march(slice_index, accumulated):
        slab_below = lax.dynamic_index_in_dim(widened, slice_index, 0, keepdims=False)
        slab_here = lax.dynamic_index_in_dim(widened, slice_index + 1, 0, keepdims=False)
        slab_above = lax.dynamic_index_in_dim(widened, slice_index + 2, 0, keepdims=False)
        sample = shade_sample(slab_below, slab_here, slab_above, tf_color, tf_extinction, thickness)
        return composite(accumulated, sample)

    blank_image = jnp.zeros((4, tile_rows, tile_cols), jnp.float32)
    partial_value = lax.fori_loop(0, local_slices, march, blank_image)
    block_rows = tile_rows // depth_count
    rounds = depth_count.bit_length() - 1
    stacked = partial_value.reshape(4, 1, tile_rows, tile_cols)
    pieces = lax.all_to_all(
        stacked.astype(jnp.bfloat16), "depth", split_axis=2, concat_axis=1, tiled=True
    ).astype(stacked.dtype)
    for halving in range(rounds):
        paired = pieces.reshape(4, pieces.shape[1] // 2, 2, block_rows, tile_cols)
        pieces = composite(paired[:, :, 0], paired[:, :, 1])
    final_image = pieces[:, 0]
    return final_image


MESH = pl.DeviceIdType.MESH
LANES = 128
PAIR = 2
HALVES = 2
SUBLANES = 8
VMEM_BYTES = 24 * 2**20


def iota(shape, dim):
    return lax.broadcasted_iota(jnp.int32, shape, dim)


def stencil(chosen_up, chosen_down):
    return jnp.where(chosen_up, 0.5, jnp.where(chosen_down, -0.5, 0.0))


def render_kernel(
    depth_count,
    tile_count,
    vort_hbm,
    color_hbm,
    extinction_hbm,
    out_ref,
    color_ref,
    extinction_ref,
    brick,
    slabs,
    row_out,
    row_in,
    row_next,
    edge_out,
    edge_in,
    edge_next,
    part_out,
    part_in,
    part_own,
    local_sem,
    table_sem,
    own_sem,
    send_sem,
    recv_sem,
    row_send_sem,
    row_recv_sem,
    row_next_send_sem,
    row_next_recv_sem,
    edge_send_sem,
    edge_recv_sem,
    edge_next_send_sem,
    edge_next_recv_sem,
    halo_send_sem,
    halo_recv_sem,
    part_send_sem,
    part_recv_sem,
    far_sem,
    side_sem,
):
    local_slices, pairs, _, _, slim, tile_cols = vort_hbm.shape
    rows = HALVES * slim
    tile_rows = depth_count * rows
    knots = extinction_hbm.shape[0]
    thickness = 1.0 / (local_slices * depth_count)
    group = local_slices * rows
    pair_slices = PAIR * local_slices
    depth = lax.axis_index("depth")
    tile = lax.axis_index("tile")
    pair = depth // PAIR
    member = depth % PAIR
    mate = 1 - member
    left = tile - 1
    right = tile + 1
    has_below = pair > 0
    has_above = pair < pairs - 1
    has_left = tile > 0
    has_right = tile < tile_count - 1
    towards = pair - 1 + 2 * member
    origin = pair + 1 - 2 * member
    gives = jnp.where(member == 0, pair, pairs - 1 - pair) > 0
    takes = jnp.where(member == 0, pairs - 1 - pair, pair) > 0

    whole = pltpu.make_async_copy(vort_hbm, brick, local_sem)
    whole.start()
    barrier = pltpu.get_barrier_semaphore()

    def greet(there, peers):
        @pl.when(there)
        def _():
            for peer in peers:
                pl.semaphore_signal(barrier, inc=1, device_id=peer, device_id_type=MESH)

    close = (tile % 2 == 1, tile % 2 == 0)
    for there, at_hand, beside in ((has_left, close[0], left), (has_right, close[1], right)):
        greet(there, [(pair * PAIR + member, beside)])
        greet(there & at_hand, [(pair * PAIR + mate, beside)])
        greet(there & at_hand & takes, [(origin * PAIR + member, beside)])
    greet(has_below, [((pair - 1) * PAIR + member, tile)])
    greet(has_above, [((pair + 1) * PAIR + member, tile)])
    pl.semaphore_signal(barrier, inc=1, device_id=(pair * PAIR + mate, tile), device_id_type=MESH)
    greeted = 1 + has_below.astype(jnp.int32) + has_above.astype(jnp.int32)
    for there, at_hand in ((has_left, close[0]), (has_right, close[1])):
        for known in (there, there & at_hand, there & at_hand & gives):
            greeted = greeted + known.astype(jnp.int32)

    def tell(there, place, sem):
        @pl.when(there)
        def _():
            pl.semaphore_signal(sem, inc=1, device_id=(place * PAIR + member, tile), device_id_type=MESH)

    def hear(there, sem):
        @pl.when(there)
        def _():
            pl.semaphore_wait(sem, 1)


    def remote(src, dst, sent, received, target):
        return pltpu.make_async_remote_copy(
            src_ref=src,
            dst_ref=dst,
            send_sem=sent,
            recv_sem=received,
            device_id=target,
            device_id_type=MESH,
        )

    def order(step, place=None):
        place = pair if place is None else place
        chunk = place
        for home in range(pairs):
            route = [0] * (home > 0)
            route += list(range(home - 1, 0, -1)) + list(range(pairs - 1, home, -1))
            for turn, reached in enumerate(route):
                chunk = jnp.where((place == home) & (step == turn), reached, chunk)
        return chunk

    sends = []

    def halo(chunk):
        return remote(
            brick.at[pl.ds((local_slices - 2) * member, 2), chunk, member],
            slabs.at[chunk, pl.ds(pair_slices, 2)],
            halo_send_sem.at[chunk],
            halo_recv_sem.at[chunk],
            (towards * PAIR + member, tile),
        )

    def row_halo(chunk):
        return remote(
            row_out.at[member, chunk],
            row_next.at[chunk],
            row_next_send_sem.at[chunk],
            row_next_recv_sem.at[chunk],
            (towards * PAIR + member, tile),
        )

    def push(step, between=None):

        @pl.when(gives)
        def _():
            row_halo(order(step, towards)).start()
            halo(order(step, towards)).start()

        chunk = order(step)
        copy = remote(
            row_out.at[mate, chunk],
            row_in.at[member, chunk],
            row_send_sem.at[step],
            row_recv_sem.at[chunk],
            (pair * PAIR + mate, tile),
        )
        copy.start()
        sends.append(copy)
        for half in range(HALVES):
            if half == 1 and between is not None:
                between()
            copy = remote(
                brick.at[:, chunk, mate, half],
                slot(chunk, member, half),
                send_sem.at[step, half],
                recv_sem.at[chunk, half],
                (pair * PAIR + mate, tile),
            )
            copy.start()
            sends.append(copy)

    loads = [
        pltpu.make_async_copy(color_hbm, color_ref, table_sem.at[0]),
        pltpu.make_async_copy(extinction_hbm, extinction_ref, table_sem.at[1]),
    ]
    for copy in loads:
        copy.start()

    def slot(chunk, which, half):
        return slabs.at[chunk, pl.ds(which * local_slices, local_slices), half]

    own = [
        pltpu.make_async_copy(
            vort_hbm.at[:, chunk, member, half], slot(chunk, member, half), own_sem.at[chunk, half]
        )
        for chunk in range(pairs)
        for half in range(HALVES)
    ]
    for copy in own:
        copy.start()

    whole.wait()
    packed = depth_count * HALVES * 2 * local_slices
    line = iota((packed, 1), 0)
    line_block = line // (2 * local_slices)
    line_slice = (line % (2 * local_slices)) // 2
    line_row = line_block * slim + jnp.where(line % 2 == 0, -1, slim)
    inside = (line_row >= 0) & (line_row < tile_rows)
    wanted = jnp.where(inside, line_slice * tile_rows + line_row, -1)
    pick = jnp.where(iota((packed, local_slices * tile_rows), 1) == wanted, 1.0, 0.0)
    flat = brick[...].reshape(local_slices * tile_rows, tile_cols)
    outside = jnp.dot(pick.astype(jnp.bfloat16), flat, preferred_element_type=jnp.float32)
    for block in range(depth_count):
        for half in range(HALVES):
            first = (block * HALVES + half) * 2 * local_slices
            row_out[block % PAIR, block // PAIR, half] = outside[first : first + 2 * local_slices].astype(
                jnp.bfloat16
            )
    column = iota((SUBLANES, tile_cols), 1)
    ends = iota((SUBLANES, tile_cols), 0)
    pick_ends = ((ends == 0) & (column == 0)) | ((ends == 1) & (column == tile_cols - 1))
    by_block = jnp.concatenate(
        [
            brick[z, block // PAIR, block % PAIR, half]
            for block in range(depth_count)
            for half in range(HALVES)
            for z in range(local_slices)
        ],
        axis=0,
    )
    columns = lax.dot_general(
        jnp.where(pick_ends, 1.0, 0.0).astype(jnp.bfloat16),
        by_block,
        (((1,), (1,)), ((), ())),
        preferred_element_type=jnp.float32,
    )
    for block in range(depth_count):
        for end in range(2):
            edge_out[end, block % PAIR, block // PAIR] = columns[end : end + 1, block * group : (block + 1) * group]

    @pl.when(jnp.logical_not(takes))
    def _():
        slabs[:, pair_slices:] = jnp.zeros((pairs, 2, HALVES, slim, tile_cols), jnp.bfloat16)
        row_next[...] = jnp.zeros(row_next.shape, jnp.bfloat16)

    row_in[member] = row_out[member]
    pl.semaphore_wait(barrier, greeted)
    tell(has_below & has_above, pair - 1, far_sem.at[0, 0])
    tell(has_below & has_above, pair + 1, far_sem.at[1, 0])
    sides = (has_left, has_right)
    distant = [there & jnp.logical_not(at_hand) for there, at_hand in zip(sides, close)]
    for end in range(2):

        @pl.when(distant[end])
        def _():
            pl.semaphore_signal(
                side_sem.at[1 - end],
                inc=1,
                device_id=(pair * PAIR + member, (left, right)[end]),
                device_id_type=MESH,
            )

    def edge(end, which):
        return remote(
            edge_out.at[end, which],
            edge_in.at[1 - end, member],
            edge_send_sem.at[end, which],
            edge_recv_sem.at[1 - end, member],
            (pair * PAIR + which, (left, right)[end]),
        )

    def edge_halo(end):
        return remote(
            edge_out.at[end, member],
            edge_next.at[1 - end],
            edge_next_send_sem.at[end],
            edge_next_recv_sem.at[1 - end],
            (towards * PAIR + member, (left, right)[end]),
        )

    for end in range(2):

        @pl.when(jnp.logical_not(sides[end]))
        def _():
            edge_in[end] = jnp.zeros(edge_in.shape[1:], jnp.float32)

        @pl.when(jnp.logical_not(sides[end] & takes))
        def _():
            edge_next[end] = jnp.zeros(edge_next.shape[1:], jnp.float32)

    def far_edges():
        for end in range(2):

            @pl.when(sides[end])
            def _():
                edge(end, member).start()

            @pl.when(sides[end] & close[end])
            def _():
                edge(end, mate).start()

            @pl.when(sides[end] & close[end] & gives)
            def _():
                edge_halo(end).start()

        for end in range(2):
            hear(distant[end], side_sem.at[end])

            @pl.when(distant[end])
            def _():
                edge(end, mate).start()

            @pl.when(distant[end] & gives)
            def _():
                edge_halo(end).start()

    push(0, far_edges)
    for step in range(1, pairs):
        push(step)

    stack = (pair_slices + 1) * slim
    spread = (pair_slices + 2) * slim
    lined = 2 * (pair_slices + local_slices)
    extra = -(-lined // (2 * SUBLANES)) * 2 * SUBLANES
    cell = iota((stack, spread + extra), 0)
    source = iota((stack, spread + extra), 1)
    cell_row = cell % slim
    source_row = source % slim
    slot_of = cell // slim
    slice_of = jnp.where(source < spread, source // slim, -2)
    added = slot_of == pair_slices
    last = slot_of == pair_slices - 1
    home = jnp.where(added, pair_slices + member, slot_of)
    up = (slice_of == home) & (source_row == cell_row + 1)
    down = (slice_of == home) & (source_row == cell_row - 1)
    packed_line = spread + 2 * slot_of + jnp.where(added, 2 * (local_slices - 1) * member, 0)
    up = up | ((source == packed_line + 1) & (cell_row == slim - 1))
    down = down | ((source == packed_line) & (cell_row == 0))
    along_x = stencil(up, down).astype(jnp.bfloat16)
    behind = jnp.where(
        added,
        jnp.where(member == 0, pair_slices + 1, 0),
        jnp.where(last & (member == 1), -1, slot_of + 1),
    )
    ahead = jnp.where(
        added,
        jnp.where(member == 0, pair_slices - 1, pair_slices),
        jnp.where((slot_of == 0) & (member == 1), pair_slices + 1, slot_of - 1),
    )
    same_row = source_row == cell_row
    along_z = stencil((slice_of == behind) & same_row, (slice_of == ahead) & same_row).astype(jnp.bfloat16)
    along_both = jnp.concatenate([along_x, along_z], axis=0)
    keep_first = ((member == 1) | (pair == 0)).astype(jnp.float32)
    keep_last = ((member == 0) | (pair == pairs - 1)).astype(jnp.float32)
    keep_added = takes.astype(jnp.float32)
    to_col = iota((tile_cols, tile_cols), 1)
    from_col = iota((tile_cols, tile_cols), 0)
    along_y = stencil(from_col == to_col + 1, from_col == to_col - 1).astype(jnp.bfloat16)
    place = jnp.where(
        (ends == 0) & (column == 0),
        -0.5,
        jnp.where((ends == 1) & (column == tile_cols - 1), 0.5, 0.0),
    ).astype(jnp.bfloat16)

    for copy in loads:
        copy.wait()
    folds = slim // SUBLANES
    banks = -(-knots // SUBLANES)
    knot = iota((SUBLANES, LANES), 0)

    def wide(read, count):
        spread_out = []
        for bank in range(banks):
            value = jnp.zeros((SUBLANES, LANES), jnp.float32)
            for k in range(bank * SUBLANES, min(count, (bank + 1) * SUBLANES)):
                value = jnp.where(knot == k - bank * SUBLANES, read(k), value)
            spread_out.append(jnp.concatenate([value] * (folds * tile_cols // LANES), axis=1))
        return spread_out

    def table(read):
        return wide(read, knots), wide(lambda k: read(k + 1) - read(k), knots - 1)

    tables = [table(lambda k, c=c: color_ref[c, k]) for c in range(3)]
    tables.append(table(lambda k: -thickness * extinction_ref[k]))

    def fold(value):
        return jnp.concatenate(
            [value[first : first + SUBLANES] for first in range(0, slim, SUBLANES)], axis=1
        )

    def unfold(value):
        return jnp.concatenate(
            [value[:, first * tile_cols : (first + 1) * tile_cols] for first in range(folds)], axis=0
        )

    def pick_from(choices, index):
        found = None
        for bank, choice in enumerate(choices):
            got = jnp.take_along_axis(choice, index % SUBLANES, axis=0, mode="promise_in_bounds")
            found = got if found is None else jnp.where(index >= bank * SUBLANES, got, found)
        return found

    def lookup(which, index, part):
        value, slope = tables[which]
        return pick_from(value, index) + part * pick_from(slope, index)

    def wait_recv(dst, sem):
        remote(dst, dst, local_sem, sem, (depth, tile)).wait_recv()

    for copy in own:
        copy.wait()

    for end in range(2):

        @pl.when(sides[end])
        def _():
            for which in range(PAIR):
                wait_recv(edge_in.at[end, which], edge_recv_sem.at[end, which])

        @pl.when(sides[end] & takes)
        def _():
            wait_recv(edge_next.at[end], edge_next_recv_sem.at[end])

    hear(pair < pairs - 2, far_sem.at[0, 0])
    hear(pair >= 2, far_sem.at[1, 0])
    for reach in range(1, pairs - 2):
        tell(has_below & (pair < pairs - 1 - reach), pair - 1, far_sem.at[0, reach])
        tell(has_above & (pair > reach), pair + 1, far_sem.at[1, reach])
        hear(pair < pairs - 2 - reach, far_sem.at[0, reach])
        hear(pair >= 2 + reach, far_sem.at[1, reach])

    def over(near, far):
        clear = 1.0 - near[3]
        return tuple(n + clear * f for n, f in zip(near, far))

    def shade(chunk, half):
        filled = slabs[chunk, :, half].reshape(spread, tile_cols)
        cells = jnp.concatenate(
            [filled[: pair_slices * slim], slabs[chunk, pair_slices + member, half]], axis=0
        )
        lines = [row_in[which, chunk, half].astype(jnp.float32) for which in range(PAIR)]
        lines.append(row_next[chunk, half].astype(jnp.float32))
        lines.append(jnp.zeros((extra - lined, tile_cols), jnp.float32))
        around = jnp.concatenate([filled, jnp.concatenate(lines, axis=0).astype(jnp.bfloat16)], axis=0)
        grads = jnp.dot(along_both, around, preferred_element_type=jnp.float32)
        grads_x, grads_z = grads[:stack], grads[stack:]
        start = half * local_slices * slim
        stop = start + local_slices * slim
        first, second = (
            jnp.concatenate(
                [edge_in[end, which, chunk][:, start:stop] for which in range(PAIR)]
                + [
                    jnp.where(
                        member == 0,
                        edge_next[end, chunk][:, start : start + slim],
                        edge_next[end, chunk][:, stop - slim : stop],
                    )
                ],
                axis=1,
            )
            for end in range(2)
        )
        edge_row = iota((SUBLANES, stack), 0)
        edges = jnp.where(edge_row == 0, first, jnp.where(edge_row == 1, second, 0.0))
        grads_y = jnp.dot(cells, along_y, preferred_element_type=jnp.float32) + lax.dot_general(
            edges.astype(jnp.bfloat16),
            place,
            (((0,), (0,)), ((), ())),
            preferred_element_type=jnp.float32,
        )
        partial = None
        for z in range(pair_slices + 1):
            here = slice(z * slim, (z + 1) * slim)
            gx, gy, gz = fold(grads_x[here]), fold(grads_y[here]), fold(grads_z[here])
            scalar = fold(cells[here].astype(jnp.float32))
            facing = 0.48 * gx + 0.6 * gy + 0.64 * gz
            lighting = 0.55 + 0.45 * facing * lax.rsqrt(gx * gx + gy * gy + gz * gz + 0.25)
            position = jnp.clip((scalar + 4.0) * ((knots - 1) / 8.0), 0.0, knots - 1.0)
            index = position.astype(jnp.int32)
            part = position - index.astype(jnp.float32)
            opacity = 1.0 - jnp.exp(lookup(3, index, part))
            if z == 0:
                opacity = keep_first * opacity
            if z == pair_slices - 1:
                opacity = keep_last * opacity
            if z == pair_slices:
                opacity = keep_added * opacity
            lit = opacity * lighting
            sample = tuple(lit * lookup(c, index, part) for c in range(3)) + (opacity,)
            if z == pair_slices:
                near = tuple(jnp.where(member == 0, p, t) for p, t in zip(partial, sample))
                sample = tuple(jnp.where(member == 0, t, p) for p, t in zip(partial, sample))
                partial = near
            partial = sample if partial is None else over(partial, sample)
        return partial

    def send_part(step, half):
        chunk = order(step)
        return remote(
            part_out.at[chunk, half],
            part_in.at[pair, half],
            part_send_sem.at[chunk, half],
            part_recv_sem.at[pair, half],
            (chunk * PAIR + member, tile),
        )

    def march(step, carry):
        chunk = order(step)

        @pl.when(takes)
        def _():
            wait_recv(row_next.at[chunk], row_next_recv_sem.at[chunk])
            wait_recv(slabs.at[chunk, pl.ds(pair_slices, 2)], halo_recv_sem.at[chunk])

        wait_recv(row_in.at[mate, chunk], row_recv_sem.at[chunk])
        for half in range(HALVES):
            wait_recv(slot(chunk, mate, half), recv_sem.at[chunk, half])
            partial = shade(chunk, half)
            for channel in range(4):
                image = unfold(partial[channel])
                part_own[half, channel] = image
                part_out[chunk, half, channel] = image.astype(jnp.bfloat16)

            @pl.when(step < pairs - 1)
            def _():
                send_part(step, half).start()

        return carry

    lax.fori_loop(0, pairs, march, 0)
    part_in[pair] = part_out[pair]
    for copy in sends:
        copy.wait_send()
    for end in range(2):

        @pl.when(sides[end])
        def _():
            for which in range(PAIR):
                edge(end, which).wait_send()

        @pl.when(sides[end] & gives)
        def _():
            edge_halo(end).wait_send()

    for step in range(pairs - 1):
        for half in range(HALVES):
            send_part(step, half).wait_send()

    @pl.when(gives)
    def _():
        for chunk in range(pairs):
            halo(chunk).wait_send()
            row_halo(chunk).wait_send()

    for half in range(HALVES):
        for step in range(pairs - 1):
            wait_recv(part_in.at[order(step), half], part_recv_sem.at[order(step), half])
        total = None
        for source in range(pairs):
            layer = tuple(
                jnp.where(pair == source, part_own[half, c], part_in[source, half, c].astype(jnp.float32))
                for c in range(4)
            )
            total = layer if total is None else over(total, layer)
        for channel in range(4):
            out_ref[channel, half * slim : (half + 1) * slim] = total[channel]


def render(vorticity, tf_color, tf_extinction):
    depth_count = lax.axis_size("depth")
    tile_count = lax.axis_size("tile")
    local_slices, tile_rows, tile_cols = vorticity.shape
    rows = tile_rows // depth_count
    slim = rows // HALVES
    group = local_slices * rows
    pairs = depth_count // PAIR
    dma = pltpu.SemaphoreType.DMA
    return pl.pallas_call(
        functools.partial(render_kernel, depth_count, tile_count),
        out_shape=pltpu.VMEM((4, rows, tile_cols), jnp.float32),
        in_specs=[
            pl.BlockSpec(memory_space=pltpu.HBM),
            pl.BlockSpec(memory_space=pltpu.HBM),
            pl.BlockSpec(memory_space=pltpu.HBM),
        ],
        out_specs=pl.BlockSpec(memory_space=pltpu.VMEM),
        scratch_shapes=[
            pltpu.SMEM(tf_color.shape, jnp.float32),
            pltpu.SMEM(tf_extinction.shape, jnp.float32),
            pltpu.VMEM((local_slices, pairs, PAIR, HALVES, slim, tile_cols), jnp.bfloat16),
            pltpu.VMEM((pairs, PAIR * local_slices + 2, HALVES, slim, tile_cols), jnp.bfloat16),
            pltpu.VMEM((PAIR, pairs, HALVES, 2 * local_slices, tile_cols), jnp.bfloat16),
            pltpu.VMEM((PAIR, pairs, HALVES, 2 * local_slices, tile_cols), jnp.bfloat16),
            pltpu.VMEM((pairs, HALVES, 2 * local_slices, tile_cols), jnp.bfloat16),
            pltpu.VMEM((2, PAIR, pairs, 1, group), jnp.float32),
            pltpu.VMEM((2, PAIR, pairs, 1, group), jnp.float32),
            pltpu.VMEM((2, pairs, 1, group), jnp.float32),
            pltpu.VMEM((pairs, HALVES, 4, slim, tile_cols), jnp.bfloat16),
            pltpu.VMEM((pairs, HALVES, 4, slim, tile_cols), jnp.bfloat16),
            pltpu.VMEM((HALVES, 4, slim, tile_cols), jnp.float32),
            dma,
            dma((2,)),
            dma((pairs, HALVES)),
            dma((pairs, HALVES)),
            dma((pairs, HALVES)),
            dma((pairs,)),
            dma((pairs,)),
            dma((pairs,)),
            dma((pairs,)),
            dma((2, PAIR)),
            dma((2, PAIR)),
            dma((2,)),
            dma((2,)),
            dma((pairs,)),
            dma((pairs,)),
            dma((pairs, HALVES)),
            dma((pairs, HALVES)),
            pltpu.SemaphoreType.REGULAR((2, max(pairs - 2, 1))),
            pltpu.SemaphoreType.REGULAR((2,)),
        ],
        compiler_params=pltpu.CompilerParams(collective_id=0, has_side_effects=True, vmem_limit_bytes=VMEM_BYTES),
        name="render",
    )(*(pltpu.with_memory_space_constraint(given, pltpu.HBM) for given in (vorticity.reshape(local_slices, pairs, PAIR, HALVES, slim, tile_cols), tf_color, tf_extinction)))


def fits(vorticity, knots):
    local_slices, tile_rows, tile_cols = vorticity.shape
    depth_count = lax.axis_size("depth")
    rows = tile_rows // depth_count
    return (
        tile_rows % depth_count == 0
        and rows % (HALVES * 2 * SUBLANES) == 0
        and tile_cols % LANES == 0
        and (local_slices * rows) % LANES == 0
        and 2 * local_slices == SUBLANES
        and knots <= LANES
        and depth_count % PAIR == 0
        and depth_count & (depth_count - 1) == 0
        and depth_count <= 16
        and lax.axis_size("tile") > 1
    )


def choose(vorticity, tf_color, tf_extinction):
    if fits(vorticity, tf_extinction.shape[0]):
        return render(vorticity, tf_color, tf_extinction)
    return local(vorticity, tf_color, tf_extinction)


def solution(mesh):
    placed = (P("depth", None, "tile"), P(), P())
    return jax.shard_map(
        choose, mesh=mesh, in_specs=placed, out_specs=P(None, "depth", "tile"), check_vma=False
    )
```

```python
import functools

import jax
import jax.numpy as jnp
from jax import lax
from jax.experimental import pallas as pl
from jax.experimental.pallas import tpu as pltpu
from jax.sharding import PartitionSpec as P


def extended(cells, sides, width):
    for axis, dim in sides:
        count = lax.axis_size(axis)
        ends = count - 1
        head = lax.slice_in_dim(cells, 0, width, axis=dim)
        tail = lax.slice_in_dim(cells, cells.shape[dim] - width, cells.shape[dim], axis=dim)
        cells = jnp.concatenate(
            [
                lax.ppermute(tail, axis, [(i, (i + 1) % count) for i in range(ends)]),
                cells,
                lax.ppermute(head, axis, [((i + 1) % count, i) for i in range(ends)]),
            ],
            axis=dim,
        )
    return cells


def shade_sample(slab_below, slab_here, slab_above, tf_color, tf_extinction, thickness):
    middle = slab_here.astype(jnp.float32)
    grad_z = 0.5 * (
        slab_above[1:-1, 1:-1].astype(jnp.float32) - slab_below[1:-1, 1:-1].astype(jnp.float32)
    )
    grad_x = 0.5 * (middle[2:, 1:-1] - middle[:-2, 1:-1])
    grad_y = 0.5 * (middle[1:-1, 2:] - middle[1:-1, :-2])
    scalar = middle[1:-1, 1:-1]
    facing = 0.48 * grad_x + 0.6 * grad_y + 0.64 * grad_z
    lighting = 0.55 + 0.45 * facing / jnp.sqrt(
        grad_x * grad_x + grad_y * grad_y + grad_z * grad_z + 0.25
    )
    count_knots = tf_extinction.shape[0]
    position = jnp.clip((scalar + 4.0) * ((count_knots - 1) / 8.0), 0.0, count_knots - 1.0)
    knot_points = jnp.arange(count_knots, dtype=jnp.float32)
    weights = jnp.maximum(0.0, 1.0 - jnp.abs(position[None] - knot_points[:, None, None]))
    colour_mix = jnp.einsum("ck,kxy->cxy", tf_color, weights, precision=lax.Precision.HIGHEST)
    extinction = jnp.einsum("k,kxy->xy", tf_extinction, weights, precision=lax.Precision.HIGHEST)
    opacity = 1.0 - jnp.exp(-extinction * thickness)
    return jnp.concatenate([opacity[None] * lighting[None] * colour_mix, opacity[None]], axis=0)


def composite(nearer, farther):
    return nearer + (1.0 - nearer[3:4]) * farther


def local(vorticity, tf_color, tf_extinction):
    depth_count = lax.axis_size("depth")
    local_slices = vorticity.shape[0]
    tile_rows = vorticity.shape[1]
    tile_cols = vorticity.shape[2]
    thickness = 1.0 / (local_slices * depth_count)
    padded = extended(vorticity, (("depth", 0), ("tile", 2)), 1)
    widened = jnp.pad(padded, ((0, 0), (1, 1), (0, 0)))

    def march(slice_index, accumulated):
        slab_below = lax.dynamic_index_in_dim(widened, slice_index, 0, keepdims=False)
        slab_here = lax.dynamic_index_in_dim(widened, slice_index + 1, 0, keepdims=False)
        slab_above = lax.dynamic_index_in_dim(widened, slice_index + 2, 0, keepdims=False)
        sample = shade_sample(slab_below, slab_here, slab_above, tf_color, tf_extinction, thickness)
        return composite(accumulated, sample)

    blank_image = jnp.zeros((4, tile_rows, tile_cols), jnp.float32)
    partial_value = lax.fori_loop(0, local_slices, march, blank_image)
    block_rows = tile_rows // depth_count
    rounds = depth_count.bit_length() - 1
    stacked = partial_value.reshape(4, 1, tile_rows, tile_cols)
    pieces = lax.all_to_all(
        stacked.astype(jnp.bfloat16), "depth", split_axis=2, concat_axis=1, tiled=True
    ).astype(stacked.dtype)
    for halving in range(rounds):
        paired = pieces.reshape(4, pieces.shape[1] // 2, 2, block_rows, tile_cols)
        pieces = composite(paired[:, :, 0], paired[:, :, 1])
    final_image = pieces[:, 0]
    return final_image


MESH = pl.DeviceIdType.MESH
LANES = 128
PAIR = 2
HALVES = 2
SUBLANES = 8
VMEM_BYTES = 24 * 2**20


def iota(shape, dim):
    return lax.broadcasted_iota(jnp.int32, shape, dim)


def stencil(chosen_up, chosen_down):
    return jnp.where(chosen_up, 0.5, jnp.where(chosen_down, -0.5, 0.0))


def render_kernel(
    depth_count,
    tile_count,
    vort_hbm,
    color_hbm,
    extinction_hbm,
    out_ref,
    color_ref,
    extinction_ref,
    brick,
    slabs,
    row_out,
    row_in,
    row_next,
    edge_out,
    edge_in,
    edge_next,
    part_out,
    part_in,
    part_own,
    local_sem,
    table_sem,
    own_sem,
    send_sem,
    recv_sem,
    row_send_sem,
    row_recv_sem,
    row_next_send_sem,
    row_next_recv_sem,
    edge_send_sem,
    edge_recv_sem,
    edge_next_send_sem,
    edge_next_recv_sem,
    halo_send_sem,
    halo_recv_sem,
    part_send_sem,
    part_recv_sem,
    far_sem,
    side_sem,
):
    local_slices, pairs, _, _, slim, tile_cols = vort_hbm.shape
    rows = HALVES * slim
    tile_rows = depth_count * rows
    knots = extinction_hbm.shape[0]
    thickness = 1.0 / (local_slices * depth_count)
    group = local_slices * rows
    pair_slices = PAIR * local_slices
    depth = lax.axis_index("depth")
    tile = lax.axis_index("tile")
    pair = depth // PAIR
    member = depth % PAIR
    mate = 1 - member
    left = tile - 1
    right = tile + 1
    has_below = pair > 0
    has_above = pair < pairs - 1
    has_left = tile > 0
    has_right = tile < tile_count - 1
    towards = pair - 1 + 2 * member
    origin = pair + 1 - 2 * member
    gives = jnp.where(member == 0, pair, pairs - 1 - pair) > 0
    takes = jnp.where(member == 0, pairs - 1 - pair, pair) > 0

    whole = pltpu.make_async_copy(vort_hbm, brick, local_sem)
    whole.start()
    barrier = pltpu.get_barrier_semaphore()

    def greet(there, peers):
        @pl.when(there)
        def _():
            for peer in peers:
                pl.semaphore_signal(barrier, inc=1, device_id=peer, device_id_type=MESH)

    close = (tile % 2 == 1, tile % 2 == 0)
    for there, at_hand, beside in ((has_left, close[0], left), (has_right, close[1], right)):
        greet(there, [(pair * PAIR + member, beside)])
        greet(there & at_hand, [(pair * PAIR + mate, beside)])
        greet(there & at_hand & takes, [(origin * PAIR + member, beside)])
    greet(has_below, [((pair - 1) * PAIR + member, tile)])
    greet(has_above, [((pair + 1) * PAIR + member, tile)])
    pl.semaphore_signal(barrier, inc=1, device_id=(pair * PAIR + mate, tile), device_id_type=MESH)
    greeted = 1 + has_below.astype(jnp.int32) + has_above.astype(jnp.int32)
    for there, at_hand in ((has_left, close[0]), (has_right, close[1])):
        for known in (there, there & at_hand, there & at_hand & gives):
            greeted = greeted + known.astype(jnp.int32)

    def tell(there, place, sem):
        @pl.when(there)
        def _():
            pl.semaphore_signal(sem, inc=1, device_id=(place * PAIR + member, tile), device_id_type=MESH)

    def hear(there, sem):
        @pl.when(there)
        def _():
            pl.semaphore_wait(sem, 1)


    def remote(src, dst, sent, received, target):
        return pltpu.make_async_remote_copy(
            src_ref=src,
            dst_ref=dst,
            send_sem=sent,
            recv_sem=received,
            device_id=target,
            device_id_type=MESH,
        )

    def order(step, place=None):
        place = pair if place is None else place
        chunk = place
        for home in range(pairs):
            route = [0] * (home > 0)
            route += list(range(home - 1, 0, -1)) + list(range(pairs - 1, home, -1))
            for turn, reached in enumerate(route):
                chunk = jnp.where((place == home) & (step == turn), reached, chunk)
        return chunk

    sends = []

    def halo(chunk):
        return remote(
            brick.at[pl.ds((local_slices - 2) * member, 2), chunk, member],
            slabs.at[chunk, pl.ds(pair_slices, 2)],
            halo_send_sem.at[chunk],
            halo_recv_sem.at[chunk],
            (towards * PAIR + member, tile),
        )

    def row_halo(chunk):
        return remote(
            row_out.at[member, chunk],
            row_next.at[chunk],
            row_next_send_sem.at[chunk],
            row_next_recv_sem.at[chunk],
            (towards * PAIR + member, tile),
        )

    def push(step, between=None):

        @pl.when(gives)
        def _():
            row_halo(order(step, towards)).start()
            halo(order(step, towards)).start()

        chunk = order(step)
        copy = remote(
            row_out.at[mate, chunk],
            row_in.at[member, chunk],
            row_send_sem.at[step],
            row_recv_sem.at[chunk],
            (pair * PAIR + mate, tile),
        )
        copy.start()
        sends.append(copy)
        for half in range(HALVES):
            if half == 1 and between is not None:
                between()
            copy = remote(
                brick.at[:, chunk, mate, half],
                slot(chunk, member, half),
                send_sem.at[step, half],
                recv_sem.at[chunk, half],
                (pair * PAIR + mate, tile),
            )
            copy.start()
            sends.append(copy)

    loads = [
        pltpu.make_async_copy(color_hbm, color_ref, table_sem.at[0]),
        pltpu.make_async_copy(extinction_hbm, extinction_ref, table_sem.at[1]),
    ]
    for copy in loads:
        copy.start()

    def slot(chunk, which, half):
        return slabs.at[chunk, pl.ds(which * local_slices, local_slices), half]

    whole.wait()
    packed = depth_count * HALVES * 2 * local_slices
    line = iota((packed, 1), 0)
    line_block = line // (2 * local_slices)
    line_slice = (line % (2 * local_slices)) // 2
    line_row = line_block * slim + jnp.where(line % 2 == 0, -1, slim)
    inside = (line_row >= 0) & (line_row < tile_rows)
    wanted = jnp.where(inside, line_slice * tile_rows + line_row, -1)
    pick = jnp.where(iota((packed, local_slices * tile_rows), 1) == wanted, 1.0, 0.0)
    flat = brick[...].reshape(local_slices * tile_rows, tile_cols)
    outside = jnp.dot(pick.astype(jnp.bfloat16), flat, preferred_element_type=jnp.float32)
    for block in range(depth_count):
        for half in range(HALVES):
            first = (block * HALVES + half) * 2 * local_slices
            row_out[block % PAIR, block // PAIR, half] = outside[first : first + 2 * local_slices].astype(
                jnp.bfloat16
            )
    column = iota((SUBLANES, tile_cols), 1)
    ends = iota((SUBLANES, tile_cols), 0)
    pick_ends = ((ends == 0) & (column == 0)) | ((ends == 1) & (column == tile_cols - 1))
    by_block = jnp.concatenate(
        [
            brick[z, block // PAIR, block % PAIR, half]
            for block in range(depth_count)
            for half in range(HALVES)
            for z in range(local_slices)
        ],
        axis=0,
    )
    columns = lax.dot_general(
        jnp.where(pick_ends, 1.0, 0.0).astype(jnp.bfloat16),
        by_block,
        (((1,), (1,)), ((), ())),
        preferred_element_type=jnp.float32,
    )
    for block in range(depth_count):
        for end in range(2):
            edge_out[end, block % PAIR, block // PAIR] = columns[end : end + 1, block * group : (block + 1) * group]

    @pl.when(jnp.logical_not(takes))
    def _():
        slabs[:, pair_slices:] = jnp.zeros((pairs, 2, HALVES, slim, tile_cols), jnp.bfloat16)
        row_next[...] = jnp.zeros(row_next.shape, jnp.bfloat16)

    row_in[member] = row_out[member]
    pl.semaphore_wait(barrier, greeted)
    tell(has_below & has_above, pair - 1, far_sem.at[0, 0])
    tell(has_below & has_above, pair + 1, far_sem.at[1, 0])
    sides = (has_left, has_right)
    distant = [there & jnp.logical_not(at_hand) for there, at_hand in zip(sides, close)]
    for end in range(2):

        @pl.when(distant[end])
        def _():
            pl.semaphore_signal(
                side_sem.at[1 - end],
                inc=1,
                device_id=(pair * PAIR + member, (left, right)[end]),
                device_id_type=MESH,
            )

    def edge(end, which):
        return remote(
            edge_out.at[end, which],
            edge_in.at[1 - end, member],
            edge_send_sem.at[end, which],
            edge_recv_sem.at[1 - end, member],
            (pair * PAIR + which, (left, right)[end]),
        )

    def edge_halo(end):
        return remote(
            edge_out.at[end, member],
            edge_next.at[1 - end],
            edge_next_send_sem.at[end],
            edge_next_recv_sem.at[1 - end],
            (towards * PAIR + member, (left, right)[end]),
        )

    for end in range(2):

        @pl.when(jnp.logical_not(sides[end]))
        def _():
            edge_in[end] = jnp.zeros(edge_in.shape[1:], jnp.float32)

        @pl.when(jnp.logical_not(sides[end] & takes))
        def _():
            edge_next[end] = jnp.zeros(edge_next.shape[1:], jnp.float32)

    def far_edges():
        for end in range(2):

            @pl.when(sides[end])
            def _():
                edge(end, member).start()

            @pl.when(sides[end] & close[end])
            def _():
                edge(end, mate).start()

            @pl.when(sides[end] & close[end] & gives)
            def _():
                edge_halo(end).start()

        for end in range(2):
            hear(distant[end], side_sem.at[end])

            @pl.when(distant[end])
            def _():
                edge(end, mate).start()

            @pl.when(distant[end] & gives)
            def _():
                edge_halo(end).start()

    push(0, far_edges)
    own = [
        pltpu.make_async_copy(
            vort_hbm.at[:, chunk, member, half], slot(chunk, member, half), own_sem.at[chunk, half]
        )
        for chunk in range(pairs)
        for half in range(HALVES)
    ]
    for copy in own:
        copy.start()

    for step in range(1, pairs):
        push(step)

    stack = (pair_slices + 1) * slim
    spread = (pair_slices + 2) * slim
    lined = 2 * (pair_slices + local_slices)
    extra = -(-lined // (2 * SUBLANES)) * 2 * SUBLANES
    cell = iota((stack, spread + extra), 0)
    source = iota((stack, spread + extra), 1)
    cell_row = cell % slim
    source_row = source % slim
    slot_of = cell // slim
    slice_of = jnp.where(source < spread, source // slim, -2)
    added = slot_of == pair_slices
    last = slot_of == pair_slices - 1
    home = jnp.where(added, pair_slices + member, slot_of)
    up = (slice_of == home) & (source_row == cell_row + 1)
    down = (slice_of == home) & (source_row == cell_row - 1)
    packed_line = spread + 2 * slot_of + jnp.where(added, 2 * (local_slices - 1) * member, 0)
    up = up | ((source == packed_line + 1) & (cell_row == slim - 1))
    down = down | ((source == packed_line) & (cell_row == 0))
    along_x = stencil(up, down).astype(jnp.bfloat16)
    behind = jnp.where(
        added,
        jnp.where(member == 0, pair_slices + 1, 0),
        jnp.where(last & (member == 1), -1, slot_of + 1),
    )
    ahead = jnp.where(
        added,
        jnp.where(member == 0, pair_slices - 1, pair_slices),
        jnp.where((slot_of == 0) & (member == 1), pair_slices + 1, slot_of - 1),
    )
    same_row = source_row == cell_row
    along_z = stencil((slice_of == behind) & same_row, (slice_of == ahead) & same_row).astype(jnp.bfloat16)
    along_both = jnp.concatenate([along_x, along_z], axis=0)
    keep_first = ((member == 1) | (pair == 0)).astype(jnp.float32)
    keep_last = ((member == 0) | (pair == pairs - 1)).astype(jnp.float32)
    keep_added = takes.astype(jnp.float32)
    to_col = iota((tile_cols, tile_cols), 1)
    from_col = iota((tile_cols, tile_cols), 0)
    along_y = stencil(from_col == to_col + 1, from_col == to_col - 1).astype(jnp.bfloat16)
    place = jnp.where(
        (ends == 0) & (column == 0),
        -0.5,
        jnp.where((ends == 1) & (column == tile_cols - 1), 0.5, 0.0),
    ).astype(jnp.bfloat16)

    for copy in loads:
        copy.wait()
    folds = slim // SUBLANES
    banks = -(-knots // SUBLANES)
    knot = iota((SUBLANES, LANES), 0)

    def wide(read, count):
        spread_out = []
        for bank in range(banks):
            value = jnp.zeros((SUBLANES, LANES), jnp.float32)
            for k in range(bank * SUBLANES, min(count, (bank + 1) * SUBLANES)):
                value = jnp.where(knot == k - bank * SUBLANES, read(k), value)
            spread_out.append(jnp.concatenate([value] * (folds * tile_cols // LANES), axis=1))
        return spread_out

    def table(read):
        return wide(read, knots), wide(lambda k: read(k + 1) - read(k), knots - 1)

    tables = [table(lambda k, c=c: color_ref[c, k]) for c in range(3)]
    tables.append(table(lambda k: -thickness * extinction_ref[k]))

    def fold(value):
        return jnp.concatenate(
            [value[first : first + SUBLANES] for first in range(0, slim, SUBLANES)], axis=1
        )

    def unfold(value):
        return jnp.concatenate(
            [value[:, first * tile_cols : (first + 1) * tile_cols] for first in range(folds)], axis=0
        )

    def pick_from(choices, index):
        found = None
        for bank, choice in enumerate(choices):
            got = jnp.take_along_axis(choice, index % SUBLANES, axis=0, mode="promise_in_bounds")
            found = got if found is None else jnp.where(index >= bank * SUBLANES, got, found)
        return found

    def lookup(which, index, part):
        value, slope = tables[which]
        return pick_from(value, index) + part * pick_from(slope, index)

    def wait_recv(dst, sem):
        remote(dst, dst, local_sem, sem, (depth, tile)).wait_recv()

    for copy in own:
        copy.wait()

    for end in range(2):

        @pl.when(sides[end])
        def _():
            for which in range(PAIR):
                wait_recv(edge_in.at[end, which], edge_recv_sem.at[end, which])

        @pl.when(sides[end] & takes)
        def _():
            wait_recv(edge_next.at[end], edge_next_recv_sem.at[end])

    hear(pair < pairs - 2, far_sem.at[0, 0])
    hear(pair >= 2, far_sem.at[1, 0])
    for reach in range(1, pairs - 2):
        tell(has_below & (pair < pairs - 1 - reach), pair - 1, far_sem.at[0, reach])
        tell(has_above & (pair > reach), pair + 1, far_sem.at[1, reach])
        hear(pair < pairs - 2 - reach, far_sem.at[0, reach])
        hear(pair >= 2 + reach, far_sem.at[1, reach])

    def over(near, far):
        clear = 1.0 - near[3]
        return tuple(n + clear * f for n, f in zip(near, far))

    def shade(chunk, half):
        filled = slabs[chunk, :, half].reshape(spread, tile_cols)
        cells = jnp.concatenate(
            [filled[: pair_slices * slim], slabs[chunk, pair_slices + member, half]], axis=0
        )
        lines = [row_in[which, chunk, half].astype(jnp.float32) for which in range(PAIR)]
        lines.append(row_next[chunk, half].astype(jnp.float32))
        lines.append(jnp.zeros((extra - lined, tile_cols), jnp.float32))
        around = jnp.concatenate([filled, jnp.concatenate(lines, axis=0).astype(jnp.bfloat16)], axis=0)
        grads = jnp.dot(along_both, around, preferred_element_type=jnp.float32)
        grads_x, grads_z = grads[:stack], grads[stack:]
        start = half * local_slices * slim
        stop = start + local_slices * slim
        first, second = (
            jnp.concatenate(
                [edge_in[end, which, chunk][:, start:stop] for which in range(PAIR)]
                + [
                    jnp.where(
                        member == 0,
                        edge_next[end, chunk][:, start : start + slim],
                        edge_next[end, chunk][:, stop - slim : stop],
                    )
                ],
                axis=1,
            )
            for end in range(2)
        )
        edge_row = iota((SUBLANES, stack), 0)
        edges = jnp.where(edge_row == 0, first, jnp.where(edge_row == 1, second, 0.0))
        grads_y = jnp.dot(cells, along_y, preferred_element_type=jnp.float32) + lax.dot_general(
            edges.astype(jnp.bfloat16),
            place,
            (((0,), (0,)), ((), ())),
            preferred_element_type=jnp.float32,
        )
        partial = None
        for z in range(pair_slices + 1):
            here = slice(z * slim, (z + 1) * slim)
            gx, gy, gz = fold(grads_x[here]), fold(grads_y[here]), fold(grads_z[here])
            scalar = fold(cells[here].astype(jnp.float32))
            facing = 0.48 * gx + 0.6 * gy + 0.64 * gz
            lighting = 0.55 + 0.45 * facing * lax.rsqrt(gx * gx + gy * gy + gz * gz + 0.25)
            position = jnp.clip((scalar + 4.0) * ((knots - 1) / 8.0), 0.0, knots - 1.0)
            index = position.astype(jnp.int32)
            part = position - index.astype(jnp.float32)
            opacity = 1.0 - jnp.exp(lookup(3, index, part))
            if z == 0:
                opacity = keep_first * opacity
            if z == pair_slices - 1:
                opacity = keep_last * opacity
            if z == pair_slices:
                opacity = keep_added * opacity
            lit = opacity * lighting
            sample = tuple(lit * lookup(c, index, part) for c in range(3)) + (opacity,)
            if z == pair_slices:
                near = tuple(jnp.where(member == 0, p, t) for p, t in zip(partial, sample))
                sample = tuple(jnp.where(member == 0, t, p) for p, t in zip(partial, sample))
                partial = near
            partial = sample if partial is None else over(partial, sample)
        return partial

    def send_part(step, half):
        chunk = order(step)
        return remote(
            part_out.at[chunk, half],
            part_in.at[pair, half],
            part_send_sem.at[chunk, half],
            part_recv_sem.at[pair, half],
            (chunk * PAIR + member, tile),
        )

    def march(step, carry):
        chunk = order(step)

        @pl.when(takes)
        def _():
            wait_recv(row_next.at[chunk], row_next_recv_sem.at[chunk])
            wait_recv(slabs.at[chunk, pl.ds(pair_slices, 2)], halo_recv_sem.at[chunk])

        wait_recv(row_in.at[mate, chunk], row_recv_sem.at[chunk])
        for half in range(HALVES):
            wait_recv(slot(chunk, mate, half), recv_sem.at[chunk, half])
            partial = shade(chunk, half)
            for channel in range(4):
                image = unfold(partial[channel])
                part_own[half, channel] = image
                part_out[chunk, half, channel] = image.astype(jnp.bfloat16)

            @pl.when(step < pairs - 1)
            def _():
                send_part(step, half).start()

        return carry

    lax.fori_loop(0, pairs, march, 0)
    part_in[pair] = part_out[pair]
    for copy in sends:
        copy.wait_send()
    for end in range(2):

        @pl.when(sides[end])
        def _():
            for which in range(PAIR):
                edge(end, which).wait_send()

        @pl.when(sides[end] & gives)
        def _():
            edge_halo(end).wait_send()

    for step in range(pairs - 1):
        for half in range(HALVES):
            send_part(step, half).wait_send()

    @pl.when(gives)
    def _():
        for chunk in range(pairs):
            halo(chunk).wait_send()
            row_halo(chunk).wait_send()

    for half in range(HALVES):
        for step in range(pairs - 1):
            wait_recv(part_in.at[order(step), half], part_recv_sem.at[order(step), half])
        total = None
        for source in range(pairs):
            layer = tuple(
                jnp.where(pair == source, part_own[half, c], part_in[source, half, c].astype(jnp.float32))
                for c in range(4)
            )
            total = layer if total is None else over(total, layer)
        for channel in range(4):
            out_ref[channel, half * slim : (half + 1) * slim] = total[channel]


def render(vorticity, tf_color, tf_extinction):
    depth_count = lax.axis_size("depth")
    tile_count = lax.axis_size("tile")
    local_slices, tile_rows, tile_cols = vorticity.shape
    rows = tile_rows // depth_count
    slim = rows // HALVES
    group = local_slices * rows
    pairs = depth_count // PAIR
    dma = pltpu.SemaphoreType.DMA
    return pl.pallas_call(
        functools.partial(render_kernel, depth_count, tile_count),
        out_shape=pltpu.VMEM((4, rows, tile_cols), jnp.float32),
        in_specs=[
            pl.BlockSpec(memory_space=pltpu.HBM),
            pl.BlockSpec(memory_space=pltpu.HBM),
            pl.BlockSpec(memory_space=pltpu.HBM),
        ],
        out_specs=pl.BlockSpec(memory_space=pltpu.VMEM),
        scratch_shapes=[
            pltpu.SMEM(tf_color.shape, jnp.float32),
            pltpu.SMEM(tf_extinction.shape, jnp.float32),
            pltpu.VMEM((local_slices, pairs, PAIR, HALVES, slim, tile_cols), jnp.bfloat16),
            pltpu.VMEM((pairs, PAIR * local_slices + 2, HALVES, slim, tile_cols), jnp.bfloat16),
            pltpu.VMEM((PAIR, pairs, HALVES, 2 * local_slices, tile_cols), jnp.bfloat16),
            pltpu.VMEM((PAIR, pairs, HALVES, 2 * local_slices, tile_cols), jnp.bfloat16),
            pltpu.VMEM((pairs, HALVES, 2 * local_slices, tile_cols), jnp.bfloat16),
            pltpu.VMEM((2, PAIR, pairs, 1, group), jnp.float32),
            pltpu.VMEM((2, PAIR, pairs, 1, group), jnp.float32),
            pltpu.VMEM((2, pairs, 1, group), jnp.float32),
            pltpu.VMEM((pairs, HALVES, 4, slim, tile_cols), jnp.bfloat16),
            pltpu.VMEM((pairs, HALVES, 4, slim, tile_cols), jnp.bfloat16),
            pltpu.VMEM((HALVES, 4, slim, tile_cols), jnp.float32),
            dma,
            dma((2,)),
            dma((pairs, HALVES)),
            dma((pairs, HALVES)),
            dma((pairs, HALVES)),
            dma((pairs,)),
            dma((pairs,)),
            dma((pairs,)),
            dma((pairs,)),
            dma((2, PAIR)),
            dma((2, PAIR)),
            dma((2,)),
            dma((2,)),
            dma((pairs,)),
            dma((pairs,)),
            dma((pairs, HALVES)),
            dma((pairs, HALVES)),
            pltpu.SemaphoreType.REGULAR((2, max(pairs - 2, 1))),
            pltpu.SemaphoreType.REGULAR((2,)),
        ],
        compiler_params=pltpu.CompilerParams(collective_id=0, has_side_effects=True, vmem_limit_bytes=VMEM_BYTES),
        name="render",
    )(*(pltpu.with_memory_space_constraint(given, pltpu.HBM) for given in (vorticity.reshape(local_slices, pairs, PAIR, HALVES, slim, tile_cols), tf_color, tf_extinction)))


def fits(vorticity, knots):
    local_slices, tile_rows, tile_cols = vorticity.shape
    depth_count = lax.axis_size("depth")
    rows = tile_rows // depth_count
    return (
        tile_rows % depth_count == 0
        and rows % (HALVES * 2 * SUBLANES) == 0
        and tile_cols % LANES == 0
        and (local_slices * rows) % LANES == 0
        and 2 * local_slices == SUBLANES
        and knots <= LANES
        and depth_count % PAIR == 0
        and depth_count & (depth_count - 1) == 0
        and depth_count <= 16
        and lax.axis_size("tile") > 1
    )


def choose(vorticity, tf_color, tf_extinction):
    if fits(vorticity, tf_extinction.shape[0]):
        return render(vorticity, tf_color, tf_extinction)
    return local(vorticity, tf_color, tf_extinction)


def solution(mesh):
    placed = (P("depth", None, "tile"), P(), P())
    return jax.shard_map(
        choose, mesh=mesh, in_specs=placed, out_specs=P(None, "depth", "tile"), check_vma=False
    )
```
